32 devices in a mesh: group: 4 (over y, x), expert: 8 (over z, core).
Axes of the slice: x: 2, y: 2, z: 4, core: 2. Of those that a mesh axis runs over, the one named last changes fastest.
Arguments:
- tokens: bfloat16 [12288, 2048], P(('group', 'expert')), may hold values from -6 to 6
- query_weight: bfloat16 [2048, 2048], P(('group', 'expert')), may hold values from -0.125 to 0.125
- key_weight: bfloat16 [2048, 2048], P(('group', 'expert')), may hold values from -0.125 to 0.125
- value_weight: bfloat16 [2048, 2048], P(('group', 'expert')), may hold values from -0.125 to 0.125
- output_weight: bfloat16 [2048, 2048], P(('group', 'expert')), may hold values from -2 to 2
- router_weight: bfloat16 [2048, 8], P(('group', 'expert')), may hold values from -0.0625 to 0.0625
- attnorm: bfloat16 [2048], P(('group', 'expert')), may hold values from 0.5 to 1.5
- querynorm: bfloat16 [2048], P(('group', 'expert')), may hold values from 0.5 to 1.5
- keynorm: bfloat16 [2048], P(('group', 'expert')), may hold values from 0.5 to 1.5
- mixnorm: bfloat16 [2048], P(('group', 'expert')), may hold values from 0.5 to 1.5
- gate_weight: bfloat16 [8, 2048, 1024], P('expert'), may hold values from -0.125 to 0.125
- up_weight: bfloat16 [8, 2048, 1024], P('expert'), may hold values from -0.125 to 0.125
- down_weight: bfloat16 [8, 1024, 2048], P('expert'), may hold values from -1 to 1
- routes: int32 [12288, 2], P(('group', 'expert')), may hold values from 0 to 7, all different within a row; in each aligned block of 384 rows (0 to 383, 384 to 767, ...) at most 192 rows name the same one
- lengths: int32 [4, 4], P('group'), may hold values from 1 to 2048, 3072 in all within a row
- seq_order: int32 [4, 4], P('group'), may hold values from 0 to 3, each once within a row
- cotangent: bfloat16 [12288, 2048], P(('group', 'expert')), may hold values from -6 to 6
Outputs:
- layer_result: bfloat16 [12288, 2048], P(('group', 'expert'))
- tokens_grad: bfloat16 [12288, 2048], P(('group', 'expert'))
- query_grad: float32 [2048, 2048], P(('group', 'expert'))
- key_grad: float32 [2048, 2048], P(('group', 'expert'))
- value_grad: float32 [2048, 2048], P(('group', 'expert'))
- output_grad: float32 [2048, 2048], P(('group', 'expert'))
- router_grad: float32 [2048, 8], P(('group', 'expert'))
- attnorm_grad: float32 [2048], P(('group', 'expert'))
- querynorm_grad: float32 [2048], P(('group', 'expert'))
- keynorm_grad: float32 [2048], P(('group', 'expert'))
- mixnorm_grad: float32 [2048], P(('group', 'expert'))
- gate_grad: float32 [8, 2048, 1024], P('expert')
- up_grad: float32 [8, 2048, 1024], P('expert')
- down_grad: float32 [8, 1024, 2048], P('expert')
The draws below stay inside these ranges and needn't reach their ends.
Inputs may be any that keep to these rules, and one draw needn't show every extreme that they name: `routes`: the 2 entries of a row name different experts, every expert is named somewhere; at most 192 of the rows of one device name one expert, and in every draw some device's rows name some expert exactly 192 times. Each group's 4 lengths sum to 3072, and the largest of each group is exactly 2048. `seq_order`: each group's row holds every number 0 to 3 once.
All inputs are finite; a program needn't handle non-finite values.
Results may differ from the reference program's by a relative error of at most 0.025.
Values may be sent and summed in bfloat16 or wider, within the bound.
A program may use at most 384 MiB of HBM per device.

```python
import math
import jax
import jax.numpy as jnp
import numpy as np
from jax import lax

D = 2048
HEADS = 16
HEAD_DIM = 128
FF = 1024
TOP = 2
LONGEST = 2048
EXPERTS = 8
GROUP_TOK = 3072
SEQS = 4
TOK_DEV = 384
TOKENS = 12288
CAP = 192
N_GROUP = 4


def block_levels(own_key, dims, split, smallest, largest):
    loudness, own = 1.0, jax.random.fold_in(own_key, 6)
    for dim, shards_of in split:
        steps = jnp.exp(jax.random.uniform(jax.random.fold_in(own, dim), (shards_of,), jnp.float32, smallest / len(split), largest / len(split)))
        loudness = loudness * jnp.repeat(steps, dims[dim] // shards_of).reshape([-1 if axis == dim else 1 for axis in range(len(dims))])
    return loudness


def length_profile(amount, total, limit, skew):
    weights = [(1 << 20) // math.isqrt(grade ** skew) + 1 for grade in range(2, amount + 1)]
    surplus, given = total - limit - (amount - 1), [1] * (amount - 1)
    while surplus > 0:
        movable = [i for i in range(amount - 1) if given[i] < limit]
        whole, left = sum([weights[i] for i in movable]), surplus
        for i in movable:
            extra = min(limit - given[i], max(1, left * weights[i] // whole), surplus)
            given[i] = given[i] + extra
            surplus = surplus - extra
    return np.array([limit] + given)


def ragged(key, amount, total, most, slope):
    if amount == 2:
        one = jax.random.randint(key, (), max(1, total - most), min(most, total - 1) + 1)
        return jnp.stack([one, total - one])
    sizes = jnp.asarray(length_profile(amount, total, most, slope), jnp.int32)
    twos = (amount - 1) // 2
    source_of, sink = sizes[1:1 + 2 * twos:2], sizes[2:2 + 2 * twos:2]
    slack = jnp.minimum(source_of - 1, most - sink)
    moved = jax.random.randint(jax.random.fold_in(key, 1), (twos,), 0, 1 << 20) % (slack + 1)
    sizes = sizes.at[1:1 + 2 * twos:2].set(source_of - moved).at[2:2 + 2 * twos:2].set(sink + moved)
    return sizes[jax.random.permutation(jax.random.fold_in(key, 2), amount)]


def routed_block(key, own, number, rows, number_of, top, most, skew):
    sequence = jax.random.permutation(key, number_of)
    heavy_load, ordinary = load_shares(number_of, rows * top, most, skew, True), load_shares(number_of, rows * top, most, skew, False)
    places = jnp.arange(number_of)

    def named(tallies, offset_by):
        used = int((tallies > 0).sum())
        fixed = max(1, used // 4)
        moved = fixed + (places - fixed + offset_by * (used - fixed)) % max(1, number_of - fixed)
        return jnp.zeros((number_of,), jnp.int32).at[sequence[jnp.where(places < fixed, places, moved)]].set(jnp.asarray(tallies, jnp.int32))

    tallies = jnp.where(number % 4 == 0, named(heavy_load, number // 4), named(ordinary, number - number // 4 - 1))
    mixed = jax.random.permutation(jax.random.fold_in(own, 3), number_of)
    donor, sink = mixed[0:number_of // 2 * 2:2], mixed[1:number_of // 2 * 2:2]
    slack = jnp.minimum(tallies[donor] - 1, most - tallies[sink]) // 2
    slack = jnp.where((donor == sequence[0]) | (sink == sequence[0]) | (tallies[sink] == 0), 0, jnp.maximum(slack, 0))
    moved = jax.random.randint(jax.random.fold_in(own, 4), (number_of // 2,), 0, 1 << 20) % (slack + 1)
    tallies = tallies.at[donor].add(-moved).at[sink].add(moved)
    items = jnp.searchsorted(jnp.cumsum(tallies), jnp.arange(rows * top), side="right").astype(jnp.int32)
    grid = items.reshape(top, rows).T
    grid = grid[jax.random.permutation(jax.random.fold_in(own, 1), rows)]
    offset_by = jax.random.randint(jax.random.fold_in(own, 2), (rows, 1), 0, top)
    return jnp.take_along_axis(grid, (jnp.arange(top)[None, :] + offset_by) % top, axis=1)


def load_shares(number_of, total, limit, skew, full):
    loads = [(1 << 20) // math.isqrt(grade ** skew) + 1 for grade in range(1, number_of + 1)]
    largest = limit if full else min(limit, max(-(-total // number_of), total * loads[0] // sum(loads)))
    least = 1 if total - largest >= number_of - 1 else 0
    counts, surplus = [largest] + [least] * (number_of - 1), total - largest - least * (number_of - 1)
    while surplus > 0:
        candidates = [i for i in range(1, number_of) if counts[i] < largest] or [i for i in range(1, number_of) if counts[i] < limit]
        mass, remaining = sum([loads[i] for i in candidates]), surplus
        for i in candidates:
            extra = min(limit - counts[i], max(1, remaining * loads[i] // mass), surplus)
            counts[i] = counts[i] + extra
            surplus = surplus - extra
    return np.array(counts)


def noise(own_key, shape, spread, most, pieces=(), kind=jnp.bfloat16):
    values = jax.random.normal(own_key, shape, jnp.float32) * spread
    if len(pieces) > 0:
        values = block_levels(own_key, shape, pieces, -0.22, 0.18) * values
    return jnp.clip(values, min=-most, max=most).astype(kind)


def setup_inputs(seed: int = 0) -> dict:
    key_of = jax.random.split(jax.random.key(seed), 18)
    tokens = noise(key_of[0], (TOKENS, D), 1.0, 6.0, ((0, 32),))
    query_weight = noise(key_of[1], (D, D), D ** -0.5, 0.125, ((0, 32),))
    key_weight = noise(key_of[2], (D, D), D ** -0.5, 0.125, ((0, 32),))
    value_weight = noise(key_of[3], (D, D), D ** -0.5, 0.125, ((0, 32),))
    output_weight = noise(key_of[4], (D, D), (max(D // 256, 1)) ** -0.5, 2.0, ((0, 32),))
    router_weight = noise(key_of[5], (D, EXPERTS), (4 * D) ** -0.5, 0.0625, ((0, 32),))
    attnorm = jnp.clip(1.0 + 0.1 * jax.random.normal(key_of[6], (D,), jnp.float32), 0.5, 1.5).astype(jnp.bfloat16)
    querynorm = jnp.clip(1.0 + 0.1 * jax.random.normal(key_of[7], (D,), jnp.float32), 0.5, 1.5).astype(jnp.bfloat16)
    keynorm = jnp.clip(1.0 + 0.1 * jax.random.normal(key_of[8], (D,), jnp.float32), 0.5, 1.5).astype(jnp.bfloat16)
    mixnorm = jnp.clip(1.0 + 0.1 * jax.random.normal(key_of[9], (D,), jnp.float32), 0.5, 1.5).astype(jnp.bfloat16)
    gate_weight = noise(key_of[10], (EXPERTS, D, FF), D ** -0.5, 0.125, ((0, 8),))
    up_weight = noise(key_of[11], (EXPERTS, D, FF), D ** -0.5, 0.125, ((0, 8),))
    down_weight = noise(key_of[12], (EXPERTS, FF, D), (FF // 32) ** -0.5, 1.0, ((0, 8),))
    routes_keys = jax.random.split(jax.random.fold_in(key_of[13], 1), TOKENS // TOK_DEV)
    routes_turns = jax.random.permutation(jax.random.fold_in(key_of[13], 3), TOKENS // TOK_DEV)
    routes = jax.vmap(lambda own, number: routed_block(jax.random.fold_in(key_of[13], 2), own, number, TOK_DEV, EXPERTS, TOP, CAP, 1))(routes_keys, routes_turns).reshape((TOKENS, TOP))
    lengths = jax.vmap(lambda own: ragged(own, SEQS, GROUP_TOK, LONGEST, 2))(jax.random.split(key_of[14], N_GROUP)).reshape((N_GROUP, SEQS)).astype(jnp.int32)
    seq_order = jax.vmap(lambda own: jax.random.permutation(own, SEQS))(jax.random.split(key_of[15], N_GROUP)).reshape((N_GROUP, SEQS)).astype(jnp.int32)
    cotangent = noise(key_of[16], (TOKENS, D), 1.0, 6.0, ((0, 32),))
    return dict(tokens=tokens, query_weight=query_weight, key_weight=key_weight, value_weight=value_weight, output_weight=output_weight, router_weight=router_weight, attnorm=attnorm, querynorm=querynorm, keynorm=keynorm, mixnorm=mixnorm, gate_weight=gate_weight, up_weight=up_weight, down_weight=down_weight, routes=routes, lengths=lengths, seq_order=seq_order, cotangent=cotangent)


@jax.custom_vjp
def low(v):
    return lax.optimization_barrier(v.astype(jnp.bfloat16)).astype(jnp.float32)

@jax.custom_vjp
def low_back(v):
    return v

def low_keep(v):
    return (low(v), None)

def low_pass(kept, grad):
    return (grad,)

def back_keep(v):
    return (v, None)

def back_low(kept, grad):
    return (low(grad),)
low.defvjp(low_keep, low_pass)
low_back.defvjp(back_keep, back_low)
highest = lax.Precision.HIGHEST
masked_score = -1e+30

def rms_scale(values, gain):
    return values * lax.rsqrt(lax.optimization_barrier(jnp.mean(values * values, axis=-1, keepdims=True)) + 1e-05) * gain

def angle_tables(position, head_size):
    half_size = head_size // 2
    frequency = 10000.0 ** (-(jnp.arange(half_size, dtype=jnp.float32) * 2.0 / head_size))
    angles = position.astype(jnp.float32)[:, None] * frequency[None, :]
    angles = jnp.concatenate([angles, angles], axis=1)
    return (jnp.cos(angles)[:, None, :], jnp.sin(angles)[:, None, :])

def rotate(values, cosine, sine_part):
    half_size = values.shape[-1] // 2
    turned = jnp.concatenate([-values[..., half_size:], values[..., :half_size]], axis=-1)
    return values * cosine + turned * sine_part

def placement_of(token_index, length_row, order_row):
    chosen = (order_row[:, None] == jnp.arange(SEQS, dtype=jnp.int32)[None, :]).astype(jnp.int32)
    placed = lax.optimization_barrier(jnp.sum(chosen * length_row[None, :], axis=1))
    seq_ends = jnp.cumsum(placed)
    passed = (token_index[:, None] >= seq_ends[None, :]).astype(jnp.int32)
    segment = lax.optimization_barrier(jnp.sum(passed, axis=1))
    seq_begin = lax.optimization_barrier(jnp.sum(passed * placed[None, :], axis=1))
    return (segment, token_index - seq_begin)

def forward(params, tokens_in, routes, segment, position):
    query_weight, key_weight, value_weight, output_weight, router_weight, attnorm, querynorm, keynorm, mixnorm, gate_weight, up_weight, down_weight = params
    normed = low(rms_scale(tokens_in, attnorm))
    query_pre = low_back(jnp.dot(normed, query_weight, precision=highest))
    key_pre = low_back(jnp.dot(normed, key_weight, precision=highest))
    value_pre = low_back(jnp.dot(normed, value_weight, precision=highest))
    cosine, sine_part = angle_tables(position, HEAD_DIM)
    queries = low(rotate(rms_scale(query_pre, querynorm).reshape(TOKENS, HEADS, HEAD_DIM), cosine, sine_part))
    keys_all = low(rotate(rms_scale(key_pre, keynorm).reshape(TOKENS, HEADS, HEAD_DIM), cosine, sine_part))
    values_all = low(value_pre).reshape(TOKENS, HEADS, HEAD_DIM)
    scale_factor = HEAD_DIM ** (-0.5)
    group_index = jnp.arange(GROUP_TOK, dtype=jnp.int32)
    causal = group_index[:, None] >= group_index[None, :]

    def attend_group(items):
        query_group, key_group, value_group, segment_group = items
        scores = low_back(jnp.einsum('qhd,khd->hqk', query_group, key_group, precision=highest) * scale_factor)
        allowed = causal & (segment_group[:, None] == segment_group[None, :])
        scores = jnp.where(allowed[None], scores, masked_score)
        shifted = jnp.exp(scores - lax.optimization_barrier(jnp.max(scores, axis=2, keepdims=True)))
        weights = low(shifted / lax.optimization_barrier(jnp.sum(shifted, axis=2, keepdims=True)))
        return jnp.einsum('hqk,khd->qhd', weights, value_group, precision=highest)
    attended = lax.map(jax.checkpoint(attend_group), (queries.reshape(N_GROUP, GROUP_TOK, HEADS, HEAD_DIM), keys_all.reshape(N_GROUP, GROUP_TOK, HEADS, HEAD_DIM), values_all.reshape(N_GROUP, GROUP_TOK, HEADS, HEAD_DIM), segment.reshape(N_GROUP, GROUP_TOK)))
    attended = low_back(low(attended.reshape(TOKENS, D)))
    projected = low_back(jnp.dot(attended, output_weight, precision=highest))
    middle = tokens_in + projected
    mixed = low(rms_scale(middle, mixnorm))
    logits = low_back(jnp.dot(mixed, router_weight, precision=highest))
    shifted = jnp.exp(logits - lax.optimization_barrier(jnp.max(logits, axis=1, keepdims=True)))
    share = shifted / lax.optimization_barrier(jnp.sum(shifted, axis=1, keepdims=True))
    picked = lax.optimization_barrier(jnp.sum((routes[:, :, None] == jnp.arange(EXPERTS, dtype=jnp.int32)[None, None, :]).astype(jnp.float32), axis=1))
    combine = share * picked

    def one_expert(running, items):
        gate_one, up_one, down_one, column = items
        copies = low_back(mixed)
        gate_pre = low_back(jnp.dot(copies, gate_one, precision=highest))
        up_pre = low_back(jnp.dot(copies, up_one, precision=highest))
        hidden = low(jax.nn.sigmoid(gate_pre) * gate_pre * up_pre)
        result = low_back(low(jnp.dot(hidden, down_one, precision=highest)))
        return (running + column[:, None] * result, None)
    mixture = lax.scan(jax.checkpoint(one_expert), jnp.zeros((TOKENS, D), jnp.float32), (gate_weight, up_weight, down_weight, combine.T))[0]
    return middle + mixture

def reference(tokens, query_weight, key_weight, value_weight, output_weight, router_weight, attnorm, querynorm, keynorm, mixnorm, gate_weight, up_weight, down_weight, routes, lengths, seq_order, cotangent):
    params = tuple((weight_arg.astype(jnp.float32) for weight_arg in (query_weight, key_weight, value_weight, output_weight, router_weight, attnorm, querynorm, keynorm, mixnorm, gate_weight, up_weight, down_weight)))
    group_index = jnp.arange(GROUP_TOK, dtype=jnp.int32)
    segment, position = jax.vmap(lambda length_row, order_row: placement_of(group_index, length_row, order_row))(lengths, seq_order)
    segment = segment.reshape(TOKENS)
    position = position.reshape(TOKENS)
    tokens_in = tokens.astype(jnp.float32)
    result, pullback = jax.vjp(lambda params_in, tokens_arg: forward(params_in, tokens_arg, routes, segment, position), params, tokens_in)
    param_grads, tokens_grad = pullback(cotangent.astype(jnp.float32))
    return (result.astype(jnp.bfloat16), tokens_grad.astype(jnp.bfloat16), param_grads[0], param_grads[1], param_grads[2], param_grads[3], param_grads[4], param_grads[5], param_grads[6], param_grads[7], param_grads[8], param_grads[9], param_grads[10], param_grads[11])
```

```python
import functools

import jax
import jax.numpy as jnp
from jax import lax
from jax.experimental import pallas as pl
from jax.experimental.pallas import tpu as pltpu
from jax.sharding import PartitionSpec as P

HEADS = 16
HEAD_DIM = 128
TOP = 2
EPS = 1e-05
NEG = -1e30
MESH = pl.DeviceIdType.MESH
BF = jnp.bfloat16
F32 = jnp.float32


def share_all(block, collective_id):
    groups, ranks = lax.axis_size("group"), lax.axis_size("expert")
    total = groups * ranks

    def kernel(x_ref, o_ref, send_sem, recv_sem):
        me = lax.axis_index("group") * ranks + lax.axis_index("expert")

        def place(step):
            flat = lax.rem(me + step, total)
            return (flat // ranks, lax.rem(flat, ranks))

        barrier = pltpu.get_barrier_semaphore()

        def greet(step, carry):
            pl.semaphore_signal(barrier, inc=1, device_id=place(step), device_id_type=MESH)
            return carry

        lax.fori_loop(1, total, greet, 0)
        pl.semaphore_wait(barrier, total - 1)

        def copy(step):
            return pltpu.make_async_remote_copy(
                src_ref=x_ref,
                dst_ref=o_ref.at[me],
                send_sem=send_sem.at[step],
                recv_sem=recv_sem.at[step],
                device_id=place(step),
                device_id_type=MESH,
            )

        def send(step, carry):
            copy(step).start()
            return carry

        lax.fori_loop(1, total, send, 0)
        o_ref[me] = x_ref[...]

        def settle(step, carry):
            copy(step).wait()
            return carry

        lax.fori_loop(1, total, settle, 0)

    return pl.pallas_call(
        kernel,
        out_shape=jax.ShapeDtypeStruct((total,) + block.shape, block.dtype),
        in_specs=[pl.BlockSpec(memory_space=pltpu.VMEM)],
        out_specs=pl.BlockSpec(memory_space=pltpu.VMEM),
        scratch_shapes=[pltpu.SemaphoreType.DMA((total,)), pltpu.SemaphoreType.DMA((total,))],
        compiler_params=pltpu.CompilerParams(collective_id=collective_id, has_side_effects=True),
        name="share_all",
    )(block)


def share_group(block, collective_id, add=False):
    ranks = lax.axis_size("expert")

    def kernel(x_ref, o_ref, *scratch):
        if add:
            land, send_sem, recv_sem = scratch
        else:
            send_sem, recv_sem = scratch
            land = o_ref
        me = lax.axis_index("expert")
        barrier = pltpu.get_barrier_semaphore()
        for step in range(1, ranks):
            pl.semaphore_signal(
                barrier,
                inc=1,
                device_id={"expert": lax.rem(me + step, ranks)},
                device_id_type=MESH,
            )
        pl.semaphore_wait(barrier, ranks - 1)
        copies = []
        for step in range(1, ranks):
            copy = pltpu.make_async_remote_copy(
                src_ref=x_ref,
                dst_ref=land.at[me],
                send_sem=send_sem.at[step],
                recv_sem=recv_sem.at[step],
                device_id={"expert": lax.rem(me + step, ranks)},
                device_id_type=MESH,
            )
            copy.start()
            copies.append(copy)
        land[me] = x_ref[...]
        for copy in copies:
            copy.wait()
        if add:
            total = land[0]
            for rank in range(1, ranks):
                total = total + land[rank]
            o_ref[...] = total

    landing = (ranks,) + block.shape
    scratch = [pltpu.SemaphoreType.DMA((ranks,)), pltpu.SemaphoreType.DMA((ranks,))]
    if add:
        scratch = [pltpu.VMEM(landing, block.dtype)] + scratch
    return pl.pallas_call(
        kernel,
        out_shape=jax.ShapeDtypeStruct(block.shape if add else landing, block.dtype),
        in_specs=[pl.BlockSpec(memory_space=pltpu.VMEM)],
        out_specs=pl.BlockSpec(memory_space=pltpu.VMEM),
        scratch_shapes=scratch,
        compiler_params=pltpu.CompilerParams(collective_id=collective_id, has_side_effects=True),
        name="sum_group" if add else "share_group",
    )(block)


def partner_swap(block):
    ranks = lax.axis_size("expert")
    return lax.ppermute(block, "expert", [(i, i ^ 1) for i in range(ranks)])


def chip_shift(block, step=1):
    ranks = lax.axis_size("expert")
    return lax.ppermute(block, "expert", [(i, (i + 2 * step) % ranks) for i in range(ranks)])


def ring_gather(block, axis):
    ranks = lax.axis_size("expert")
    chips = ranks // 2
    me = lax.axis_index("expert")
    chip, core = me // 2, me % 2
    size = block.shape[axis]
    shape = list(block.shape)
    shape[axis] = size * ranks
    whole = jnp.zeros(shape, block.dtype)
    moving = block
    for step in range(chips):
        if step:
            moving = chip_shift(moving)
        other = partner_swap(moving)
        source = lax.rem(chip - step + chips, chips) * 2
        whole = lax.dynamic_update_slice_in_dim(whole, moving, (source + core) * size, axis)
        whole = lax.dynamic_update_slice_in_dim(whole, other, (source + 1 - core) * size, axis)
    return whole


def ring_scatter(partial):
    ranks = lax.axis_size("expert")
    chips = ranks // 2
    me = lax.axis_index("expert")
    chip, core = me // 2, me % 2
    rows, width = partial.shape[0] // ranks, partial.shape[1]
    halves = partial.reshape(chips, 2, rows, width)
    away = lax.dynamic_index_in_dim(halves, 1 - core, 1, keepdims=False)
    mine = lax.dynamic_index_in_dim(halves, core, 1, keepdims=False)
    pair = (mine.astype(F32) + partner_swap(away).astype(F32)).astype(BF)

    def for_chip(step):
        return lax.dynamic_index_in_dim(
            pair, lax.rem(chip - step + chips, chips), 0, keepdims=False
        )

    moving = for_chip(1)
    for step in range(2, chips):
        moving = (chip_shift(moving).astype(F32) + for_chip(step).astype(F32)).astype(BF)
    return chip_shift(moving).astype(F32) + for_chip(0).astype(F32)


def attention_forward(queries, keys, values, starts, lowest):
    rows = queries.shape[0]
    heads = queries.shape[1] // HEAD_DIM
    blocks, _, block = starts.shape
    scale = HEAD_DIM ** (-0.5)

    def kernel(low_ref, start_ref, q_ref, k_ref, v_ref, o_ref, lse_ref):
        i = pl.program_id(1)
        q = q_ref[...]
        start = start_ref[0]
        q_index = i * block + lax.broadcasted_iota(jnp.int32, (1, block), 1)
        k_local = lax.broadcasted_iota(jnp.int32, (block, block), 0)

        def step(j, carry):
            top, total, acc = carry
            at = pl.multiple_of(j * block, block)
            k = k_ref[pl.ds(at, block), :]
            v = v_ref[pl.ds(at, block), :]
            s = (
                lax.dot_general(k, q, (((1,), (1,)), ((), ())), preferred_element_type=F32)
                * scale
            )
            k_index = k_local + j * block
            s = jnp.where((k_index <= q_index) & (k_index >= start), s, NEG)
            new_top = jnp.maximum(top, jnp.max(s, axis=0, keepdims=True))
            p = jnp.exp(s - new_top)
            shrink = jnp.exp(top - new_top)
            total = total * shrink + jnp.sum(p, axis=0, keepdims=True)
            acc = acc * shrink + lax.dot_general(
                v, p.astype(BF), (((0,), (0,)), ((), ())), preferred_element_type=F32
            )
            return (new_top, total, acc)

        top, total, acc = lax.fori_loop(
            low_ref[i],
            i + 1,
            step,
            (
                jnp.full((1, block), NEG, F32),
                jnp.zeros((1, block), F32),
                jnp.zeros((HEAD_DIM, block), F32),
            ),
        )
        o_ref[...] = (acc / total).T.astype(BF)
        lse_ref[0, 0] = top + jnp.log(total)

    return pl.pallas_call(
        kernel,
        out_shape=(
            jax.ShapeDtypeStruct((rows, heads * HEAD_DIM), BF),
            jax.ShapeDtypeStruct((heads, blocks, 1, block), F32),
        ),
        grid_spec=pltpu.PrefetchScalarGridSpec(
            num_scalar_prefetch=1,
            grid=(heads, blocks),
            in_specs=[
                pl.BlockSpec((1, 1, block), lambda h, i, low: (i, 0, 0)),
                pl.BlockSpec((block, HEAD_DIM), lambda h, i, low: (i, h)),
                pl.BlockSpec((rows, HEAD_DIM), lambda h, i, low: (0, h)),
                pl.BlockSpec((rows, HEAD_DIM), lambda h, i, low: (0, h)),
            ],
            out_specs=[
                pl.BlockSpec((block, HEAD_DIM), lambda h, i, low: (i, h)),
                pl.BlockSpec((1, 1, 1, block), lambda h, i, low: (h, i, 0, 0)),
            ],
        ),
        compiler_params=pltpu.CompilerParams(vmem_limit_bytes=48 << 20),
        cost_estimate=pl.CostEstimate(
            flops=2 * rows * rows * HEAD_DIM * heads,
            bytes_accessed=8 * rows * heads * HEAD_DIM,
            transcendentals=rows * rows * heads // 2,
        ),
        name="attention_forward",
    )(lowest, starts, queries, keys, values)


def attention_backward(queries, keys, values, douts, lse, delta, starts, highest):
    rows = queries.shape[0]
    heads = queries.shape[1] // HEAD_DIM
    blocks, _, block = starts.shape
    scale = HEAD_DIM ** (-0.5)

    def kernel(
        high_ref, start_ref, q_ref, do_ref, k_ref, v_ref, lse_ref, delta_ref, dq_ref, dk_ref, dv_ref
    ):
        j = pl.program_id(1)

        @pl.when(j == 0)
        def _():
            dq_ref[...] = jnp.zeros_like(dq_ref)

        k = k_ref[...]
        v = v_ref[...]
        k_index = j * block + lax.broadcasted_iota(jnp.int32, (block, block), 0)
        q_local = lax.broadcasted_iota(jnp.int32, (1, block), 1)

        def step(i, carry):
            dk, dv = carry
            at = pl.multiple_of(i * block, block)
            q = q_ref[pl.ds(at, block), :]
            do = do_ref[pl.ds(at, block), :]
            s = (
                lax.dot_general(k, q, (((1,), (1,)), ((), ())), preferred_element_type=F32)
                * scale
            )
            allowed = (k_index <= q_local + i * block) & (k_index >= start_ref[i])
            p = jnp.exp(jnp.where(allowed, s, NEG) - lse_ref[0, i])
            dv = dv + jnp.dot(p.astype(BF), do, preferred_element_type=F32)
            dp = lax.dot_general(v, do, (((1,), (1,)), ((), ())), preferred_element_type=F32)
            ds = (p * (dp - delta_ref[0, i])).astype(BF)
            dk = dk + jnp.dot(ds, q, preferred_element_type=F32)
            dq_ref[pl.ds(at, block), :] += (
                lax.dot_general(ds, k, (((0,), (0,)), ((), ())), preferred_element_type=F32)
                * scale
            )
            return (dk, dv)

        zero = jnp.zeros((block, HEAD_DIM), F32)
        dk, dv = lax.fori_loop(j, high_ref[j] + 1, step, (zero, zero))
        dk_ref[...] = dk * scale
        dv_ref[...] = dv

    whole = pl.BlockSpec((rows, HEAD_DIM), lambda h, j, high: (0, h))
    part = pl.BlockSpec((block, HEAD_DIM), lambda h, j, high: (j, h))
    line = pl.BlockSpec((1, blocks, 1, block), lambda h, j, high: (h, 0, 0, 0))
    shape = jax.ShapeDtypeStruct((rows, heads * HEAD_DIM), F32)
    return pl.pallas_call(
        kernel,
        out_shape=(shape, shape, shape),
        grid_spec=pltpu.PrefetchScalarGridSpec(
            num_scalar_prefetch=1,
            grid=(heads, blocks),
            in_specs=[
                pl.BlockSpec((blocks, 1, block), lambda h, j, high: (0, 0, 0)),
                whole,
                whole,
                part,
                part,
                line,
                line,
            ],
            out_specs=[whole, part, part],
        ),
        compiler_params=pltpu.CompilerParams(vmem_limit_bytes=48 << 20),
        cost_estimate=pl.CostEstimate(
            flops=5 * rows * rows * HEAD_DIM * heads,
            bytes_accessed=20 * rows * heads * HEAD_DIM,
            transcendentals=rows * rows * heads // 2,
        ),
        name="attention_backward",
    )(highest, starts, queries, douts, keys, values, lse, delta)


def inverse_rms(total, width):
    return lax.rsqrt(total / width + EPS)


def spin(values, cosine, sine):
    half = HEAD_DIM // 2
    pieces = []
    for at in range(0, values.shape[1], HEAD_DIM):
        low, high = values[:, at : at + half], values[:, at + half : at + HEAD_DIM]
        pieces += [low * cosine - high * sine, high * cosine + low * sine]
    return jnp.concatenate(pieces, axis=1)


def norm_back(values, inverse, gain, grad):
    scaled = values * inverse
    weighted = grad * gain
    mean = jnp.mean(scaled * weighted, axis=-1, keepdims=True)
    return inverse * (weighted - scaled * mean), jnp.sum(grad * scaled, axis=0)


def dot_nt(a, b):
    return lax.dot_general(a, b, (((1,), (1,)), ((), ())), preferred_element_type=F32)


def dot_tn(a, b):
    return lax.dot_general(a, b, (((0,), (0,)), ((), ())), preferred_element_type=F32)


def dot_nn(a, b):
    return jnp.dot(a, b, preferred_element_type=F32)


def layout_of(lengths, seq_order, rows):
    length_row, order_row = lengths[0], seq_order[0]
    count = order_row.shape[0]
    chosen = (order_row[:, None] == jnp.arange(count, dtype=jnp.int32)[None, :]).astype(jnp.int32)
    placed = jnp.sum(chosen * length_row[None, :], axis=1)
    ends = jnp.sum(
        jnp.where(jnp.arange(count)[None, :] <= jnp.arange(count)[:, None], placed[None, :], 0),
        axis=1,
    )
    index = jnp.arange(rows, dtype=jnp.int32)
    passed = (index[:, None] >= ends[None, :]).astype(jnp.int32)
    begin = jnp.sum(passed * placed[None, :], axis=1)
    segment = jnp.sum(passed, axis=1)
    inside = (segment[:, None] == jnp.arange(count, dtype=jnp.int32)[None, :]).astype(jnp.int32)
    final = jnp.sum(inside * ends[None, :], axis=1) - 1
    return index, begin, final


def body(
    tokens,
    query_weight,
    key_weight,
    value_weight,
    output_weight,
    router_weight,
    attnorm,
    querynorm,
    keynorm,
    mixnorm,
    gate_weight,
    up_weight,
    down_weight,
    routes,
    lengths,
    seq_order,
    cotangent,
):
    rows, width = tokens.shape
    ranks = lax.axis_size("expert")
    groups = lax.axis_size("group")
    me = lax.axis_index("expert")
    all_rows = rows * ranks
    capacity = 2 * rows * TOP // ranks
    columns = width // ranks
    shard = query_weight.shape[0]
    experts = router_weight.shape[1]
    block = rows
    blocks = all_rows // block

    small = jnp.concatenate(
        [attnorm, querynorm, keynorm, mixnorm, router_weight.T.reshape(-1)], axis=0
    )
    packed = jnp.zeros((2048,), BF).at[: small.shape[0]].set(small).reshape(16, 128)
    everyone = share_all(packed, 1).reshape(groups * ranks, 2048)
    attn_gain = everyone[:, :shard].reshape(width).astype(F32)
    query_gain = everyone[:, shard : 2 * shard].reshape(width).astype(F32)
    key_gain = everyone[:, 2 * shard : 3 * shard].reshape(width).astype(F32)
    mix_gain = everyone[:, 3 * shard : 4 * shard].reshape(width).astype(F32)
    router_t = (
        everyone[:, 4 * shard : (4 + experts) * shard]
        .reshape(groups * ranks, experts, shard)
        .transpose(1, 0, 2)
        .reshape(experts, width)
    )
    my_query_gain = lax.dynamic_slice_in_dim(query_gain, me * columns, columns)
    my_key_gain = lax.dynamic_slice_in_dim(key_gain, me * columns, columns)

    stacked = jnp.concatenate(
        [
            part.reshape(shard, ranks, columns).transpose(1, 0, 2)
            for part in (query_weight, key_weight, value_weight)
        ],
        axis=2,
    )
    stacked = lax.all_to_all(stacked, "expert", split_axis=0, concat_axis=0, tiled=True)
    in_weight = lax.all_gather(stacked.reshape(ranks * shard, 3 * columns), "group", axis=0, tiled=True)
    full_output = lax.all_gather(output_weight, ("group", "expert"), axis=0, tiled=True)

    index, begin, final = layout_of(lengths, seq_order, all_rows)
    starts = begin.reshape(blocks, 1, block)
    lowest = begin.reshape(blocks, block)[:, 0] // block
    highest = final.reshape(blocks, block)[:, block - 1] // block
    position = (index - begin).astype(F32)
    frequency = 10000.0 ** (-(jnp.arange(HEAD_DIM // 2, dtype=F32) * 2.0 / HEAD_DIM))
    angles = position[:, None] * frequency[None, :]
    cosine, sine = jnp.cos(angles), jnp.sin(angles)

    all_routes = share_group(
        jnp.zeros((8, 128), jnp.int32)
        .reshape(-1)
        .at[: rows * TOP]
        .set(routes.T.reshape(-1))
        .reshape(8, 128),
        2,
    )
    all_routes = all_routes.reshape(ranks, -1)[:, : rows * TOP].reshape(ranks, TOP, rows)
    named = jnp.any(all_routes == me, axis=1)
    counted = jnp.cumsum(named.astype(jnp.int32), axis=1) - 1
    slot_of = jnp.where(named, counted, -1)
    pick = (
        slot_of[:, None, :] == jnp.arange(capacity, dtype=jnp.int32)[None, :, None]
    ).astype(BF)

    def select(array):
        return jnp.einsum(
            "rst,rtd->rsd",
            pick,
            array.reshape(ranks, rows, -1),
            preferred_element_type=F32,
        ).astype(BF).reshape(ranks * capacity, -1)

    def place(array):
        return jnp.einsum(
            "rst,rsd->rtd",
            pick,
            array.reshape(ranks, capacity, -1),
            preferred_element_type=F32,
        ).astype(BF).reshape(all_rows, -1)

    all_tokens = ring_gather(tokens, 0)
    tokens_f = all_tokens.astype(F32)
    token_inverse = lax.rsqrt(jnp.mean(tokens_f * tokens_f, axis=-1, keepdims=True) + EPS)
    normed = (tokens_f * token_inverse * attn_gain).astype(BF)
    pre = dot_nn(normed, in_weight)
    query_pre, key_pre, value_pre = (
        pre[:, :columns],
        pre[:, columns : 2 * columns],
        pre[:, 2 * columns :],
    )
    squares = jnp.stack([jnp.sum(query_pre * query_pre, axis=1), jnp.sum(key_pre * key_pre, axis=1)])
    squares = share_group(squares.reshape(-1, 128), 3, add=True).reshape(2, all_rows)
    query_inverse = lax.rsqrt(squares[0] / width + EPS)[:, None]
    key_inverse = lax.rsqrt(squares[1] / width + EPS)[:, None]
    queries = spin(query_pre * query_inverse * my_query_gain, cosine, sine).astype(BF)
    keys = spin(key_pre * key_inverse * my_key_gain, cosine, sine).astype(BF)
    values = value_pre.astype(BF)
    attended_mine, lse = attention_forward(queries, keys, values, starts, lowest)
    all_cot = ring_gather(cotangent, 0)
    attended = ring_gather(attended_mine, 1)

    def own_rows(array):
        return lax.dynamic_slice_in_dim(array, me * rows, rows, 0)

    own_attended = own_rows(attended)
    middle = tokens.astype(F32) + dot_nn(own_attended, full_output)
    middle_inverse = lax.rsqrt(jnp.mean(middle * middle, axis=-1, keepdims=True) + EPS)
    mixed = (middle * middle_inverse * mix_gain).astype(BF)
    logits = dot_nt(mixed, router_t)
    shifted = jnp.exp(logits - jnp.max(logits, axis=1, keepdims=True))
    share = shifted / jnp.sum(shifted, axis=1, keepdims=True)

    middle_e = select(all_tokens).astype(F32) + dot_nn(select(attended), full_output)
    inverse_e = lax.rsqrt(jnp.mean(middle_e * middle_e, axis=-1, keepdims=True) + EPS)
    mixed_e = (middle_e * inverse_e * mix_gain).astype(BF)
    logits_e = dot_nt(mixed_e, router_t)
    shifted_e = jnp.exp(logits_e - jnp.max(logits_e, axis=1, keepdims=True))
    mine_hot = (jnp.arange(experts, dtype=jnp.int32) == me).astype(F32)
    gates_e = (
        jnp.sum(shifted_e * mine_hot, axis=1, keepdims=True)
        / jnp.sum(shifted_e, axis=1, keepdims=True)
    )
    gate_pre = dot_nn(mixed_e, gate_weight[0])
    up_pre = dot_nn(mixed_e, up_weight[0])
    sigma = jax.nn.sigmoid(gate_pre)
    hidden = (gate_pre * sigma * up_pre).astype(BF)
    expert_out = dot_nn(hidden, down_weight[0]).astype(BF)
    out_f = expert_out.astype(F32)
    layer_result = (middle + ring_scatter(place((gates_e * out_f).astype(BF)))).astype(BF)

    cot_e = select(all_cot).astype(F32)
    dcopy = (gates_e * cot_e).astype(BF)
    dgates_e = jnp.sum(out_f * cot_e, axis=1)
    dhidden = dot_nt(dcopy, down_weight[0])
    dgate_pre = (dhidden * up_pre * sigma * (1.0 + gate_pre * (1.0 - sigma))).astype(BF)
    dup_pre = (dhidden * gate_pre * sigma).astype(BF)
    dinputs = (dot_nt(dgate_pre, gate_weight[0]) + dot_nt(dup_pre, up_weight[0])).astype(BF)
    dmixed = ring_scatter(place(dinputs))
    down_term = dot_tn(hidden, dcopy).astype(BF)
    gate_term = dot_tn(mixed_e, dgate_pre).astype(BF)
    up_term = dot_tn(mixed_e, dup_pre).astype(BF)
    gate_sum, up_sum, down_sum = (
        lax.psum(gate_term, "group").astype(F32)[None],
        lax.psum(up_term, "group").astype(F32)[None],
        lax.psum(down_term, "group").astype(F32)[None],
    )

    dgates_t = jnp.sum(
        pick.astype(F32) * dgates_e.reshape(ranks, capacity)[:, :, None], axis=1
    ).reshape(-1, 128)
    dshare = own_rows(share_group(dgates_t, 4).reshape(experts, all_rows).T)
    dlogits = (share * (dshare - jnp.sum(share * dshare, axis=1, keepdims=True))).astype(BF)
    router_term = dot_tn(dlogits, mixed)
    dmixed = dmixed + dot_nn(dlogits, router_t)
    middle_part, mixnorm_term = norm_back(middle, middle_inverse, mix_gain, dmixed)
    dmiddle = cotangent.astype(F32) + middle_part
    dprojected = dmiddle.astype(BF)
    output_term = dot_tn(own_attended, dprojected)
    output_sum = lax.psum_scatter(
        output_term.astype(BF), ("group", "expert"), scatter_dimension=0, tiled=True
    ).astype(F32)
    dattended_own = dot_nt(dprojected, full_output).astype(BF)
    dattended = lax.all_to_all(
        dattended_own.reshape(rows, ranks, columns).transpose(1, 0, 2),
        "expert",
        split_axis=0,
        concat_axis=0,
        tiled=True,
    ).reshape(all_rows, columns)

    heads = columns // HEAD_DIM
    delta = jnp.stack(
        [
            jnp.sum(
                dattended[:, h * HEAD_DIM : (h + 1) * HEAD_DIM].astype(F32)
                * attended_mine[:, h * HEAD_DIM : (h + 1) * HEAD_DIM].astype(F32),
                axis=1,
            )
            for h in range(heads)
        ]
    ).reshape(heads, blocks, 1, block)
    dquery, dkey, dvalue = attention_backward(
        queries, keys, values, dattended, lse, delta, starts, highest
    )
    dquery_n = spin(dquery, cosine, -sine)
    dkey_n = spin(dkey, cosine, -sine)
    query_n = query_pre * query_inverse
    key_n = key_pre * key_inverse
    query_w = dquery_n * my_query_gain
    key_w = dkey_n * my_key_gain
    means = jnp.stack([jnp.sum(query_n * query_w, axis=1), jnp.sum(key_n * key_w, axis=1)])
    means = share_group(means.reshape(-1, 128), 5, add=True).reshape(2, all_rows) / width
    querynorm_term = jnp.sum(dquery_n * query_n, axis=0)
    keynorm_term = jnp.sum(dkey_n * key_n, axis=0)
    dquery_pre = query_inverse * (query_w - query_n * means[0][:, None])
    dkey_pre = key_inverse * (key_w - key_n * means[1][:, None])
    dpre = jnp.concatenate([dquery_pre.astype(BF), dkey_pre.astype(BF), dvalue.astype(BF)], axis=1)
    dnormed = ring_scatter(dot_nt(dpre, in_weight).astype(BF))
    in_term = dot_tn(normed, dpre).astype(BF)
    in_sum = lax.psum_scatter(in_term, "group", scatter_dimension=0, tiled=True)
    in_sum = lax.all_to_all(
        in_sum.reshape(ranks, shard, 3 * columns), "expert", split_axis=0, concat_axis=0, tiled=True
    )
    query_sum, key_sum, value_sum = (
        in_sum[:, :, i * columns : (i + 1) * columns]
        .transpose(1, 0, 2)
        .reshape(shard, width)
        .astype(F32)
        for i in range(3)
    )
    own_f = tokens.astype(F32)
    dinput, attnorm_term = norm_back(own_f, own_rows(token_inverse), attn_gain, dnormed)
    tokens_grad = (dmiddle + dinput).astype(BF)

    def spread(part):
        return lax.dynamic_update_slice(jnp.zeros((width,), F32), part, (me * columns,))

    terms = jnp.concatenate(
        [
            router_term,
            attnorm_term[None],
            spread(querynorm_term)[None],
            spread(keynorm_term)[None],
            mixnorm_term[None],
        ],
        axis=0,
    )
    sums = lax.psum_scatter(terms.T, ("group", "expert"), scatter_dimension=0, tiled=True)
    router_sum = sums[:, :experts]
    gains = sums[:, experts:].T
    return (
        layer_result,
        tokens_grad,
        query_sum,
        key_sum,
        value_sum,
        output_sum,
        router_sum,
        gains[0],
        gains[1],
        gains[2],
        gains[3],
        gate_sum,
        up_sum,
        down_sum,
    )


def solution(mesh):
    rows = P(("group", "expert"), None)
    line = P(("group", "expert"))
    expert = P("expert", None, None)
    group = P("group", None)
    return jax.shard_map(
        body,
        mesh=mesh,
        in_specs=(
            (rows,) * 6 + (line,) * 4 + (expert,) * 3 + (rows, group, group, rows)
        ),
        out_specs=(rows,) * 7 + (line,) * 4 + (expert,) * 3,
        check_vma=False,
    )
```

```python
import functools

import jax
import jax.numpy as jnp
from jax import lax
from jax.experimental import pallas as pl
from jax.experimental.pallas import tpu as pltpu
from jax.sharding import PartitionSpec as P

HEADS = 16
HEAD_DIM = 128
TOP = 2
EPS = 1e-05
NEG = -1e30
MESH = pl.DeviceIdType.MESH
BF = jnp.bfloat16
F32 = jnp.float32


def cost(microseconds):
    return pl.CostEstimate(
        flops=int(microseconds * 1e6), bytes_accessed=1 << 16, transcendentals=0
    )


def row_sums(x):
    ones = jnp.ones((8, x.shape[1]), BF)
    high = x.astype(BF)
    low = (x - high.astype(F32)).astype(BF)
    contract = (((1,), (1,)), ((), ()))
    return (
        lax.dot_general(ones, high, contract, preferred_element_type=F32)
        + lax.dot_general(ones, low, contract, preferred_element_type=F32)
    )[:1]


def exchange_small(collective_id, world=None, group=None, added=None):
    groups, ranks = lax.axis_size("group"), lax.axis_size("expert")
    total = groups * ranks
    near_blocks = [block for block in (group, added) if block is not None]
    count = len(near_blocks)

    def kernel(*refs):
        refs = list(refs)
        world_in = refs.pop(0) if world is not None else None
        near_in = [refs.pop(0) for _ in range(count)]
        world_out = refs.pop(0) if world is not None else None
        near_out = [refs.pop(0) for _ in range(count)]
        rank = lax.axis_index("expert")
        me = lax.axis_index("group") * ranks + rank
        barrier = pltpu.get_barrier_semaphore()

        def far(step):
            flat = lax.rem(me + step, total)
            return (flat // ranks, lax.rem(flat, ranks))

        def near(step):
            return {"expert": lax.rem(rank + step, ranks)}

        if world is not None:

            def greet(step, carry):
                pl.semaphore_signal(barrier, inc=1, device_id=far(step), device_id_type=MESH)
                return carry

            lax.fori_loop(1, total, greet, 0)
            pl.semaphore_wait(barrier, total - 1)
        else:
            for step in range(1, ranks):
                pl.semaphore_signal(barrier, inc=1, device_id=near(step), device_id_type=MESH)
            pl.semaphore_wait(barrier, ranks - 1)
        lands = list(near_out)
        if added is not None:
            lands[-1] = refs.pop(0)
        if count:
            near_send, near_recv = refs.pop(0), refs.pop(0)
        near_copies = []
        for which in range(count):
            for step in range(1, ranks):
                copy = pltpu.make_async_remote_copy(
                    src_ref=near_in[which],
                    dst_ref=lands[which].at[rank],
                    send_sem=near_send.at[which, step],
                    recv_sem=near_recv.at[which, step],
                    device_id=near(step),
                    device_id_type=MESH,
                )
                copy.start()
                near_copies.append(copy)
            lands[which][rank] = near_in[which][...]
        if world is not None:
            far_send, far_recv = refs.pop(0), refs.pop(0)

            def far_copy(step):
                return pltpu.make_async_remote_copy(
                    src_ref=world_in,
                    dst_ref=world_out.at[me],
                    send_sem=far_send.at[step],
                    recv_sem=far_recv.at[step],
                    device_id=far(step),
                    device_id_type=MESH,
                )

            def send(step, carry):
                far_copy(step).start()
                return carry

            lax.fori_loop(1, total, send, 0)
            world_out[me] = world_in[...]

            def settle(step, carry):
                far_copy(step).wait()
                return carry

            lax.fori_loop(1, total, settle, 0)
        for copy in near_copies:
            copy.wait()
        if added is not None:
            summed = lands[-1][0]
            for other in range(1, ranks):
                summed = summed + lands[-1][other]
            near_out[-1][...] = summed

    inputs, outputs, scratch = [], [], []
    if world is not None:
        inputs.append(world)
        outputs.append(jax.ShapeDtypeStruct((total,) + world.shape, world.dtype))
    if group is not None:
        inputs.append(group)
        outputs.append(jax.ShapeDtypeStruct((ranks,) + group.shape, group.dtype))
    if added is not None:
        inputs.append(added)
        outputs.append(jax.ShapeDtypeStruct(added.shape, added.dtype))
        scratch.append(pltpu.VMEM((ranks,) + added.shape, added.dtype))
    if count:
        scratch += [pltpu.SemaphoreType.DMA((count, ranks))] * 2
    if world is not None:
        scratch += [pltpu.SemaphoreType.DMA((total,)), pltpu.SemaphoreType.DMA((total,))]
    vmem = pl.BlockSpec(memory_space=pltpu.VMEM)
    return pl.pallas_call(
        kernel,
        out_shape=tuple(outputs),
        in_specs=[vmem] * len(inputs),
        out_specs=tuple([vmem] * len(outputs)),
        scratch_shapes=scratch,
        compiler_params=pltpu.CompilerParams(collective_id=collective_id, has_side_effects=True),
        name="exchange_small",
    )(*inputs)


def tie(*trees):
    leaves, shape = jax.tree.flatten(trees)
    return jax.tree.unflatten(shape, lax.optimization_barrier(leaves))


def partner_swap(block):
    ranks = lax.axis_size("expert")
    return lax.ppermute(block, "expert", [(i, i ^ 1) for i in range(ranks)])


def chip_shift(block, step=1):
    ranks = lax.axis_size("expert")
    return lax.ppermute(block, "expert", [(i, (i + 2 * step) % ranks) for i in range(ranks)])


def place_of():
    ranks = lax.axis_size("expert")
    me = lax.axis_index("expert")
    return ranks // 2, me // 2, me % 2


def source_chip(step):
    chips, chip, _ = place_of()
    return lax.rem(chip - step + chips, chips)


def assemble(pieces, axis):
    _, _, core = place_of()
    first = pieces[0][0]
    size = first.shape[axis]
    shape = list(first.shape)
    shape[axis] = size * 2 * len(pieces)
    whole = jnp.zeros(shape, first.dtype)
    for step, (mine, other) in enumerate(pieces):
        at = source_chip(step) * 2
        whole = lax.dynamic_update_slice_in_dim(whole, mine, (at + core) * size, axis)
        whole = lax.dynamic_update_slice_in_dim(whole, other, (at + 1 - core) * size, axis)
    return whole


def exchange_chips(blocks):
    chips, chip, core = place_of()
    pairs = blocks.reshape((chips, 2) + blocks.shape[1:])
    keep, give = [], []
    for step in range(chips):
        pair = lax.dynamic_index_in_dim(pairs, lax.rem(chip + step, chips), 0, keepdims=False)
        if step:
            pair = chip_shift(pair, step)
        keep.append(lax.dynamic_index_in_dim(pair, core, 0))
        give.append(lax.dynamic_index_in_dim(pair, 1 - core, 0))
    return keep, jnp.concatenate(give, axis=0)


def exchange_cores(keep, give):
    given = partner_swap(give)
    return assemble([(part, given[i : i + 1]) for i, part in enumerate(keep)], 0)


def rank_exchange(blocks):
    return exchange_cores(*exchange_chips(blocks))


def add3(arrived, mine, swapped):
    return (arrived.astype(F32) + mine.astype(F32) + swapped.astype(F32)).astype(BF)


def add2(mine, swapped):
    return (mine.astype(F32) + swapped.astype(F32)).astype(BF)


def attention_forward(queries, keys, values, starts, lowest):
    rows = queries.shape[0]
    heads = queries.shape[1] // HEAD_DIM
    blocks, _, block = starts.shape
    scale = HEAD_DIM ** (-0.5)

    def kernel(low_ref, start_ref, q_ref, k_ref, v_ref, o_ref, lse_ref):
        i = pl.program_id(1)
        q = q_ref[...]
        start = start_ref[0]
        q_index = i * block + lax.broadcasted_iota(jnp.int32, (1, block), 1)
        k_local = lax.broadcasted_iota(jnp.int32, (block, block), 0)

        def step(j, carry):
            top, total, acc = carry
            at = pl.multiple_of(j * block, block)
            k = k_ref[pl.ds(at, block), :]
            v = v_ref[pl.ds(at, block), :]
            s = (
                lax.dot_general(k, q, (((1,), (1,)), ((), ())), preferred_element_type=F32)
                * scale
            )
            k_index = k_local + j * block
            s = jnp.where((k_index <= q_index) & (k_index >= start), s, NEG)
            new_top = jnp.maximum(top, jnp.max(s, axis=0, keepdims=True))
            p = jnp.exp(s - new_top)
            shrink = jnp.exp(top - new_top)
            total = total * shrink + jnp.sum(p, axis=0, keepdims=True)
            acc = acc * shrink + lax.dot_general(
                v, p.astype(BF), (((0,), (0,)), ((), ())), preferred_element_type=F32
            )
            return (new_top, total, acc)

        top, total, acc = lax.fori_loop(
            low_ref[i],
            i + 1,
            step,
            (
                jnp.full((1, block), NEG, F32),
                jnp.zeros((1, block), F32),
                jnp.zeros((HEAD_DIM, block), F32),
            ),
        )
        o_ref[...] = (acc / total).T.astype(BF)
        lse_ref[0, 0] = top + jnp.log(total)

    return pl.pallas_call(
        kernel,
        out_shape=(
            jax.ShapeDtypeStruct((rows, heads * HEAD_DIM), BF),
            jax.ShapeDtypeStruct((heads, blocks, 1, block), F32),
        ),
        grid_spec=pltpu.PrefetchScalarGridSpec(
            num_scalar_prefetch=1,
            grid=(heads, blocks),
            in_specs=[
                pl.BlockSpec((1, 1, block), lambda h, i, low: (i, 0, 0)),
                pl.BlockSpec((block, HEAD_DIM), lambda h, i, low: (i, h)),
                pl.BlockSpec((rows, HEAD_DIM), lambda h, i, low: (0, h)),
                pl.BlockSpec((rows, HEAD_DIM), lambda h, i, low: (0, h)),
            ],
            out_specs=[
                pl.BlockSpec((block, HEAD_DIM), lambda h, i, low: (i, h)),
                pl.BlockSpec((1, 1, 1, block), lambda h, i, low: (h, i, 0, 0)),
            ],
        ),
        compiler_params=pltpu.CompilerParams(vmem_limit_bytes=48 << 20),
        cost_estimate=cost(35),
        name="attention_forward",
    )(lowest, starts, queries, keys, values)


def attention_backward(queries, keys, values, douts, lse, delta, starts, highest):
    rows = queries.shape[0]
    heads = queries.shape[1] // HEAD_DIM
    blocks, _, block = starts.shape
    scale = HEAD_DIM ** (-0.5)

    def kernel(
        high_ref,
        start_ref,
        q_ref,
        do_ref,
        k_ref,
        v_ref,
        lse_ref,
        delta_ref,
        dq_ref,
        dk_ref,
        dv_ref,
        q_sum_ref,
        k_sum_ref,
    ):
        j = pl.program_id(1)

        @pl.when(j == 0)
        def _():
            dq_ref[...] = jnp.zeros_like(dq_ref)

        k = k_ref[...]
        v = v_ref[...]
        k_index = j * block + lax.broadcasted_iota(jnp.int32, (block, block), 0)
        q_local = lax.broadcasted_iota(jnp.int32, (1, block), 1)

        def step(i, carry):
            dk, dv = carry
            at = pl.multiple_of(i * block, block)
            q = q_ref[pl.ds(at, block), :]
            do = do_ref[pl.ds(at, block), :]
            s = (
                lax.dot_general(k, q, (((1,), (1,)), ((), ())), preferred_element_type=F32)
                * scale
            )
            allowed = (k_index <= q_local + i * block) & (k_index >= start_ref[i])
            p = jnp.exp(jnp.where(allowed, s, NEG) - lse_ref[0, i])
            dv = dv + jnp.dot(p.astype(BF), do, preferred_element_type=F32)
            dp = lax.dot_general(v, do, (((1,), (1,)), ((), ())), preferred_element_type=F32)
            ds = (p * (dp - delta_ref[0, i])).astype(BF)
            dk = dk + jnp.dot(ds, q, preferred_element_type=F32)
            dq_ref[pl.ds(at, block), :] += (
                lax.dot_general(ds, k, (((0,), (0,)), ((), ())), preferred_element_type=F32)
                * scale
            )
            return (dk, dv)

        zero = jnp.zeros((block, HEAD_DIM), F32)
        dk, dv = lax.fori_loop(j, high_ref[j] + 1, step, (zero, zero))
        dk = dk * scale
        dk_ref[...] = dk
        dv_ref[...] = dv.astype(BF)
        k_sum_ref[0, 0] = row_sums(k.astype(F32) * dk)

        @pl.when(j == pl.num_programs(1) - 1)
        def _():
            for i in range(blocks):
                at = slice(i * block, (i + 1) * block)
                q_sum_ref[0, i] = row_sums(q_ref[at, :].astype(F32) * dq_ref[at, :])

    whole = pl.BlockSpec((rows, HEAD_DIM), lambda h, j, high: (0, h))
    part = pl.BlockSpec((block, HEAD_DIM), lambda h, j, high: (j, h))
    line = pl.BlockSpec((1, blocks, 1, block), lambda h, j, high: (h, 0, 0, 0))
    shape = jax.ShapeDtypeStruct((rows, heads * HEAD_DIM), F32)
    return pl.pallas_call(
        kernel,
        out_shape=(
            shape,
            shape,
            jax.ShapeDtypeStruct(shape.shape, BF),
            jax.ShapeDtypeStruct((heads, blocks, 1, block), F32),
            jax.ShapeDtypeStruct((heads, blocks, 1, block), F32),
        ),
        grid_spec=pltpu.PrefetchScalarGridSpec(
            num_scalar_prefetch=1,
            grid=(heads, blocks),
            in_specs=[
                pl.BlockSpec((blocks, 1, block), lambda h, j, high: (0, 0, 0)),
                whole,
                whole,
                part,
                part,
                line,
                line,
            ],
            out_specs=[
                whole,
                part,
                part,
                line,
                pl.BlockSpec((1, 1, 1, block), lambda h, j, high: (h, j, 0, 0)),
            ],
        ),
        compiler_params=pltpu.CompilerParams(vmem_limit_bytes=48 << 20),
        cost_estimate=cost(46),
        name="attention_backward",
    )(highest, starts, queries, douts, keys, values, lse, delta)


def gather_heads(tokens, pick, mine, other, source, core, out_weight, whole):
    ranks, capacity, rows = pick.shape
    columns = mine.shape[1]
    width = out_weight.shape[1]
    first = whole is None
    pair = 2 * capacity

    def kernel(at_ref, base_ref, pick_ref, mine_ref, other_ref, w_ref, out_ref, parts):
        core = at_ref[1]
        for half in range(2):
            at = half * capacity
            chosen = pick_ref[half]
            spots = slice(half * rows, (half + 1) * rows)
            if first:
                out_ref[at : at + capacity, :] = jnp.dot(
                    chosen, base_ref[spots, :], preferred_element_type=F32
                )
            for part_ref, which in ((mine_ref, core), (other_ref, 1 - core)):
                parts[
                    at : at + capacity, pl.ds(pl.multiple_of(which * columns, columns), columns)
                ] = jnp.dot(chosen, part_ref[spots, :], preferred_element_type=F32).astype(BF)
        base = out_ref if first else base_ref
        out_ref[...] = base[...] + jnp.dot(
            parts[...], w_ref[...], preferred_element_type=F32
        )

    heads_spec = pl.BlockSpec((2 * rows, columns), lambda r, at: (r, 0))
    total_spec = pl.BlockSpec((pair, width), lambda r, at: (r, 0))
    return pl.pallas_call(
        kernel,
        out_shape=jax.ShapeDtypeStruct((ranks * capacity, width), F32),
        grid_spec=pltpu.PrefetchScalarGridSpec(
            num_scalar_prefetch=1,
            grid=(ranks // 2,),
            in_specs=[
                pl.BlockSpec((2 * rows, width), lambda r, at: (r, 0)) if first else total_spec,
                pl.BlockSpec((2, capacity, rows), lambda r, at: (r, 0, 0)),
                heads_spec,
                heads_spec,
                pl.BlockSpec((2 * columns, width), lambda r, at: (at[0], 0)),
            ],
            out_specs=total_spec,
            scratch_shapes=[pltpu.VMEM((pair, 2 * columns), BF)],
        ),
        input_output_aliases={} if first else {1: 0},
        compiler_params=pltpu.CompilerParams(vmem_limit_bytes=40 << 20),
        cost_estimate=cost(8),
        name="gather_heads",
    )(
        jnp.stack([source, core]).astype(jnp.int32),
        tokens if first else whole,
        pick,
        mine,
        other,
        out_weight,
    )


def expert_forward(
    order, whole, pick, pick_t, mine, other, out_weight, mix_gain, router, hot, gate_w, up_w, down_w
):
    ranks, capacity, rows = pick.shape
    columns = mine.shape[1]
    width = out_weight.shape[1]
    hidden_width = gate_w.shape[1]
    chips = ranks // 2
    pair = 2 * capacity

    def kernel(
        order_ref,
        base_ref,
        pick_ref,
        turned_ref,
        mine_ref,
        other_ref,
        wo_ref,
        gain_ref,
        router_ref,
        hot_ref,
        wg_ref,
        wu_ref,
        wd_ref,
        mixed_ref,
        gates_ref,
        gate_ref,
        up_ref,
        hidden_ref,
        out_ref,
        own_ref,
        away_ref,
        scratch,
        parts,
    ):
        core = order_ref[2 * chips + 1]
        for half in range(2):
            at = half * capacity
            for part_ref, which in ((mine_ref, core), (other_ref, 1 - core)):
                parts[
                    at : at + capacity, pl.ds(pl.multiple_of(which * columns, columns), columns)
                ] = jnp.dot(
                    pick_ref[half],
                    part_ref[half * rows : (half + 1) * rows, :],
                    preferred_element_type=F32,
                ).astype(BF)
        total = base_ref[...] + jnp.dot(parts[...], wo_ref[...], preferred_element_type=F32)
        inverse = lax.rsqrt(jnp.mean(total * total, axis=1, keepdims=True) + EPS)
        mixed = (total * inverse * gain_ref[...]).astype(BF)
        mixed_ref[...] = mixed
        logits = lax.dot_general(
            mixed, router_ref[...], (((1,), (1,)), ((), ())), preferred_element_type=F32
        )
        lane = lax.broadcasted_iota(jnp.int32, logits.shape, 1)
        logits = jnp.where(lane < ranks, logits, NEG)
        shifted = jnp.exp(logits - jnp.max(logits, axis=1, keepdims=True))
        gates = jnp.sum(shifted * hot_ref[...], axis=1, keepdims=True) / jnp.sum(
            shifted, axis=1, keepdims=True
        )
        gates_ref[...] = jnp.broadcast_to(gates, gates_ref.shape)
        gate = jnp.dot(mixed, wg_ref[...], preferred_element_type=F32)
        gate_ref[...] = gate
        up = jnp.dot(mixed, wu_ref[...], preferred_element_type=F32)
        up_ref[...] = up
        hidden = (gate * jax.nn.sigmoid(gate) * up).astype(BF)
        hidden_ref[...] = hidden
        result = jnp.dot(hidden, wd_ref[...], preferred_element_type=F32).astype(BF)
        out_ref[...] = result
        scratch[...] = (gates * result.astype(F32)).astype(BF)
        for half, place_ref in ((core, own_ref), (1 - core, away_ref)):
            at = pl.ds(pl.multiple_of(half * capacity, capacity), capacity)
            place_ref[0] = jnp.dot(
                turned_ref[half], scratch[at, :], preferred_element_type=F32
            ).astype(BF)

    def chip_rows(n, m):
        return pl.BlockSpec((n, m), lambda i, order: (order[i], 0))

    def fixed(n, m):
        return pl.BlockSpec((n, m), lambda i, order: (0, 0), pipeline_mode=pl.Buffered(1))

    def slot(i, order):
        return (order[chips + i], 0, 0)

    all_slots = ranks * capacity
    return pl.pallas_call(
        kernel,
        out_shape=(
            jax.ShapeDtypeStruct((all_slots, width), BF),
            jax.ShapeDtypeStruct((all_slots, 128), F32),
            jax.ShapeDtypeStruct((all_slots, hidden_width), F32),
            jax.ShapeDtypeStruct((all_slots, hidden_width), F32),
            jax.ShapeDtypeStruct((all_slots, hidden_width), BF),
            jax.ShapeDtypeStruct((all_slots, width), BF),
            jax.ShapeDtypeStruct((chips, rows, width), BF),
            jax.ShapeDtypeStruct((chips, rows, width), BF),
        ),
        grid_spec=pltpu.PrefetchScalarGridSpec(
            num_scalar_prefetch=1,
            grid=(chips,),
            in_specs=[
                chip_rows(pair, width),
                pl.BlockSpec((2, capacity, rows), lambda i, order: (order[i], 0, 0)),
                pl.BlockSpec((2, rows, capacity), lambda i, order: (order[i], 0, 0)),
                chip_rows(2 * rows, columns),
                chip_rows(2 * rows, columns),
                pl.BlockSpec(
                    (2 * columns, width),
                    lambda i, order: (order[2 * chips], 0),
                    pipeline_mode=pl.Buffered(1),
                ),
                fixed(1, width),
                fixed(128, width),
                fixed(1, 128),
                fixed(width, hidden_width),
                fixed(width, hidden_width),
                fixed(hidden_width, width),
            ],
            out_specs=[
                chip_rows(pair, width),
                chip_rows(pair, 128),
                chip_rows(pair, hidden_width),
                chip_rows(pair, hidden_width),
                chip_rows(pair, hidden_width),
                chip_rows(pair, width),
                pl.BlockSpec((1, rows, width), slot),
                pl.BlockSpec((1, rows, width), slot),
            ],
            scratch_shapes=[pltpu.VMEM((pair, width), BF), pltpu.VMEM((pair, 2 * columns), BF)],
        ),
        compiler_params=pltpu.CompilerParams(vmem_limit_bytes=58 << 20),
        cost_estimate=cost(45),
        name="expert_forward",
    )(
        order.astype(jnp.int32),
        whole,
        pick,
        pick_t,
        mine,
        other,
        out_weight,
        mix_gain,
        router,
        hot,
        gate_w,
        up_w,
        down_w,
    )


def expert_backward(
    sources, core, rank, pick, pick_t, cotangents, gates, gate, up, hidden, result, weights, whole
):
    ranks, capacity, rows = pick.shape
    count = len(sources)
    width = cotangents[0][0].shape[1]
    hidden_width = weights[0].shape[1]
    pair = 2 * capacity
    wide = width + 128

    def kernel(at_ref, pick_ref, turned_ref, *refs):
        cots = refs[: 2 * count]
        gates_ref, gate_ref, up_ref, out_ref, wg_ref, wu_ref, wd_ref = refs[2 * count : 2 * count + 7]
        own_ref, away_ref, dcopy_ref, dgate_ref, dup_ref, rows_s, back_s, gates_s = refs[-8:]
        core, rank = at_ref[count], at_ref[count + 1]
        step = pl.program_id(0)

        for which in range(count):

            @pl.when(step == which)
            def _(which=which):
                for half, part_ref in ((core, cots[2 * which]), (1 - core, cots[2 * which + 1])):
                    at = pl.ds(pl.multiple_of(half * capacity, capacity), capacity)
                    rows_s[at, :] = jnp.dot(
                        pick_ref[half], part_ref[...], preferred_element_type=F32
                    )

        incoming = rows_s[...]
        dgates = jnp.sum(out_ref[...].astype(F32) * incoming, axis=1, keepdims=True)
        high = dgates.astype(BF)
        low = (dgates - high.astype(F32)).astype(BF)
        lane = lax.broadcasted_iota(jnp.int32, (pair, 128), 1)
        gates_s[...] = jnp.where(
            lane == rank,
            high.astype(F32),
            jnp.where(lane == rank + ranks, low.astype(F32), 0.0),
        ).astype(BF)
        dcopy = (gates_ref[:, :1] * incoming).astype(BF)
        dcopy_ref[...] = dcopy
        dhidden = lax.dot_general(
            dcopy, wd_ref[...], (((1,), (1,)), ((), ())), preferred_element_type=F32
        )
        gate, up = gate_ref[...], up_ref[...]
        sigma = jax.nn.sigmoid(gate)
        scaled = dhidden * sigma
        dgate = (scaled * up * (1.0 + gate * (1.0 - sigma))).astype(BF)
        dup = (scaled * gate).astype(BF)
        dgate_ref[...] = dgate
        dup_ref[...] = dup
        back_s[...] = (
            lax.dot_general(
                dgate, wg_ref[...], (((1,), (1,)), ((), ())), preferred_element_type=F32
            )
            + lax.dot_general(
                dup, wu_ref[...], (((1,), (1,)), ((), ())), preferred_element_type=F32
            )
        ).astype(BF)
        for half, place_ref in ((core, own_ref), (1 - core, away_ref)):
            at = pl.ds(pl.multiple_of(half * capacity, capacity), capacity)
            turned = turned_ref[half]
            place_ref[0, :, :width] = jnp.dot(
                turned, back_s[at, :], preferred_element_type=F32
            ).astype(BF)
            place_ref[0, :, width:] = jnp.dot(
                turned, gates_s[at, :], preferred_element_type=F32
            ).astype(BF)

    def chip_rows(n, m):
        return pl.BlockSpec((n, m), lambda i, at: (at[i], 0))

    def fixed(n, m):
        return pl.BlockSpec((n, m), lambda i, at: (0, 0), pipeline_mode=pl.Buffered(1))

    extra = [] if whole is None else list(whole)
    all_slots = ranks * capacity
    piece = pl.BlockSpec((1, rows, wide), lambda i, at: (i, 0, 0))
    return pl.pallas_call(
        kernel,
        out_shape=(
            jax.ShapeDtypeStruct((count, rows, wide), BF),
            jax.ShapeDtypeStruct((count, rows, wide), BF),
            jax.ShapeDtypeStruct((all_slots, width), BF),
            jax.ShapeDtypeStruct((all_slots, hidden_width), BF),
            jax.ShapeDtypeStruct((all_slots, hidden_width), BF),
        ),
        grid_spec=pltpu.PrefetchScalarGridSpec(
            num_scalar_prefetch=1,
            grid=(count,),
            in_specs=[
                pl.BlockSpec((2, capacity, rows), lambda i, at: (at[i], 0, 0)),
                pl.BlockSpec((2, rows, capacity), lambda i, at: (at[i], 0, 0)),
            ]
            + [fixed(rows, width)] * (2 * count)
            + [
                chip_rows(pair, 128),
                chip_rows(pair, hidden_width),
                chip_rows(pair, hidden_width),
                chip_rows(pair, width),
                fixed(width, hidden_width),
                fixed(width, hidden_width),
                fixed(hidden_width, width),
            ]
            + [pl.BlockSpec(memory_space=pl.ANY)] * len(extra),
            out_specs=[
                piece,
                piece,
                chip_rows(pair, width),
                chip_rows(pair, hidden_width),
                chip_rows(pair, hidden_width),
            ],
            scratch_shapes=[
                pltpu.VMEM((pair, width), F32),
                pltpu.VMEM((pair, width), BF),
                pltpu.VMEM((pair, 128), BF),
            ],
        ),
        input_output_aliases={10 + 2 * count + i: 2 + i for i in range(len(extra))},
        compiler_params=pltpu.CompilerParams(vmem_limit_bytes=60 << 20),
        cost_estimate=cost(12 * count),
        name="expert_backward",
    )(
        jnp.stack(list(sources) + [core, rank]).astype(jnp.int32),
        pick,
        pick_t,
        *[part for parts in cotangents for part in parts],
        gates,
        gate,
        up,
        result,
        *weights,
        *extra,
    )


def owner_backward(
    arrived, mine, swapped, share, router, middle, inverse, mix_gain, cotangent, out_weight
):
    rows, width = middle.shape
    ranks = lax.axis_size("expert")
    columns = width // ranks
    wide = arrived.shape[1]
    tile = rows // 2

    def kernel(
        arrived_ref,
        mine_ref,
        swapped_ref,
        share_ref,
        router_ref,
        middle_ref,
        inverse_ref,
        gain_ref,
        cot_ref,
        w_ref,
        dlogits_ref,
        norm_ref,
        dmiddle_ref,
        dprojected_ref,
        dattended_ref,
    ):
        @pl.when(pl.program_id(0) == 0)
        def _():
            norm_ref[...] = jnp.zeros_like(norm_ref)

        total = (
            arrived_ref[...].astype(F32)
            + mine_ref[...].astype(F32)
            + swapped_ref[...].astype(F32)
        )
        share = share_ref[...]
        dshare = total[:, width:]
        dshare = dshare + pltpu.roll(dshare, 128 - ranks, 1)
        dlogits = (
            share * (dshare - jnp.sum(share * dshare, axis=1, keepdims=True))
        ).astype(BF)
        dlogits_ref[...] = dlogits
        dmixed = total[:, :width] + jnp.dot(
            dlogits, router_ref[...], preferred_element_type=F32
        )
        inverse = inverse_ref[:, :1]
        scaled = middle_ref[...] * inverse
        weighted = dmixed * gain_ref[...]
        norm_ref[:1, :] += jnp.sum(dmixed * scaled, axis=0, keepdims=True)
        mean = jnp.mean(scaled * weighted, axis=1, keepdims=True)
        dmiddle = cot_ref[...].astype(F32) + inverse * (weighted - scaled * mean)
        dmiddle_ref[...] = dmiddle
        dprojected = dmiddle.astype(BF)
        dprojected_ref[...] = dprojected
        dattended = lax.dot_general(
            dprojected, w_ref[...], (((1,), (1,)), ((), ())), preferred_element_type=F32
        ).astype(BF)
        for rank in range(ranks):
            dattended_ref[rank] = dattended[:, rank * columns : (rank + 1) * columns]

    def rows_of(n):
        return pl.BlockSpec((tile, n), lambda i: (i, 0))

    def fixed(n, m):
        return pl.BlockSpec((n, m), lambda i: (0, 0))

    return pl.pallas_call(
        kernel,
        out_shape=(
            jax.ShapeDtypeStruct((rows, 128), BF),
            jax.ShapeDtypeStruct((8, width), F32),
            jax.ShapeDtypeStruct((rows, width), F32),
            jax.ShapeDtypeStruct((rows, width), BF),
            jax.ShapeDtypeStruct((ranks, rows, columns), BF),
        ),
        grid=(rows // tile,),
        in_specs=[
            rows_of(wide),
            rows_of(wide),
            rows_of(wide),
            rows_of(128),
            fixed(128, width),
            rows_of(width),
            rows_of(128),
            fixed(1, width),
            rows_of(width),
            fixed(width, width),
        ],
        out_specs=(
            rows_of(128),
            fixed(8, width),
            rows_of(width),
            rows_of(width),
            pl.BlockSpec((ranks, tile, columns), lambda i: (0, i, 0)),
        ),
        compiler_params=pltpu.CompilerParams(vmem_limit_bytes=48 << 20),
        cost_estimate=cost(14),
        name="owner_backward",
    )(
        arrived, mine, swapped, share, router, middle, inverse, mix_gain, cotangent, out_weight
    )


def project_in(mine, other, chip, core, weight, whole):
    rows, width = mine.shape
    columns = weight.shape[1] // 3
    ranks = lax.axis_size("expert")

    def kernel(at_ref, mine_ref, other_ref, w_ref, *refs):
        x_out, n_out, p_out, v_out, s_out = refs[-5:]
        core = at_ref[1]

        def handle(x_ref, half):
            at = pl.ds(pl.multiple_of(half * rows, rows), rows)
            x = x_ref[...]
            xf = x.astype(F32)
            n = (xf * lax.rsqrt(jnp.mean(xf * xf, axis=1, keepdims=True) + EPS)).astype(BF)
            x_out[at, :] = x
            n_out[at, :] = n
            product = jnp.dot(n, w_ref[...], preferred_element_type=F32)
            p_out[at, :] = product[:, : 2 * columns]
            v_out[at, :] = product[:, 2 * columns :].astype(BF)
            for which in range(2):
                part = product[:, which * columns : (which + 1) * columns]
                s_out[half, which : which + 1, :] = row_sums(part * part)

        handle(mine_ref, core)
        handle(other_ref, 1 - core)

    shapes = (
        jax.ShapeDtypeStruct((rows * ranks, width), BF),
        jax.ShapeDtypeStruct((rows * ranks, width), BF),
        jax.ShapeDtypeStruct((rows * ranks, 2 * columns), F32),
        jax.ShapeDtypeStruct((rows * ranks, columns), BF),
        jax.ShapeDtypeStruct((ranks, 2, rows), F32),
    )
    out_specs = [
        pl.BlockSpec((2 * rows, shape.shape[1]), lambda i, at: (at[0], 0)) for shape in shapes[:4]
    ] + [pl.BlockSpec((2, 2, rows), lambda i, at: (at[0], 0, 0))]
    extra = [] if whole is None else list(whole)
    full = pl.BlockSpec((rows, width), lambda i, at: (0, 0))
    return pl.pallas_call(
        kernel,
        out_shape=shapes,
        grid_spec=pltpu.PrefetchScalarGridSpec(
            num_scalar_prefetch=1,
            grid=(1,),
            in_specs=[full, full, pl.BlockSpec((width, 3 * columns), lambda i, at: (0, 0))]
            + [pl.BlockSpec(memory_space=pl.ANY)] * len(extra),
            out_specs=out_specs,
        ),
        input_output_aliases={4 + i: i for i in range(len(extra))},
        compiler_params=pltpu.CompilerParams(vmem_limit_bytes=48 << 20),
        cost_estimate=cost(8),
        name="project_in",
    )(jnp.stack([chip, core]).astype(jnp.int32), mine, other, weight, *extra)


def column_of(pair, function):
    pair = function(pair)
    return jnp.concatenate([pair, jnp.zeros((6, pair.shape[1]), F32)], axis=0).T


def make_heads(products, squares, gains, cosine, sine, width):
    rows = products.shape[0]
    columns = products.shape[1] // 2
    tile = squares.shape[2]

    def kernel(p_ref, s_ref, g_ref, c_ref, n_ref, q_ref, k_ref):
        cos, sin = c_ref[...], n_ref[...]
        inverses = column_of(s_ref[0], lambda total: lax.rsqrt(total / width + EPS))
        for which, out in ((0, q_ref), (1, k_ref)):
            inverse = inverses[:, which : which + 1]
            for h in range(0, columns, HEAD_DIM):
                x = p_ref[:, which * columns + h : which * columns + h + HEAD_DIM]
                x = x * inverse * g_ref[which : which + 1, h : h + HEAD_DIM]
                out[:, h : h + HEAD_DIM] = (
                    x * cos + pltpu.roll(x, HEAD_DIM // 2, 1) * sin
                ).astype(BF)

    def rows_of(n):
        return pl.BlockSpec((tile, n), lambda i: (i, 0))

    shape = jax.ShapeDtypeStruct((rows, columns), BF)
    return pl.pallas_call(
        kernel,
        out_shape=(shape, shape),
        grid=(rows // tile,),
        in_specs=[
            rows_of(2 * columns),
            pl.BlockSpec((1, 2, tile), lambda i: (i, 0, 0)),
            pl.BlockSpec((2, columns), lambda i: (0, 0)),
            rows_of(HEAD_DIM),
            rows_of(HEAD_DIM),
        ],
        out_specs=[rows_of(columns)] * 2,
        cost_estimate=cost(8),
        name="make_heads",
    )(products, squares, gains, cosine, sine)


def project_back(
    sources, core, products, squares, gains, cosine, sine, dq, dk, dv, means, weight, whole
):
    all_rows = products.shape[0]
    columns = products.shape[1] // 2
    rows = squares.shape[2]
    width = weight.shape[0]
    count = len(sources)

    def kernel(at_ref, p_ref, s_ref, m_ref, g_ref, c_ref, n_ref, dq_ref, dk_ref, dv_ref, w_ref, *refs):
        out_ref, own_ref, away_ref, gain_ref = refs[-4:]
        core = at_ref[count]

        @pl.when(pl.program_id(0) == 0)
        def _():
            gain_ref[...] = jnp.zeros_like(gain_ref)

        for half, place_ref in ((core, own_ref), (1 - core, away_ref)):
            at = pl.ds(pl.multiple_of(half * rows, rows), rows)
            cos, sin = c_ref[at, :], n_ref[at, :]
            inverses = column_of(s_ref[half], lambda total: lax.rsqrt(total / width + EPS))
            mean = column_of(m_ref[half], lambda total: total / width)
            for which, d_ref in ((0, dq_ref), (1, dk_ref)):
                inverse = inverses[:, which : which + 1]
                for h in range(0, columns, HEAD_DIM):
                    here = which * columns + h
                    scaled = p_ref[at, here : here + HEAD_DIM] * inverse
                    d = d_ref[at, h : h + HEAD_DIM]
                    d = d * cos - pltpu.roll(d, HEAD_DIM // 2, 1) * sin
                    weighted = d * g_ref[which : which + 1, h : h + HEAD_DIM]
                    gain_ref[which : which + 1, h : h + HEAD_DIM] += jnp.sum(
                        d * scaled, axis=0, keepdims=True
                    )
                    out_ref[at, here : here + HEAD_DIM] = (
                        inverse * (weighted - scaled * mean[:, which : which + 1])
                    ).astype(BF)
            out_ref[at, 2 * columns :] = dv_ref[at, :]
            place_ref[0] = lax.dot_general(
                out_ref[at, :], w_ref[...], (((1,), (1,)), ((), ())), preferred_element_type=F32
            ).astype(BF)

    def chip_rows(n):
        return pl.BlockSpec((2 * rows, n), lambda i, at: (at[i], 0))

    pair = pl.BlockSpec((2, 2, rows), lambda i, at: (at[i], 0, 0))
    piece = pl.BlockSpec((1, rows, width), lambda i, at: (i, 0, 0))
    extra = [] if whole is None else [whole]
    return pl.pallas_call(
        kernel,
        out_shape=(
            jax.ShapeDtypeStruct((all_rows, 3 * columns), BF),
            jax.ShapeDtypeStruct((count, rows, width), BF),
            jax.ShapeDtypeStruct((count, rows, width), BF),
            jax.ShapeDtypeStruct((8, columns), F32),
        ),
        grid_spec=pltpu.PrefetchScalarGridSpec(
            num_scalar_prefetch=1,
            grid=(count,),
            in_specs=[
                chip_rows(2 * columns),
                pair,
                pair,
                pl.BlockSpec((2, columns), lambda i, at: (0, 0)),
                chip_rows(HEAD_DIM),
                chip_rows(HEAD_DIM),
                chip_rows(columns),
                chip_rows(columns),
                chip_rows(columns),
                pl.BlockSpec((width, 3 * columns), lambda i, at: (0, 0)),
            ]
            + [pl.BlockSpec(memory_space=pl.ANY)] * len(extra),
            out_specs=[
                chip_rows(3 * columns),
                piece,
                piece,
                pl.BlockSpec((8, columns), lambda i, at: (0, 0)),
            ],
        ),
        input_output_aliases={11: 0} if extra else {},
        compiler_params=pltpu.CompilerParams(vmem_limit_bytes=48 << 20),
        cost_estimate=cost(8 * count),
        name="project_back",
    )(
        jnp.stack(list(sources) + [core]).astype(jnp.int32),
        products,
        squares,
        means,
        gains,
        cosine,
        sine,
        dq,
        dk,
        dv,
        weight,
        *extra,
    )


def norm_back(values, inverse, gain, grad):
    scaled = values * inverse
    weighted = grad * gain
    mean = jnp.mean(scaled * weighted, axis=-1, keepdims=True)
    return inverse * (weighted - scaled * mean), jnp.sum(grad * scaled, axis=0)


def dot_nt(a, b):
    return lax.dot_general(a, b, (((1,), (1,)), ((), ())), preferred_element_type=F32)


def dot_tn(a, b):
    return lax.dot_general(a, b, (((0,), (0,)), ((), ())), preferred_element_type=F32)


def dot_nn(a, b):
    return jnp.dot(a, b, preferred_element_type=F32)


def layout_of(lengths, seq_order, rows):
    length_row, order_row = lengths[0], seq_order[0]
    count = order_row.shape[0]
    chosen = (order_row[:, None] == jnp.arange(count, dtype=jnp.int32)[None, :]).astype(jnp.int32)
    placed = jnp.sum(chosen * length_row[None, :], axis=1)
    ends = jnp.sum(
        jnp.where(jnp.arange(count)[None, :] <= jnp.arange(count)[:, None], placed[None, :], 0),
        axis=1,
    )
    index = jnp.arange(rows, dtype=jnp.int32)
    passed = (index[:, None] >= ends[None, :]).astype(jnp.int32)
    begin = jnp.sum(passed * placed[None, :], axis=1)
    segment = jnp.sum(passed, axis=1)
    inside = (segment[:, None] == jnp.arange(count, dtype=jnp.int32)[None, :]).astype(jnp.int32)
    final = jnp.sum(inside * ends[None, :], axis=1) - 1
    return index, begin, final


def body(
    tokens,
    query_weight,
    key_weight,
    value_weight,
    output_weight,
    router_weight,
    attnorm,
    querynorm,
    keynorm,
    mixnorm,
    gate_weight,
    up_weight,
    down_weight,
    routes,
    lengths,
    seq_order,
    cotangent,
):
    rows, width = tokens.shape
    ranks = lax.axis_size("expert")
    groups = lax.axis_size("group")
    me = lax.axis_index("expert")
    chips, _, core = place_of()
    all_rows = rows * ranks
    capacity = 2 * rows * TOP // ranks
    columns = width // ranks
    shard = query_weight.shape[0]
    experts = router_weight.shape[1]
    block = rows
    blocks = all_rows // block
    heads = columns // HEAD_DIM

    own_gain = attnorm.astype(F32)[:, None]
    stacked = jnp.concatenate(
        [
            (part.astype(F32) * own_gain)
            .astype(BF)
            .reshape(shard, ranks, columns)
            .transpose(1, 0, 2)
            for part in (query_weight, key_weight, value_weight)
        ],
        axis=2,
    )
    tok, tok_other = [tokens, chip_shift(tokens)], [partner_swap(tokens)]
    stacked = rank_exchange(stacked)
    in_weight = lax.all_gather(
        stacked.reshape(ranks * shard, 3 * columns), "group", axis=0, tiled=True
    )

    small = jnp.concatenate(
        [querynorm, keynorm, mixnorm, router_weight.T.reshape(-1)], axis=0
    )
    packed = jnp.zeros((2048,), BF).at[: small.shape[0]].set(small).reshape(16, 128)
    packed_routes = (
        jnp.zeros((1024,), jnp.int32)
        .at[: rows * TOP]
        .set(routes.T.reshape(-1))
        .reshape(8, 128)
    )
    packed, packed_routes, _ = tie(packed, packed_routes, stacked)
    everyone, all_routes = exchange_small(1, world=packed, group=packed_routes)
    everyone = everyone.reshape(groups * ranks, 2048)
    query_gain = everyone[:, :shard].reshape(width).astype(F32)
    key_gain = everyone[:, shard : 2 * shard].reshape(width).astype(F32)
    mix_gain = everyone[:, 2 * shard : 3 * shard].reshape(1, width).astype(F32)
    router = jnp.pad(
        everyone[:, 3 * shard : (3 + experts) * shard]
        .reshape(groups * ranks, experts, shard)
        .transpose(1, 0, 2)
        .reshape(experts, width),
        ((0, 128 - experts), (0, 0)),
    )
    my_gains = jnp.stack(
        [
            lax.dynamic_slice_in_dim(query_gain, me * columns, columns),
            lax.dynamic_slice_in_dim(key_gain, me * columns, columns),
        ]
    )

    index, begin, final = layout_of(lengths, seq_order, all_rows)
    starts = begin.reshape(blocks, 1, block)
    lowest = begin.reshape(blocks, block)[:, 0] // block
    highest = final.reshape(blocks, block)[:, block - 1] // block
    position = (index - begin).astype(F32)
    frequency = 10000.0 ** (-(jnp.arange(HEAD_DIM // 2, dtype=F32) * 2.0 / HEAD_DIM))
    angles = position[:, None] * frequency[None, :]
    cosine, sine = jnp.cos(angles), jnp.sin(angles)
    cosine = jnp.concatenate([cosine, cosine], axis=1)
    sine = jnp.concatenate([-sine, sine], axis=1)

    all_routes = all_routes.reshape(ranks, -1)[:, : rows * TOP].reshape(ranks, TOP, rows)
    named = jnp.any(all_routes == me, axis=1)
    counted = jnp.cumsum(named.astype(jnp.int32), axis=1) - 1
    slot_of = jnp.where(named, counted, -1)
    slots = jnp.arange(capacity, dtype=jnp.int32)
    pick = (slot_of[:, None, :] == slots[None, :, None]).astype(BF)
    pick_t = (slot_of[:, :, None] == slots[None, None, :]).astype(BF)

    tables = (my_gains, mix_gain, router, starts, lowest, highest, cosine, sine, pick, pick_t)
    state, ready = None, 0
    for step in range(1, chips):
        tok, tok_other, state, tables = tie(tok, tok_other, state, tables)
        tok_other.append(partner_swap(tok[step]))
        if step + 1 < chips:
            tok.append(chip_shift(tok[step]))
        while ready <= step:
            state = project_in(
                tok[ready], tok_other[ready], source_chip(ready), core, in_weight, state
            )
            ready += 1
    my_gains, mix_gain, router, starts, lowest, highest, cosine, sine, pick, pick_t = tables
    output_weight_, _ = tie(output_weight, tok)
    full_output = lax.all_gather(output_weight_, ("group", "expert"), axis=0, tiled=True)
    all_tokens, normed, products, values, squares = state
    (squares,) = exchange_small(2, added=squares)
    queries, keys = make_heads(products, squares, my_gains, cosine, sine, width)

    cotangent_, _ = tie(cotangent, squares)
    cot = [cotangent_, chip_shift(cotangent_)]
    attended_mine, lse = attention_forward(queries, keys, values, starts, lowest)
    att = [attended_mine]
    att, cot = tie(att, cot)
    att_other = [partner_swap(att[0])]
    att.append(chip_shift(att[0]))
    att, att_other = tie(att, att_other)
    middle_e, ready = None, 0
    for step in range(1, chips):
        att_other.append(partner_swap(att[step]))
        if step + 1 < chips:
            att.append(chip_shift(att[step]))
            while ready < step or (ready == step and step + 2 == chips):
                middle_e = gather_heads(
                    all_tokens,
                    pick,
                    att[ready],
                    att_other[ready],
                    source_chip(ready),
                    core,
                    full_output,
                    middle_e,
                )
                ready += 1
            att, att_other, middle_e = tie(att, att_other, middle_e)

    cot, middle_e = tie(cot, middle_e)
    cot_other = [partner_swap(cot[0]), partner_swap(cot[1])]
    cot, _ = tie(cot, att)
    cot += [chip_shift(cot[1])] + [chip_shift(cot[0], step) for step in range(3, chips)]
    order = [source_chip(step % chips) for step in range(1, chips + 1)]
    order += [jnp.int32(step % chips) for step in range(1, chips + 1)]
    order += [source_chip(chips - 1), core]
    hot = (jnp.arange(128, dtype=jnp.int32) == me).astype(F32)[None]
    weights = (gate_weight[0], up_weight[0], down_weight[0])
    mixed_e, gates_e, gate_pre, up_pre, hidden, expert_out, out_own, out_away = expert_forward(
        jnp.stack(order),
        middle_e,
        pick,
        pick_t,
        att[-1],
        att_other[-1],
        full_output,
        mix_gain,
        router,
        hot,
        *weights,
    )
    forward = (gates_e, gate_pre, up_pre, hidden, expert_out)

    own_1, away_1, *saved = expert_backward(
        [source_chip(1)],
        core,
        me,
        pick,
        pick_t,
        [(cot[1], cot_other[1])],
        *forward,
        weights,
        None,
    )
    cot, cot_other, own_1, away_1, saved = tie(cot, cot_other, own_1, away_1, saved)
    cot_other += [partner_swap(cot[step]) for step in range(2, chips)]
    dmixed_moving = add2(own_1[0], partner_swap(away_1[0]))
    cot_other, dmixed_moving, own_att_pieces = tie(
        cot_other, dmixed_moving, (att, att_other)
    )
    dmixed_moving = chip_shift(dmixed_moving)
    rest = list(range(2, chips)) + [0]
    own, away, *saved = expert_backward(
        [source_chip(step) for step in rest],
        core,
        me,
        pick,
        pick_t,
        [(cot[step], cot_other[step]) for step in rest],
        *forward,
        weights,
        saved,
    )
    dmixed_moving, own, away, saved, out_away = tie(dmixed_moving, own, away, saved, out_away)
    swapped = [partner_swap(away[i]) for i in range(chips - 1)]
    out_first = partner_swap(out_away[1])
    dmixed_moving = add3(dmixed_moving, own[0], swapped[0])
    dmixed_moving, saved = tie(dmixed_moving, saved)
    dmixed_moving = chip_shift(dmixed_moving)
    dcopy, dgate_pre, dup_pre = saved
    sums = [
        dot_tn(hidden, dcopy).astype(BF),
        dot_tn(mixed_e, dgate_pre).astype(BF),
        dot_tn(mixed_e, dup_pre).astype(BF),
    ]
    dmixed_moving, sums = tie(dmixed_moving, sums)
    down_sum, gate_sum, up_sum = (lax.psum(term, "group") for term in sums)
    for step in range(3, chips):
        dmixed_moving = add3(dmixed_moving, own[step - 2], swapped[step - 2])
        dmixed_moving, att_pieces = tie(dmixed_moving, own_att_pieces)
        dmixed_moving = chip_shift(dmixed_moving)

    own_attended = jnp.zeros((rows, width), BF)
    for step in range(chips):
        at = source_chip(step) * 2
        for pieces, rank in ((att_pieces[0], at + core), (att_pieces[1], at + 1 - core)):
            piece = lax.dynamic_slice_in_dim(pieces[step], me * rows, rows, 0)
            own_attended = lax.dynamic_update_slice(own_attended, piece, (0, rank * columns))
    middle = tokens.astype(F32) + dot_nn(own_attended, full_output)
    middle_inverse = lax.rsqrt(jnp.mean(middle * middle, axis=-1, keepdims=True) + EPS)
    mixed = (middle * middle_inverse * mix_gain).astype(BF)
    logits = dot_nt(mixed, router)
    logits = jnp.where(jnp.arange(128, dtype=jnp.int32)[None] < experts, logits, NEG)
    shifted = jnp.exp(logits - jnp.max(logits, axis=1, keepdims=True))
    share = shifted / jnp.sum(shifted, axis=1, keepdims=True)
    middle_inverse = jnp.broadcast_to(middle_inverse, (rows, 128))
    halves = own_attended.reshape(rows, groups * chips, 2, shard)
    att_mine = lax.dynamic_index_in_dim(halves, core, 2, keepdims=False).reshape(rows, -1)
    att_away = lax.dynamic_index_in_dim(halves, 1 - core, 2, keepdims=False).reshape(rows, -1)
    out_moving = add2(out_own[1], out_first)
    dmixed_moving, middle, middle_inverse, mixed, share, att_mine, att_away, out_moving = tie(
        dmixed_moving, middle, middle_inverse, mixed, share, att_mine, att_away, out_moving
    )
    out_moving = chip_shift(out_moving)
    dlogits, mixnorm_term, dmiddle, dprojected, dattended_own = owner_backward(
        dmixed_moving,
        own[chips - 2],
        swapped[chips - 2],
        share,
        router,
        middle,
        middle_inverse,
        mix_gain,
        cotangent,
        full_output,
    )

    pairs = dattended_own.reshape(chips, 2, rows, columns)
    _, chip, _ = place_of()
    parts = [
        lax.dynamic_index_in_dim(pairs, lax.rem(chip + step, chips), 0, keepdims=False)
        for step in range(chips)
    ]
    parts, dprojected = tie(parts, dprojected)
    parts = parts[:1] + [chip_shift(parts[step], step) for step in range(1, chips)]
    output_mine = dot_tn(att_mine, dprojected).astype(BF)
    output_away = dot_tn(att_away, dprojected).astype(BF)
    parts, output_mine, output_away, out_moving = tie(parts, output_mine, output_away, out_moving)
    kept = [lax.dynamic_index_in_dim(part, core, 0) for part in parts]
    given = [lax.dynamic_index_in_dim(part, 1 - core, 0) for part in parts]
    dattended = exchange_cores(kept, jnp.concatenate(given, axis=0)).reshape(all_rows, columns)
    out_second = partner_swap(out_away[2])
    delta = jnp.stack(
        [
            jnp.sum(
                dattended[:, h * HEAD_DIM : (h + 1) * HEAD_DIM].astype(F32)
                * attended_mine[:, h * HEAD_DIM : (h + 1) * HEAD_DIM].astype(F32),
                axis=1,
            )
            for h in range(heads)
        ]
    ).reshape(heads, blocks, 1, block)
    out_moving = add3(out_moving, out_own[2], out_second)

    out_moving, dattended, delta, output_mine, output_away = tie(
        out_moving, dattended, delta, output_mine, output_away
    )
    out_moving = chip_shift(out_moving)
    out_swapped = [partner_swap(out_away[step]) for step in (3, 0)]
    output_pair = add2(output_mine, partner_swap(output_away))
    dquery, dkey, dvalue, query_part, key_part = attention_backward(
        queries, keys, values, dattended, lse, delta, starts, highest
    )
    out_moving, out_swapped, output_pair, dquery, dkey, dvalue, query_part, key_part = tie(
        out_moving, out_swapped, output_pair, dquery, dkey, dvalue, query_part, key_part
    )
    partials = jnp.stack(
        [jnp.sum(query_part[:, :, 0], axis=0), jnp.sum(key_part[:, :, 0], axis=0)], axis=1
    )
    (means,) = exchange_small(3, added=partials)
    out_moving = add3(out_moving, out_own[3], out_swapped[0])
    out_moving, means = tie(out_moving, means)
    out_moving = chip_shift(out_moving)
    back = (products, squares, my_gains, cosine, sine, dquery, dkey, dvalue)
    dpre, dn_own_1, dn_away_1, gains_1 = project_back(
        [source_chip(1)], core, *back, means, in_weight, None
    )
    dnormed_moving = add2(dn_own_1[0], partner_swap(dn_away_1[0]))
    dnormed_moving, dpre, down_sum, gate_sum, up_sum = tie(
        dnormed_moving, dpre, down_sum, gate_sum, up_sum
    )
    dnormed_moving = chip_shift(dnormed_moving)
    output_pair, _ = tie(output_pair, down_sum)
    output_pair = lax.psum_scatter(
        output_pair, "group", scatter_dimension=0, tiled=True
    ).reshape(chips, shard, width)
    dpre, dn_own, dn_away, gains_2 = project_back(
        [source_chip(step) for step in rest], core, *back, means, in_weight, dpre
    )
    in_term = jnp.concatenate(
        [
            dot_tn(normed, dpre).astype(BF),
            dot_tn(mixed, dlogits).astype(BF)[:, :experts],
            mixnorm_term[0].astype(BF)[:, None],
            jnp.zeros((width, 128 - experts - 1), BF),
        ],
        axis=1,
    )
    dnormed_moving, dn_own, dn_away, in_term, out_moving = tie(
        dnormed_moving, dn_own, dn_away, in_term, out_moving
    )
    in_sum = lax.psum_scatter(in_term, "group", scatter_dimension=0, tiled=True)
    dn_swapped = [partner_swap(dn_away[i]) for i in range(chips - 1)]
    dnormed_moving = add3(dnormed_moving, dn_own[0], dn_swapped[0])
    gain_terms = gains_1 + gains_2
    dnormed_moving, gain_terms, out_moving, down_sum, gate_sum, up_sum = tie(
        dnormed_moving, gain_terms, out_moving, down_sum, gate_sum, up_sum
    )
    dnormed_moving = chip_shift(dnormed_moving)
    layer_result = (
        middle
        + out_moving.astype(F32)
        + out_own[0].astype(F32)
        + out_swapped[1].astype(F32)
    ).astype(BF)
    down_sum, gate_sum, up_sum = (
        term.astype(F32)[None] for term in (down_sum, gate_sum, up_sum)
    )
    (gain_shares,) = exchange_small(4, world=gain_terms)
    dnormed_moving, dn_swapped, down_sum, gate_sum, up_sum, gain_shares, layer_result = tie(
        dnormed_moving, dn_swapped, down_sum, gate_sum, up_sum, gain_shares, layer_result
    )
    dnormed_moving = add3(dnormed_moving, dn_own[1], dn_swapped[1])
    dnormed_moving, output_pair = tie(dnormed_moving, output_pair)
    dnormed_moving = chip_shift(dnormed_moving)

    def to_chip(step):
        part = lax.dynamic_index_in_dim(
            output_pair, source_chip(chips - step), 0, keepdims=False
        )
        return chip_shift(part, step)

    output_parts = [to_chip(step) for step in range(1, chips)]
    kept, given = exchange_chips(in_sum.reshape(ranks, shard, 3 * columns + 128))
    output_sum = sum(
        [part.astype(F32) for part in output_parts],
        lax.dynamic_index_in_dim(output_pair, source_chip(0), 0, keepdims=False).astype(F32),
    )
    kept, given, dnormed_moving, output_sum = tie(kept, given, dnormed_moving, output_sum)
    in_sum = exchange_cores(kept, given)
    dnormed = (
        dnormed_moving.astype(F32)
        + dn_own[chips - 2].astype(F32)
        + dn_swapped[chips - 2].astype(F32)
    )

    norm_grads = jnp.sum(
        gain_shares.reshape(groups, ranks, 8, columns)[:, :, :2], axis=0
    )
    norm_grads = norm_grads.transpose(1, 0, 2).reshape(2, width)
    flat = lax.axis_index("group") * ranks + me
    norm_grads = lax.dynamic_slice_in_dim(norm_grads, flat * shard, shard, 1)
    raw = [
        in_sum[:, :, i * columns : (i + 1) * columns]
        .transpose(1, 0, 2)
        .reshape(shard, width)
        .astype(F32)
        for i in range(3)
    ]
    others = jnp.sum(in_sum[:, :, 3 * columns :].astype(F32), axis=0)
    attnorm_grad = sum(
        jnp.sum(grad * weight.astype(F32), axis=1)
        for grad, weight in zip(raw, (query_weight, key_weight, value_weight))
    )
    query_sum, key_sum, value_sum = (grad * own_gain for grad in raw)
    own_f = tokens.astype(F32)
    own_inverse = lax.rsqrt(jnp.mean(own_f * own_f, axis=-1, keepdims=True) + EPS)
    scaled = own_f * own_inverse
    dinput = own_inverse * (dnormed - scaled * jnp.mean(scaled * dnormed, axis=-1, keepdims=True))
    tokens_grad = (dmiddle + dinput).astype(BF)
    return (
        layer_result,
        tokens_grad,
        query_sum,
        key_sum,
        value_sum,
        output_sum,
        others[:, :experts],
        attnorm_grad,
        norm_grads[0],
        norm_grads[1],
        others[:, experts],
        gate_sum,
        up_sum,
        down_sum,
    )


def solution(mesh):
    rows = P(("group", "expert"), None)
    line = P(("group", "expert"))
    expert = P("expert", None, None)
    group = P("group", None)
    return jax.shard_map(
        body,
        mesh=mesh,
        in_specs=(
            (rows,) * 6 + (line,) * 4 + (expert,) * 3 + (rows, group, group, rows)
        ),
        out_specs=(rows,) * 7 + (line,) * 4 + (expert,) * 3,
        check_vma=False,
    )
```

```python
import functools

import jax
import jax.numpy as jnp
from jax import lax
from jax.experimental import pallas as pl
from jax.experimental.pallas import tpu as pltpu
from jax.sharding import PartitionSpec as P

HEADS = 16
HEAD_DIM = 128
TOP = 2
EPS = 1e-05
NEG = -1e30
MESH = pl.DeviceIdType.MESH
BF = jnp.bfloat16
F32 = jnp.float32


def cost(microseconds):
    return pl.CostEstimate(
        flops=int(microseconds * 1e6), bytes_accessed=1 << 16, transcendentals=0
    )


def row_sums(x):
    ones = jnp.ones((8, x.shape[1]), BF)
    high = x.astype(BF)
    low = (x - high.astype(F32)).astype(BF)
    contract = (((1,), (1,)), ((), ()))
    return (
        lax.dot_general(ones, high, contract, preferred_element_type=F32)
        + lax.dot_general(ones, low, contract, preferred_element_type=F32)
    )[:1]


def exchange_small(collective_id, world=None, group=None, added=None):
    groups, ranks = lax.axis_size("group"), lax.axis_size("expert")
    total = groups * ranks
    near_blocks = [block for block in (group, added) if block is not None]
    count = len(near_blocks)

    def kernel(*refs):
        refs = list(refs)
        world_in = refs.pop(0) if world is not None else None
        near_in = [refs.pop(0) for _ in range(count)]
        world_out = refs.pop(0) if world is not None else None
        near_out = [refs.pop(0) for _ in range(count)]
        rank = lax.axis_index("expert")
        me = lax.axis_index("group") * ranks + rank
        barrier = pltpu.get_barrier_semaphore()

        def far(step):
            flat = lax.rem(me + step, total)
            return (flat // ranks, lax.rem(flat, ranks))

        def near(step):
            return {"expert": lax.rem(rank + step, ranks)}

        if world is not None:

            def greet(step, carry):
                pl.semaphore_signal(barrier, inc=1, device_id=far(step), device_id_type=MESH)
                return carry

            lax.fori_loop(1, total, greet, 0)
            pl.semaphore_wait(barrier, total - 1)
        else:
            for step in range(1, ranks):
                pl.semaphore_signal(barrier, inc=1, device_id=near(step), device_id_type=MESH)
            pl.semaphore_wait(barrier, ranks - 1)
        lands = list(near_out)
        if added is not None:
            lands[-1] = refs.pop(0)
        if count:
            near_send, near_recv = refs.pop(0), refs.pop(0)
        near_copies = []
        for which in range(count):
            for step in range(1, ranks):
                copy = pltpu.make_async_remote_copy(
                    src_ref=near_in[which],
                    dst_ref=lands[which].at[rank],
                    send_sem=near_send.at[which, step],
                    recv_sem=near_recv.at[which, step],
                    device_id=near(step),
                    device_id_type=MESH,
                )
                copy.start()
                near_copies.append(copy)
            lands[which][rank] = near_in[which][...]
        if world is not None:
            far_send, far_recv = refs.pop(0), refs.pop(0)

            def far_copy(step):
                return pltpu.make_async_remote_copy(
                    src_ref=world_in,
                    dst_ref=world_out.at[me],
                    send_sem=far_send.at[step],
                    recv_sem=far_recv.at[step],
                    device_id=far(step),
                    device_id_type=MESH,
                )

            def send(step, carry):
                far_copy(step).start()
                return carry

            lax.fori_loop(1, total, send, 0)
            world_out[me] = world_in[...]

            def settle(step, carry):
                far_copy(step).wait()
                return carry

            lax.fori_loop(1, total, settle, 0)
        for copy in near_copies:
            copy.wait()
        if added is not None:
            summed = lands[-1][0]
            for other in range(1, ranks):
                summed = summed + lands[-1][other]
            near_out[-1][...] = summed

    inputs, outputs, scratch = [], [], []
    if world is not None:
        inputs.append(world)
        outputs.append(jax.ShapeDtypeStruct((total,) + world.shape, world.dtype))
    if group is not None:
        inputs.append(group)
        outputs.append(jax.ShapeDtypeStruct((ranks,) + group.shape, group.dtype))
    if added is not None:
        inputs.append(added)
        outputs.append(jax.ShapeDtypeStruct(added.shape, added.dtype))
        scratch.append(pltpu.VMEM((ranks,) + added.shape, added.dtype))
    if count:
        scratch += [pltpu.SemaphoreType.DMA((count, ranks))] * 2
    if world is not None:
        scratch += [pltpu.SemaphoreType.DMA((total,)), pltpu.SemaphoreType.DMA((total,))]
    vmem = pl.BlockSpec(memory_space=pltpu.VMEM)
    return pl.pallas_call(
        kernel,
        out_shape=tuple(outputs),
        in_specs=[vmem] * len(inputs),
        out_specs=tuple([vmem] * len(outputs)),
        scratch_shapes=scratch,
        compiler_params=pltpu.CompilerParams(collective_id=collective_id, has_side_effects=True),
        name="exchange_small",
    )(*inputs)


def tie(*trees):
    leaves, shape = jax.tree.flatten(trees)
    return jax.tree.unflatten(shape, lax.optimization_barrier(leaves))


def partner_swap(block):
    ranks = lax.axis_size("expert")
    return lax.ppermute(block, "expert", [(i, i ^ 1) for i in range(ranks)])


def chip_shift(block, step=1):
    ranks = lax.axis_size("expert")
    return lax.ppermute(block, "expert", [(i, (i + 2 * step) % ranks) for i in range(ranks)])


def place_of():
    ranks = lax.axis_size("expert")
    me = lax.axis_index("expert")
    return ranks // 2, me // 2, me % 2


def source_chip(step):
    chips, chip, _ = place_of()
    return lax.rem(chip - step + chips, chips)


def assemble(pieces, axis):
    _, _, core = place_of()
    first = pieces[0][0]
    size = first.shape[axis]
    shape = list(first.shape)
    shape[axis] = size * 2 * len(pieces)
    whole = jnp.zeros(shape, first.dtype)
    for step, (mine, other) in enumerate(pieces):
        at = source_chip(step) * 2
        whole = lax.dynamic_update_slice_in_dim(whole, mine, (at + core) * size, axis)
        whole = lax.dynamic_update_slice_in_dim(whole, other, (at + 1 - core) * size, axis)
    return whole


def exchange_chips(blocks):
    chips, chip, core = place_of()
    pairs = blocks.reshape((chips, 2) + blocks.shape[1:])
    keep, give = [], []
    for step in range(chips):
        pair = lax.dynamic_index_in_dim(pairs, lax.rem(chip + step, chips), 0, keepdims=False)
        if step:
            pair = chip_shift(pair, step)
        keep.append(lax.dynamic_index_in_dim(pair, core, 0))
        give.append(lax.dynamic_index_in_dim(pair, 1 - core, 0))
    return keep, jnp.concatenate(give, axis=0)


def exchange_cores(keep, give):
    given = partner_swap(give)
    return assemble([(part, given[i : i + 1]) for i, part in enumerate(keep)], 0)


def rank_exchange(blocks):
    return exchange_cores(*exchange_chips(blocks))


def add_rows(*parts):
    parts = [part if isinstance(part, tuple) else (part[None], 0) for part in parts]
    _, rows, width = parts[0][0].shape
    tile = rows // 2

    def kernel(*refs):
        total = refs[0][0].astype(F32)
        for ref in refs[1:-1]:
            total = total + ref[0].astype(F32)
        refs[-1][...] = total.astype(BF)

    def spec(which):
        return pl.BlockSpec((1, tile, width), lambda i: (which, i, 0))

    return pl.pallas_call(
        kernel,
        out_shape=jax.ShapeDtypeStruct((rows, width), BF),
        grid=(2,),
        in_specs=[spec(which) for _, which in parts],
        out_specs=pl.BlockSpec((tile, width), lambda i: (i, 0)),
        cost_estimate=cost(3),
        name="add_rows",
    )(*[array for array, _ in parts])


def attention_forward(queries, keys, values, starts, lowest):
    rows, columns = queries.shape
    heads = columns // HEAD_DIM
    blocks, _, block = starts.shape
    scale = HEAD_DIM ** (-0.5)

    def kernel(low_ref, start_ref, q_ref, k_ref, v_ref, o_ref, lse_ref):
        i = pl.program_id(0)
        start = start_ref[0]
        q_index = i * block + lax.broadcasted_iota(jnp.int32, (1, block), 1)
        k_local = lax.broadcasted_iota(jnp.int32, (block, block), 0)

        def step(j, carry):
            at = pl.ds(pl.multiple_of(j * block, block), block)
            k_index = k_local + j * block
            allowed = (k_index <= q_index) & (k_index >= start)
            after = []
            for h in range(heads):
                top, total, acc = carry[h]
                lanes = slice(h * HEAD_DIM, (h + 1) * HEAD_DIM)
                s = lax.dot_general(
                    k_ref[at, lanes],
                    q_ref[:, lanes],
                    (((1,), (1,)), ((), ())),
                    preferred_element_type=F32,
                )
                s = jnp.where(allowed, s * scale, NEG)
                new_top = jnp.maximum(top, jnp.max(s, axis=0, keepdims=True))
                p = jnp.exp(s - new_top)
                shrink = jnp.exp(top - new_top)
                total = total * shrink + jnp.sum(p, axis=0, keepdims=True)
                acc = acc * shrink + lax.dot_general(
                    v_ref[at, lanes],
                    p.astype(BF),
                    (((0,), (0,)), ((), ())),
                    preferred_element_type=F32,
                )
                after.append((new_top, total, acc))
            return tuple(after)

        begin = (
            jnp.full((1, block), NEG, F32),
            jnp.zeros((1, block), F32),
            jnp.zeros((HEAD_DIM, block), F32),
        )
        done = lax.fori_loop(low_ref[i], i + 1, step, (begin,) * heads)
        for h, (top, total, acc) in enumerate(done):
            o_ref[:, h * HEAD_DIM : (h + 1) * HEAD_DIM] = (acc / total).T.astype(BF)
            lse_ref[h, 0] = top + jnp.log(total)

    return pl.pallas_call(
        kernel,
        out_shape=(
            jax.ShapeDtypeStruct((rows, columns), BF),
            jax.ShapeDtypeStruct((heads, blocks, 1, block), F32),
        ),
        grid_spec=pltpu.PrefetchScalarGridSpec(
            num_scalar_prefetch=1,
            grid=(blocks,),
            in_specs=[
                pl.BlockSpec((1, 1, block), lambda i, low: (i, 0, 0)),
                pl.BlockSpec((block, columns), lambda i, low: (i, 0)),
                pl.BlockSpec((rows, columns), lambda i, low: (0, 0)),
                pl.BlockSpec((rows, columns), lambda i, low: (0, 0)),
            ],
            out_specs=[
                pl.BlockSpec((block, columns), lambda i, low: (i, 0)),
                pl.BlockSpec((heads, 1, 1, block), lambda i, low: (0, i, 0, 0)),
            ],
        ),
        compiler_params=pltpu.CompilerParams(vmem_limit_bytes=48 << 20),
        cost_estimate=cost(35),
        name="attention_forward",
    )(lowest, starts, queries, keys, values)


def attention_backward(queries, keys, values, outs, douts, lse, starts, highest):
    rows, columns = queries.shape
    heads = columns // HEAD_DIM
    blocks, _, block = starts.shape
    scale = HEAD_DIM ** (-0.5)

    def kernel(
        high_ref,
        start_ref,
        q_ref,
        o_ref,
        do_ref,
        k_ref,
        v_ref,
        lse_ref,
        dq_ref,
        dk_ref,
        dv_ref,
        q_sum_ref,
        k_sum_ref,
        delta_ref,
    ):
        j = pl.program_id(0)

        @pl.when(j == 0)
        def _():
            dq_ref[...] = jnp.zeros_like(dq_ref)
            for h in range(heads):
                lanes = slice(h * HEAD_DIM, (h + 1) * HEAD_DIM)
                for i in range(blocks):
                    at = slice(i * block, (i + 1) * block)
                    delta_ref[h, i] = row_sums(
                        o_ref[at, lanes].astype(F32) * do_ref[at, lanes].astype(F32)
                    )

        k_index = j * block + lax.broadcasted_iota(jnp.int32, (block, block), 0)
        q_local = lax.broadcasted_iota(jnp.int32, (1, block), 1)
        contract = (((1,), (1,)), ((), ()))

        def step(i, carry):
            at = pl.ds(pl.multiple_of(i * block, block), block)
            allowed = (k_index <= q_local + i * block) & (k_index >= start_ref[i])
            after = []
            for h in range(heads):
                dk, dv = carry[h]
                lanes = slice(h * HEAD_DIM, (h + 1) * HEAD_DIM)
                q, do = q_ref[at, lanes], do_ref[at, lanes]
                k, v = k_ref[:, lanes], v_ref[:, lanes]
                s = lax.dot_general(k, q, contract, preferred_element_type=F32) * scale
                p = jnp.exp(jnp.where(allowed, s, NEG) - lse_ref[h, i])
                dv = dv + jnp.dot(p.astype(BF), do, preferred_element_type=F32)
                dp = lax.dot_general(v, do, contract, preferred_element_type=F32)
                ds = (p * (dp - delta_ref[h, i])).astype(BF)
                dk = dk + jnp.dot(ds, q, preferred_element_type=F32)
                dq_ref[at, lanes] += (
                    lax.dot_general(ds, k, (((0,), (0,)), ((), ())), preferred_element_type=F32)
                    * scale
                )
                after.append((dk, dv))
            return tuple(after)

        zero = jnp.zeros((block, HEAD_DIM), F32)
        done = lax.fori_loop(j, high_ref[j] + 1, step, ((zero, zero),) * heads)
        for h, (dk, dv) in enumerate(done):
            lanes = slice(h * HEAD_DIM, (h + 1) * HEAD_DIM)
            dk = dk * scale
            dk_ref[:, lanes] = dk
            dv_ref[:, lanes] = dv.astype(BF)
            k_sum_ref[h, 0] = row_sums(k_ref[:, lanes].astype(F32) * dk)
            at = pl.ds(pl.multiple_of(j * block, block), block)
            q_sum_ref[h, 0] = row_sums(q_ref[at, lanes].astype(F32) * dq_ref[at, lanes])

    whole = pl.BlockSpec((rows, columns), lambda j, high: (0, 0))
    part = pl.BlockSpec((block, columns), lambda j, high: (j, 0))
    line = pl.BlockSpec((heads, blocks, 1, block), lambda j, high: (0, 0, 0, 0))
    bit = pl.BlockSpec((heads, 1, 1, block), lambda j, high: (0, j, 0, 0))
    shape = jax.ShapeDtypeStruct((rows, columns), F32)
    sums = jax.ShapeDtypeStruct((heads, blocks, 1, block), F32)
    return pl.pallas_call(
        kernel,
        out_shape=(shape, shape, jax.ShapeDtypeStruct((rows, columns), BF), sums, sums),
        grid_spec=pltpu.PrefetchScalarGridSpec(
            num_scalar_prefetch=1,
            grid=(blocks,),
            in_specs=[
                pl.BlockSpec((blocks, 1, block), lambda j, high: (0, 0, 0)),
                whole,
                whole,
                whole,
                part,
                part,
                line,
            ],
            out_specs=[whole, part, part, bit, bit],
            scratch_shapes=[pltpu.VMEM((heads, blocks, 1, block), F32)],
        ),
        compiler_params=pltpu.CompilerParams(vmem_limit_bytes=48 << 20),
        cost_estimate=cost(46),
        name="attention_backward",
    )(highest, starts, queries, outs, douts, keys, values, lse)


def gather_heads(tokens, pick, mine, other, source, core, out_weight, whole):
    ranks, capacity, rows = pick.shape
    columns = mine.shape[1]
    width = out_weight.shape[1]
    first = whole is None
    pair = 2 * capacity

    def kernel(at_ref, base_ref, pick_ref, mine_ref, other_ref, w_ref, out_ref, parts):
        core = at_ref[1]
        for half in range(2):
            at = half * capacity
            chosen = pick_ref[half]
            spots = slice(half * rows, (half + 1) * rows)
            if first:
                out_ref[at : at + capacity, :] = jnp.dot(
                    chosen, base_ref[spots, :], preferred_element_type=F32
                )
            for part_ref, which in ((mine_ref, core), (other_ref, 1 - core)):
                parts[
                    at : at + capacity, pl.ds(pl.multiple_of(which * columns, columns), columns)
                ] = jnp.dot(chosen, part_ref[spots, :], preferred_element_type=F32).astype(BF)
        base = out_ref if first else base_ref
        out_ref[...] = base[...] + jnp.dot(
            parts[...], w_ref[...], preferred_element_type=F32
        )

    heads_spec = pl.BlockSpec((2 * rows, columns), lambda r, at: (r, 0))
    total_spec = pl.BlockSpec((pair, width), lambda r, at: (r, 0))
    return pl.pallas_call(
        kernel,
        out_shape=jax.ShapeDtypeStruct((ranks * capacity, width), F32),
        grid_spec=pltpu.PrefetchScalarGridSpec(
            num_scalar_prefetch=1,
            grid=(ranks // 2,),
            in_specs=[
                pl.BlockSpec((2 * rows, width), lambda r, at: (r, 0)) if first else total_spec,
                pl.BlockSpec((2, capacity, rows), lambda r, at: (r, 0, 0)),
                heads_spec,
                heads_spec,
                pl.BlockSpec((2 * columns, width), lambda r, at: (at[0], 0)),
            ],
            out_specs=total_spec,
            scratch_shapes=[pltpu.VMEM((pair, 2 * columns), BF)],
        ),
        input_output_aliases={} if first else {1: 0},
        compiler_params=pltpu.CompilerParams(vmem_limit_bytes=40 << 20),
        cost_estimate=cost(8),
        name="gather_heads",
    )(
        jnp.stack([source, core]).astype(jnp.int32),
        tokens if first else whole,
        pick,
        mine,
        other,
        out_weight,
    )


def expert_forward(
    order, whole, pick, pick_t, mine, other, out_weight, mix_gain, router, hot, gate_w, up_w, down_w
):
    ranks, capacity, rows = pick.shape
    columns = mine.shape[1]
    width = out_weight.shape[1]
    hidden_width = gate_w.shape[1]
    chips = ranks // 2
    pair = 2 * capacity

    def kernel(
        order_ref,
        base_ref,
        pick_ref,
        turned_ref,
        mine_ref,
        other_ref,
        wo_ref,
        gain_ref,
        router_ref,
        hot_ref,
        wg_ref,
        wu_ref,
        wd_ref,
        mixed_ref,
        gates_ref,
        gate_ref,
        up_ref,
        hidden_ref,
        out_ref,
        own_ref,
        away_ref,
        scratch,
        parts,
    ):
        core = order_ref[2 * chips + 1]
        for half in range(2):
            at = half * capacity
            for part_ref, which in ((mine_ref, core), (other_ref, 1 - core)):
                parts[
                    at : at + capacity, pl.ds(pl.multiple_of(which * columns, columns), columns)
                ] = jnp.dot(
                    pick_ref[half],
                    part_ref[half * rows : (half + 1) * rows, :],
                    preferred_element_type=F32,
                ).astype(BF)
        total = base_ref[...] + jnp.dot(parts[...], wo_ref[...], preferred_element_type=F32)
        inverse = lax.rsqrt(jnp.mean(total * total, axis=1, keepdims=True) + EPS)
        mixed = (total * inverse * gain_ref[...]).astype(BF)
        mixed_ref[...] = mixed
        logits = lax.dot_general(
            mixed, router_ref[...], (((1,), (1,)), ((), ())), preferred_element_type=F32
        )
        lane = lax.broadcasted_iota(jnp.int32, logits.shape, 1)
        logits = jnp.where(lane < ranks, logits, NEG)
        shifted = jnp.exp(logits - jnp.max(logits, axis=1, keepdims=True))
        gates = jnp.sum(shifted * hot_ref[...], axis=1, keepdims=True) / jnp.sum(
            shifted, axis=1, keepdims=True
        )
        gates_ref[...] = jnp.broadcast_to(gates, gates_ref.shape)
        gate = jnp.dot(mixed, wg_ref[...], preferred_element_type=F32)
        gate_ref[...] = gate
        up = jnp.dot(mixed, wu_ref[...], preferred_element_type=F32)
        up_ref[...] = up
        hidden = (gate * jax.nn.sigmoid(gate) * up).astype(BF)
        hidden_ref[...] = hidden
        result = jnp.dot(hidden, wd_ref[...], preferred_element_type=F32).astype(BF)
        out_ref[...] = result
        scratch[...] = (gates * result.astype(F32)).astype(BF)
        for half, place_ref in ((core, own_ref), (1 - core, away_ref)):
            at = pl.ds(pl.multiple_of(half * capacity, capacity), capacity)
            place_ref[0] = jnp.dot(
                turned_ref[half], scratch[at, :], preferred_element_type=F32
            ).astype(BF)

    def chip_rows(n, m):
        return pl.BlockSpec((n, m), lambda i, order: (order[i], 0))

    def fixed(n, m):
        return pl.BlockSpec((n, m), lambda i, order: (0, 0), pipeline_mode=pl.Buffered(1))

    def slot(i, order):
        return (order[chips + i], 0, 0)

    all_slots = ranks * capacity
    return pl.pallas_call(
        kernel,
        out_shape=(
            jax.ShapeDtypeStruct((all_slots, width), BF),
            jax.ShapeDtypeStruct((all_slots, 128), F32),
            jax.ShapeDtypeStruct((all_slots, hidden_width), F32),
            jax.ShapeDtypeStruct((all_slots, hidden_width), F32),
            jax.ShapeDtypeStruct((all_slots, hidden_width), BF),
            jax.ShapeDtypeStruct((all_slots, width), BF),
            jax.ShapeDtypeStruct((chips, rows, width), BF),
            jax.ShapeDtypeStruct((chips, rows, width), BF),
        ),
        grid_spec=pltpu.PrefetchScalarGridSpec(
            num_scalar_prefetch=1,
            grid=(chips,),
            in_specs=[
                chip_rows(pair, width),
                pl.BlockSpec((2, capacity, rows), lambda i, order: (order[i], 0, 0)),
                pl.BlockSpec((2, rows, capacity), lambda i, order: (order[i], 0, 0)),
                chip_rows(2 * rows, columns),
                chip_rows(2 * rows, columns),
                pl.BlockSpec(
                    (2 * columns, width),
                    lambda i, order: (order[2 * chips], 0),
                    pipeline_mode=pl.Buffered(1),
                ),
                fixed(1, width),
                fixed(128, width),
                fixed(1, 128),
                fixed(width, hidden_width),
                fixed(width, hidden_width),
                fixed(hidden_width, width),
            ],
            out_specs=[
                chip_rows(pair, width),
                chip_rows(pair, 128),
                chip_rows(pair, hidden_width),
                chip_rows(pair, hidden_width),
                chip_rows(pair, hidden_width),
                chip_rows(pair, width),
                pl.BlockSpec((1, rows, width), slot),
                pl.BlockSpec((1, rows, width), slot),
            ],
            scratch_shapes=[pltpu.VMEM((pair, width), BF), pltpu.VMEM((pair, 2 * columns), BF)],
        ),
        compiler_params=pltpu.CompilerParams(vmem_limit_bytes=58 << 20),
        cost_estimate=cost(45),
        name="expert_forward",
    )(
        order.astype(jnp.int32),
        whole,
        pick,
        pick_t,
        mine,
        other,
        out_weight,
        mix_gain,
        router,
        hot,
        gate_w,
        up_w,
        down_w,
    )


def expert_backward(
    sources, core, rank, pick, pick_t, cotangents, gates, gate, up, hidden, result, weights, whole
):
    ranks, capacity, rows = pick.shape
    count = len(sources)
    width = cotangents[0][0].shape[1]
    hidden_width = weights[0].shape[1]
    pair = 2 * capacity
    wide = width + 128

    def kernel(at_ref, pick_ref, turned_ref, *refs):
        cots = refs[: 2 * count]
        gates_ref, gate_ref, up_ref, out_ref, wg_ref, wu_ref, wd_ref = refs[2 * count : 2 * count + 7]
        own_ref, away_ref, dcopy_ref, dgate_ref, dup_ref, rows_s, back_s, gates_s = refs[-8:]
        core, rank = at_ref[count], at_ref[count + 1]
        step = pl.program_id(0)

        for which in range(count):

            @pl.when(step == which)
            def _(which=which):
                for half, part_ref in ((core, cots[2 * which]), (1 - core, cots[2 * which + 1])):
                    at = pl.ds(pl.multiple_of(half * capacity, capacity), capacity)
                    rows_s[at, :] = jnp.dot(
                        pick_ref[half], part_ref[...], preferred_element_type=F32
                    )

        incoming = rows_s[...]
        dgates = jnp.sum(out_ref[...].astype(F32) * incoming, axis=1, keepdims=True)
        high = dgates.astype(BF)
        low = (dgates - high.astype(F32)).astype(BF)
        lane = lax.broadcasted_iota(jnp.int32, (pair, 128), 1)
        gates_s[...] = jnp.where(
            lane == rank,
            high.astype(F32),
            jnp.where(lane == rank + ranks, low.astype(F32), 0.0),
        ).astype(BF)
        dcopy = (gates_ref[:, :1] * incoming).astype(BF)
        dcopy_ref[...] = dcopy
        dhidden = lax.dot_general(
            dcopy, wd_ref[...], (((1,), (1,)), ((), ())), preferred_element_type=F32
        )
        gate, up = gate_ref[...], up_ref[...]
        sigma = jax.nn.sigmoid(gate)
        scaled = dhidden * sigma
        dgate = (scaled * up * (1.0 + gate * (1.0 - sigma))).astype(BF)
        dup = (scaled * gate).astype(BF)
        dgate_ref[...] = dgate
        dup_ref[...] = dup
        back_s[...] = (
            lax.dot_general(
                dgate, wg_ref[...], (((1,), (1,)), ((), ())), preferred_element_type=F32
            )
            + lax.dot_general(
                dup, wu_ref[...], (((1,), (1,)), ((), ())), preferred_element_type=F32
            )
        ).astype(BF)
        for half, place_ref in ((core, own_ref), (1 - core, away_ref)):
            at = pl.ds(pl.multiple_of(half * capacity, capacity), capacity)
            turned = turned_ref[half]
            place_ref[0, :, :width] = jnp.dot(
                turned, back_s[at, :], preferred_element_type=F32
            ).astype(BF)
            place_ref[0, :, width:] = jnp.dot(
                turned, gates_s[at, :], preferred_element_type=F32
            ).astype(BF)

    def chip_rows(n, m):
        return pl.BlockSpec((n, m), lambda i, at: (at[i], 0))

    def fixed(n, m):
        return pl.BlockSpec((n, m), lambda i, at: (0, 0), pipeline_mode=pl.Buffered(1))

    extra = [] if whole is None else list(whole)
    all_slots = ranks * capacity
    piece = pl.BlockSpec((1, rows, wide), lambda i, at: (i, 0, 0))
    return pl.pallas_call(
        kernel,
        out_shape=(
            jax.ShapeDtypeStruct((count, rows, wide), BF),
            jax.ShapeDtypeStruct((count, rows, wide), BF),
            jax.ShapeDtypeStruct((all_slots, width), BF),
            jax.ShapeDtypeStruct((all_slots, hidden_width), BF),
            jax.ShapeDtypeStruct((all_slots, hidden_width), BF),
        ),
        grid_spec=pltpu.PrefetchScalarGridSpec(
            num_scalar_prefetch=1,
            grid=(count,),
            in_specs=[
                pl.BlockSpec((2, capacity, rows), lambda i, at: (at[i], 0, 0)),
                pl.BlockSpec((2, rows, capacity), lambda i, at: (at[i], 0, 0)),
            ]
            + [fixed(rows, width)] * (2 * count)
            + [
                chip_rows(pair, 128),
                chip_rows(pair, hidden_width),
                chip_rows(pair, hidden_width),
                chip_rows(pair, width),
                fixed(width, hidden_width),
                fixed(width, hidden_width),
                fixed(hidden_width, width),
            ]
            + [pl.BlockSpec(memory_space=pl.ANY)] * len(extra),
            out_specs=[
                piece,
                piece,
                chip_rows(pair, width),
                chip_rows(pair, hidden_width),
                chip_rows(pair, hidden_width),
            ],
            scratch_shapes=[
                pltpu.VMEM((pair, width), F32),
                pltpu.VMEM((pair, width), BF),
                pltpu.VMEM((pair, 128), BF),
            ],
        ),
        input_output_aliases={10 + 2 * count + i: 2 + i for i in range(len(extra))},
        compiler_params=pltpu.CompilerParams(vmem_limit_bytes=60 << 20),
        cost_estimate=cost(12 * count),
        name="expert_backward",
    )(
        jnp.stack(list(sources) + [core, rank]).astype(jnp.int32),
        pick,
        pick_t,
        *[part for parts in cotangents for part in parts],
        gates,
        gate,
        up,
        result,
        *weights,
        *extra,
    )


def owner_backward(
    arrived, mine, swapped, share, router, middle, inverse, mix_gain, cotangent, out_weight
):
    rows, width = middle.shape
    ranks = lax.axis_size("expert")
    columns = width // ranks
    wide = arrived.shape[1]
    tile = rows // 2

    def kernel(
        arrived_ref,
        mine_ref,
        swapped_ref,
        share_ref,
        router_ref,
        middle_ref,
        inverse_ref,
        gain_ref,
        cot_ref,
        w_ref,
        dlogits_ref,
        norm_ref,
        dmiddle_ref,
        dprojected_ref,
        dattended_ref,
    ):
        @pl.when(pl.program_id(0) == 0)
        def _():
            norm_ref[...] = jnp.zeros_like(norm_ref)

        total = (
            arrived_ref[...].astype(F32)
            + mine_ref[0].astype(F32)
            + swapped_ref[...].astype(F32)
        )
        share = share_ref[...]
        dshare = total[:, width:]
        dshare = dshare + pltpu.roll(dshare, 128 - ranks, 1)
        dlogits = (
            share * (dshare - jnp.sum(share * dshare, axis=1, keepdims=True))
        ).astype(BF)
        dlogits_ref[...] = dlogits
        dmixed = total[:, :width] + jnp.dot(
            dlogits, router_ref[...], preferred_element_type=F32
        )
        inverse = inverse_ref[:, :1]
        scaled = middle_ref[...] * inverse
        weighted = dmixed * gain_ref[...]
        norm_ref[:1, :] += jnp.sum(dmixed * scaled, axis=0, keepdims=True)
        mean = jnp.mean(scaled * weighted, axis=1, keepdims=True)
        dmiddle = cot_ref[...].astype(F32) + inverse * (weighted - scaled * mean)
        dmiddle_ref[...] = dmiddle
        dprojected = dmiddle.astype(BF)
        dprojected_ref[...] = dprojected
        dattended = lax.dot_general(
            dprojected, w_ref[...], (((1,), (1,)), ((), ())), preferred_element_type=F32
        ).astype(BF)
        for rank in range(ranks):
            dattended_ref[rank] = dattended[:, rank * columns : (rank + 1) * columns]

    def rows_of(n):
        return pl.BlockSpec((tile, n), lambda i: (i, 0))

    def fixed(n, m):
        return pl.BlockSpec((n, m), lambda i: (0, 0))

    return pl.pallas_call(
        kernel,
        out_shape=(
            jax.ShapeDtypeStruct((rows, 128), BF),
            jax.ShapeDtypeStruct((8, width), F32),
            jax.ShapeDtypeStruct((rows, width), F32),
            jax.ShapeDtypeStruct((rows, width), BF),
            jax.ShapeDtypeStruct((ranks, rows, columns), BF),
        ),
        grid=(rows // tile,),
        in_specs=[
            rows_of(wide),
            pl.BlockSpec((1, tile, wide), lambda i: (mine.shape[0] - 1, i, 0)),
            rows_of(wide),
            rows_of(128),
            fixed(128, width),
            rows_of(width),
            rows_of(128),
            fixed(1, width),
            rows_of(width),
            fixed(width, width),
        ],
        out_specs=(
            rows_of(128),
            fixed(8, width),
            rows_of(width),
            rows_of(width),
            pl.BlockSpec((ranks, tile, columns), lambda i: (0, i, 0)),
        ),
        compiler_params=pltpu.CompilerParams(vmem_limit_bytes=48 << 20),
        cost_estimate=cost(14),
        name="owner_backward",
    )(
        arrived, mine, swapped, share, router, middle, inverse, mix_gain, cotangent, out_weight
    )


def project_in(mine, other, chip, core, weight, whole):
    rows, width = mine.shape
    ranks = lax.axis_size("expert")
    columns = width // ranks

    def kernel(at_ref, mine_ref, other_ref, w_ref, *refs):
        x_out, n_out, p_out, v_out, s_out = refs[-5:]
        core = at_ref[1]

        def handle(x_ref, half):
            at = pl.ds(pl.multiple_of(half * rows, rows), rows)
            x = x_ref[...]
            xf = x.astype(F32)
            n = (xf * lax.rsqrt(jnp.mean(xf * xf, axis=1, keepdims=True) + EPS)).astype(BF)
            x_out[at, :] = x
            n_out[at, :] = n
            product = jnp.dot(n, w_ref[...], preferred_element_type=F32)
            p_out[at, :] = product[:, : 2 * columns]
            v_out[at, :] = product[:, 2 * columns :].astype(BF)
            for which in range(2):
                part = product[:, which * columns : (which + 1) * columns]
                s_out[half, which : which + 1, :] = row_sums(part * part)

        handle(mine_ref, core)
        handle(other_ref, 1 - core)

    shapes = (
        jax.ShapeDtypeStruct((rows * ranks, width), BF),
        jax.ShapeDtypeStruct((rows * ranks, width), BF),
        jax.ShapeDtypeStruct((rows * ranks, 2 * columns), F32),
        jax.ShapeDtypeStruct((rows * ranks, columns), BF),
        jax.ShapeDtypeStruct((ranks, 2, rows), F32),
    )
    out_specs = [
        pl.BlockSpec((2 * rows, shape.shape[1]), lambda i, at: (at[0], 0)) for shape in shapes[:4]
    ] + [pl.BlockSpec((2, 2, rows), lambda i, at: (at[0], 0, 0))]
    extra = [] if whole is None else list(whole)
    full = pl.BlockSpec((rows, width), lambda i, at: (0, 0))
    return pl.pallas_call(
        kernel,
        out_shape=shapes,
        grid_spec=pltpu.PrefetchScalarGridSpec(
            num_scalar_prefetch=1,
            grid=(1,),
            in_specs=[full, full, pl.BlockSpec((width, 3 * columns), lambda i, at: (0, 0))]
            + [pl.BlockSpec(memory_space=pl.ANY)] * len(extra),
            out_specs=out_specs,
        ),
        input_output_aliases={4 + i: i for i in range(len(extra))},
        compiler_params=pltpu.CompilerParams(vmem_limit_bytes=48 << 20),
        cost_estimate=cost(8),
        name="project_in",
    )(jnp.stack([chip, core]).astype(jnp.int32), mine, other, weight, *extra)


def column_of(pair, function):
    pair = function(pair)
    return jnp.concatenate([pair, jnp.zeros((6, pair.shape[1]), F32)], axis=0).T


def make_heads(products, squares, gains, cosine, sine, width):
    rows = products.shape[0]
    columns = products.shape[1] // 2
    tile = squares.shape[2]

    def kernel(p_ref, s_ref, g_ref, c_ref, n_ref, q_ref, k_ref):
        cos, sin = c_ref[...], n_ref[...]
        inverses = column_of(s_ref[0], lambda total: lax.rsqrt(total / width + EPS))
        for which, out in ((0, q_ref), (1, k_ref)):
            inverse = inverses[:, which : which + 1]
            for h in range(0, columns, HEAD_DIM):
                x = p_ref[:, which * columns + h : which * columns + h + HEAD_DIM]
                x = x * inverse * g_ref[which : which + 1, h : h + HEAD_DIM]
                out[:, h : h + HEAD_DIM] = (
                    x * cos + pltpu.roll(x, HEAD_DIM // 2, 1) * sin
                ).astype(BF)

    def rows_of(n):
        return pl.BlockSpec((tile, n), lambda i: (i, 0))

    shape = jax.ShapeDtypeStruct((rows, columns), BF)
    return pl.pallas_call(
        kernel,
        out_shape=(shape, shape),
        grid=(rows // tile,),
        in_specs=[
            rows_of(2 * columns),
            pl.BlockSpec((1, 2, tile), lambda i: (i, 0, 0)),
            pl.BlockSpec((2, columns), lambda i: (0, 0)),
            rows_of(HEAD_DIM),
            rows_of(HEAD_DIM),
        ],
        out_specs=[rows_of(columns)] * 2,
        cost_estimate=cost(8),
        name="make_heads",
    )(products, squares, gains, cosine, sine)


def project_back(
    sources, core, products, squares, gains, cosine, sine, dq, dk, dv, means, weight, whole
):
    all_rows = products.shape[0]
    columns = products.shape[1] // 2
    rows = squares.shape[2]
    width = weight.shape[0]
    count = len(sources)

    def kernel(at_ref, p_ref, s_ref, m_ref, g_ref, c_ref, n_ref, dq_ref, dk_ref, dv_ref, w_ref, *refs):
        out_ref, own_ref, away_ref, gain_ref = refs[-4:]
        core = at_ref[count]

        @pl.when(pl.program_id(0) == 0)
        def _():
            gain_ref[...] = jnp.zeros_like(gain_ref)

        for half, place_ref in ((core, own_ref), (1 - core, away_ref)):
            at = pl.ds(pl.multiple_of(half * rows, rows), rows)
            cos, sin = c_ref[at, :], n_ref[at, :]
            inverses = column_of(s_ref[half], lambda total: lax.rsqrt(total / width + EPS))
            mean = column_of(m_ref[half], lambda total: total / width)
            for which, d_ref in ((0, dq_ref), (1, dk_ref)):
                inverse = inverses[:, which : which + 1]
                for h in range(0, columns, HEAD_DIM):
                    here = which * columns + h
                    scaled = p_ref[at, here : here + HEAD_DIM] * inverse
                    d = d_ref[at, h : h + HEAD_DIM]
                    d = d * cos - pltpu.roll(d, HEAD_DIM // 2, 1) * sin
                    weighted = d * g_ref[which : which + 1, h : h + HEAD_DIM]
                    gain_ref[which : which + 1, h : h + HEAD_DIM] += jnp.sum(
                        d * scaled, axis=0, keepdims=True
                    )
                    out_ref[at, here : here + HEAD_DIM] = (
                        inverse * (weighted - scaled * mean[:, which : which + 1])
                    ).astype(BF)
            out_ref[at, 2 * columns :] = dv_ref[at, :]
            place_ref[0] = lax.dot_general(
                out_ref[at, :], w_ref[...], (((1,), (1,)), ((), ())), preferred_element_type=F32
            ).astype(BF)

    def chip_rows(n):
        return pl.BlockSpec((2 * rows, n), lambda i, at: (at[i], 0))

    pair = pl.BlockSpec((2, 2, rows), lambda i, at: (at[i], 0, 0))
    piece = pl.BlockSpec((1, rows, width), lambda i, at: (i, 0, 0))
    extra = [] if whole is None else [whole]
    return pl.pallas_call(
        kernel,
        out_shape=(
            jax.ShapeDtypeStruct((all_rows, 3 * columns), BF),
            jax.ShapeDtypeStruct((count, rows, width), BF),
            jax.ShapeDtypeStruct((count, rows, width), BF),
            jax.ShapeDtypeStruct((8, columns), F32),
        ),
        grid_spec=pltpu.PrefetchScalarGridSpec(
            num_scalar_prefetch=1,
            grid=(count,),
            in_specs=[
                chip_rows(2 * columns),
                pair,
                pair,
                pl.BlockSpec((2, columns), lambda i, at: (0, 0)),
                chip_rows(HEAD_DIM),
                chip_rows(HEAD_DIM),
                chip_rows(columns),
                chip_rows(columns),
                chip_rows(columns),
                pl.BlockSpec((width, 3 * columns), lambda i, at: (0, 0)),
            ]
            + [pl.BlockSpec(memory_space=pl.ANY)] * len(extra),
            out_specs=[
                chip_rows(3 * columns),
                piece,
                piece,
                pl.BlockSpec((8, columns), lambda i, at: (0, 0)),
            ],
        ),
        input_output_aliases={11: 0} if extra else {},
        compiler_params=pltpu.CompilerParams(vmem_limit_bytes=48 << 20),
        cost_estimate=cost(8 * count),
        name="project_back",
    )(
        jnp.stack(list(sources) + [core]).astype(jnp.int32),
        products,
        squares,
        means,
        gains,
        cosine,
        sine,
        dq,
        dk,
        dv,
        weight,
        *extra,
    )


def norm_back(values, inverse, gain, grad):
    scaled = values * inverse
    weighted = grad * gain
    mean = jnp.mean(scaled * weighted, axis=-1, keepdims=True)
    return inverse * (weighted - scaled * mean), jnp.sum(grad * scaled, axis=0)


def weight_grad(a, b, tile=512):
    rows, m = a.shape
    n = b.shape[1]

    def kernel(a_ref, b_ref, o_ref):
        o_ref[...] = lax.dot_general(
            a_ref[...], b_ref[...], (((0,), (0,)), ((), ())), preferred_element_type=F32
        ).astype(BF)

    return pl.pallas_call(
        kernel,
        out_shape=jax.ShapeDtypeStruct((m, n), BF),
        grid=(m // tile,),
        in_specs=[
            pl.BlockSpec((rows, tile), lambda i: (0, i)),
            pl.BlockSpec((rows, n), lambda i: (0, 0)),
        ],
        out_specs=pl.BlockSpec((tile, n), lambda i: (i, 0)),
        compiler_params=pltpu.CompilerParams(vmem_limit_bytes=48 << 20),
        cost_estimate=cost(10),
        name="weight_grad",
    )(a, b)


def in_weight_grad(normed, dpre, mixed, dlogits, rows8, experts):
    rows, m = normed.shape
    own = mixed.shape[0]
    n = dpre.shape[1]
    tile = 512

    def kernel(a_ref, b_ref, m_ref, l_ref, r_ref, o_ref):
        contract = (((0,), (0,)), ((), ()))
        o_ref[:, :n] = lax.dot_general(
            a_ref[...], b_ref[...], contract, preferred_element_type=F32
        ).astype(BF)
        side = lax.dot_general(m_ref[...], l_ref[...], contract, preferred_element_type=F32)
        turned = r_ref[...].T
        lane = lax.broadcasted_iota(jnp.int32, side.shape, 1)
        for i in range(3):
            side = jnp.where(lane == experts + i, turned[:, i : i + 1], side)
        o_ref[:, n:] = side.astype(BF)

    return pl.pallas_call(
        kernel,
        out_shape=jax.ShapeDtypeStruct((m, n + 128), BF),
        grid=(m // tile,),
        in_specs=[
            pl.BlockSpec((rows, tile), lambda i: (0, i)),
            pl.BlockSpec((rows, n), lambda i: (0, 0)),
            pl.BlockSpec((own, tile), lambda i: (0, i)),
            pl.BlockSpec((own, 128), lambda i: (0, 0)),
            pl.BlockSpec((8, tile), lambda i: (0, i)),
        ],
        out_specs=pl.BlockSpec((tile, n + 128), lambda i: (i, 0)),
        compiler_params=pltpu.CompilerParams(vmem_limit_bytes=48 << 20),
        cost_estimate=cost(14),
        name="in_weight_grad",
    )(normed, dpre, mixed, dlogits, rows8)


def own_forward(places, pieces, tokens, out_weight, mix_gain, router, experts):
    rows, width = tokens.shape
    count = len(pieces)
    columns = width // count

    def kernel(at_ref, *refs):
        token_ref, w_ref, gain_ref, router_ref = refs[count : count + 4]
        att_ref, middle_ref, mixed_ref, share_ref, inverse_ref = refs[count + 4 :]
        for i in range(count):
            att_ref[:, pl.ds(pl.multiple_of(at_ref[i] * columns, columns), columns)] = refs[i][...]
        middle = token_ref[...].astype(F32) + jnp.dot(
            att_ref[...], w_ref[...], preferred_element_type=F32
        )
        middle_ref[...] = middle
        inverse = lax.rsqrt(jnp.mean(middle * middle, axis=1, keepdims=True) + EPS)
        inverse_ref[...] = jnp.broadcast_to(inverse, inverse_ref.shape)
        mixed = (middle * inverse * gain_ref[...]).astype(BF)
        mixed_ref[...] = mixed
        logits = lax.dot_general(
            mixed, router_ref[...], (((1,), (1,)), ((), ())), preferred_element_type=F32
        )
        lane = lax.broadcasted_iota(jnp.int32, logits.shape, 1)
        logits = jnp.where(lane < experts, logits, NEG)
        shifted = jnp.exp(logits - jnp.max(logits, axis=1, keepdims=True))
        share_ref[...] = shifted / jnp.sum(shifted, axis=1, keepdims=True)

    def fixed(n, m):
        return pl.BlockSpec((n, m), lambda i, at: (0, 0))

    return pl.pallas_call(
        kernel,
        out_shape=(
            jax.ShapeDtypeStruct((rows, width), BF),
            jax.ShapeDtypeStruct((rows, width), F32),
            jax.ShapeDtypeStruct((rows, width), BF),
            jax.ShapeDtypeStruct((rows, 128), F32),
            jax.ShapeDtypeStruct((rows, 128), F32),
        ),
        grid_spec=pltpu.PrefetchScalarGridSpec(
            num_scalar_prefetch=1,
            grid=(1,),
            in_specs=[pl.BlockSpec((rows, columns), lambda i, at: (at[count], 0))] * count
            + [fixed(rows, width), fixed(width, width), fixed(1, width), fixed(128, width)],
            out_specs=[
                fixed(rows, width),
                fixed(rows, width),
                fixed(rows, width),
                fixed(rows, 128),
                fixed(rows, 128),
            ],
        ),
        compiler_params=pltpu.CompilerParams(vmem_limit_bytes=48 << 20),
        cost_estimate=cost(10),
        name="own_forward",
    )(places, *pieces, tokens, out_weight, mix_gain, router)


def dot_nt(a, b):
    return lax.dot_general(a, b, (((1,), (1,)), ((), ())), preferred_element_type=F32)


def dot_tn(a, b):
    return lax.dot_general(a, b, (((0,), (0,)), ((), ())), preferred_element_type=F32)


def dot_nn(a, b):
    return jnp.dot(a, b, preferred_element_type=F32)


def layout_of(lengths, seq_order, rows):
    length_row, order_row = lengths[0], seq_order[0]
    count = order_row.shape[0]
    chosen = (order_row[:, None] == jnp.arange(count, dtype=jnp.int32)[None, :]).astype(jnp.int32)
    placed = jnp.sum(chosen * length_row[None, :], axis=1)
    ends = jnp.sum(
        jnp.where(jnp.arange(count)[None, :] <= jnp.arange(count)[:, None], placed[None, :], 0),
        axis=1,
    )
    index = jnp.arange(rows, dtype=jnp.int32)
    passed = (index[:, None] >= ends[None, :]).astype(jnp.int32)
    begin = jnp.sum(passed * placed[None, :], axis=1)
    segment = jnp.sum(passed, axis=1)
    inside = (segment[:, None] == jnp.arange(count, dtype=jnp.int32)[None, :]).astype(jnp.int32)
    final = jnp.sum(inside * ends[None, :], axis=1) - 1
    return index, begin, final


def body(
    tokens,
    query_weight,
    key_weight,
    value_weight,
    output_weight,
    router_weight,
    attnorm,
    querynorm,
    keynorm,
    mixnorm,
    gate_weight,
    up_weight,
    down_weight,
    routes,
    lengths,
    seq_order,
    cotangent,
):
    rows, width = tokens.shape
    ranks = lax.axis_size("expert")
    groups = lax.axis_size("group")
    me = lax.axis_index("expert")
    chips, _, core = place_of()
    all_rows = rows * ranks
    capacity = 2 * rows * TOP // ranks
    columns = width // ranks
    shard = query_weight.shape[0]
    experts = router_weight.shape[1]
    block = rows
    blocks = all_rows // block
    heads = columns // HEAD_DIM

    own_gain = attnorm.astype(F32)[:, None]
    beside = jnp.concatenate(
        [querynorm[:, None], keynorm[:, None], mixnorm[:, None], router_weight], axis=1
    )
    beside = jnp.pad(beside, ((0, 0), (0, 128 - beside.shape[1])))
    stacked = jnp.concatenate(
        [
            (part.astype(F32) * own_gain)
            .astype(BF)
            .reshape(shard, ranks, columns)
            .transpose(1, 0, 2)
            for part in (query_weight, key_weight, value_weight)
        ]
        + [jnp.broadcast_to(beside, (ranks, shard, 128))],
        axis=2,
    )
    kept, given = exchange_chips(stacked)
    tokens_, kept, given = tie(tokens, kept, given)
    tok, tok_other = [tokens, chip_shift(tokens_)], [partner_swap(tokens_)]
    stacked = exchange_cores(kept, given)
    in_weight = lax.all_gather(
        stacked.reshape(ranks * shard, 3 * columns + 128), "group", axis=0, tiled=True
    )

    index, begin, final = layout_of(lengths, seq_order, all_rows)
    starts = begin.reshape(blocks, 1, block)
    lowest = begin.reshape(blocks, block)[:, 0] // block
    highest = final.reshape(blocks, block)[:, block - 1] // block
    position = (index - begin).astype(F32)
    frequency = 10000.0 ** (-(jnp.arange(HEAD_DIM // 2, dtype=F32) * 2.0 / HEAD_DIM))
    angles = position[:, None] * frequency[None, :]
    cosine, sine = jnp.cos(angles), jnp.sin(angles)
    cosine = jnp.concatenate([cosine, cosine], axis=1)
    sine = jnp.concatenate([-sine, sine], axis=1)

    tables = (starts, lowest, highest, cosine, sine)
    state, ready = None, 0
    for step in range(1, chips):
        tok, tok_other, state, tables = tie(tok, tok_other, state, tables)
        tok_other.append(partner_swap(tok[step]))
        if step + 1 < chips:
            tok.append(chip_shift(tok[step]))
        while ready <= step:
            state = project_in(
                tok[ready], tok_other[ready], source_chip(ready), core, in_weight, state
            )
            ready += 1
    starts, lowest, highest, cosine, sine = tables
    output_weight_, _ = tie(output_weight, tok)
    full_output = lax.all_gather(output_weight_, ("group", "expert"), axis=0, tiled=True)
    all_tokens, normed, products, values, squares = state
    packed_routes = (
        jnp.zeros((1024,), jnp.int32)
        .at[: rows * TOP]
        .set(routes.T.reshape(-1))
        .reshape(8, 128)
    )
    all_routes, squares = exchange_small(2, group=packed_routes, added=squares)
    beside = in_weight[:, 3 * columns :]
    my_gains = lax.dynamic_slice_in_dim(beside, me * columns, columns, 0)[:, :2].T.astype(F32)
    mix_gain = beside[:, 2:3].T.astype(F32)
    router = jnp.pad(beside[:, 3 : 3 + experts].T, ((0, 128 - experts), (0, 0)))
    queries, keys = make_heads(products, squares, my_gains, cosine, sine, width)

    all_routes = all_routes.reshape(ranks, -1)[:, : rows * TOP].reshape(ranks, TOP, rows)
    named = jnp.any(all_routes == me, axis=1)
    counted = jnp.cumsum(named.astype(jnp.int32), axis=1) - 1
    slot_of = jnp.where(named, counted, -1)
    slots = jnp.arange(capacity, dtype=jnp.int32)
    pick = (slot_of[:, None, :] == slots[None, :, None]).astype(BF)
    pick_t = (slot_of[:, :, None] == slots[None, None, :]).astype(BF)

    cotangent_, _ = tie(cotangent, squares)
    cot = [cotangent_, chip_shift(cotangent_)]
    attended_mine, lse = attention_forward(queries, keys, values, starts, lowest)
    att = [attended_mine]
    att, cot, pick, pick_t, mix_gain, router = tie(att, cot, pick, pick_t, mix_gain, router)
    att_other = [partner_swap(att[0])]
    att.append(chip_shift(att[0]))
    att, att_other = tie(att, att_other)
    middle_e, ready = None, 0
    for step in range(1, chips):
        att_other.append(partner_swap(att[step]))
        if step + 1 < chips:
            att.append(chip_shift(att[step]))
            while ready < step or (ready == step and step + 2 == chips):
                middle_e = gather_heads(
                    all_tokens,
                    pick,
                    att[ready],
                    att_other[ready],
                    source_chip(ready),
                    core,
                    full_output,
                    middle_e,
                )
                ready += 1
            att, att_other, middle_e = tie(att, att_other, middle_e)

    cot, middle_e = tie(cot, middle_e)
    cot_other = [partner_swap(cot[0]), partner_swap(cot[1])]
    cot, _ = tie(cot, att)
    cot += [chip_shift(cot[1])] + [chip_shift(cot[0], step) for step in range(3, chips)]
    order = [source_chip(step % chips) for step in range(1, chips + 1)]
    order += [jnp.int32(step % chips) for step in range(1, chips + 1)]
    order += [source_chip(chips - 1), core]
    hot = (jnp.arange(128, dtype=jnp.int32) == me).astype(F32)[None]
    weights = (gate_weight[0], up_weight[0], down_weight[0])
    mixed_e, gates_e, gate_pre, up_pre, hidden, expert_out, out_own, out_away = expert_forward(
        jnp.stack(order),
        middle_e,
        pick,
        pick_t,
        att[-1],
        att_other[-1],
        full_output,
        mix_gain,
        router,
        hot,
        *weights,
    )
    forward = (gates_e, gate_pre, up_pre, hidden, expert_out)

    own_1, away_1, *saved = expert_backward(
        [source_chip(1)],
        core,
        me,
        pick,
        pick_t,
        [(cot[1], cot_other[1])],
        *forward,
        weights,
        None,
    )
    cot, cot_other, own_1, away_1, saved = tie(cot, cot_other, own_1, away_1, saved)
    cot_other += [partner_swap(cot[step]) for step in range(2, chips)]
    dmixed_moving = add_rows((own_1, 0), partner_swap(away_1[0]))
    cot_other, dmixed_moving, own_att_pieces = tie(
        cot_other, dmixed_moving, (att, att_other)
    )
    dmixed_moving = chip_shift(dmixed_moving)
    rest = list(range(2, chips)) + [0]
    own, away, *saved = expert_backward(
        [source_chip(step) for step in rest],
        core,
        me,
        pick,
        pick_t,
        [(cot[step], cot_other[step]) for step in rest],
        *forward,
        weights,
        saved,
    )
    dmixed_moving, own, away, saved, out_away = tie(dmixed_moving, own, away, saved, out_away)
    dmixed_moving = add_rows(dmixed_moving, (own, 0), partner_swap(away[0]))
    dmixed_moving, own, away, saved, out_away = tie(dmixed_moving, own, away, saved, out_away)
    dmixed_moving = chip_shift(dmixed_moving)
    swapped = [partner_swap(away[i]) for i in range(1, chips - 1)]
    out_first = partner_swap(out_away[1])
    dcopy, dgate_pre, dup_pre = saved
    sums = [
        weight_grad(hidden, dcopy),
        weight_grad(mixed_e, dgate_pre),
        weight_grad(mixed_e, dup_pre),
    ]
    dmixed_moving, own, swapped, sums = tie(dmixed_moving, own, swapped, sums)
    sums = lax.psum(tuple(sums), "group")
    for step in range(3, chips):
        dmixed_moving = add_rows(dmixed_moving, (own, step - 2), swapped[step - 3])
        dmixed_moving, pieces = tie(dmixed_moving, own_att_pieces)
        dmixed_moving = chip_shift(dmixed_moving)

    places = []
    for step in range(chips):
        places += [source_chip(step) * 2 + core, source_chip(step) * 2 + 1 - core]
    own_attended, middle, mixed, share, middle_inverse = own_forward(
        jnp.stack(places + [me]).astype(jnp.int32),
        [piece for pair in zip(*pieces) for piece in pair],
        tokens,
        full_output,
        mix_gain,
        router,
        experts,
    )
    halves = own_attended.reshape(rows, groups * chips, 2, shard)
    att_mine = lax.dynamic_index_in_dim(halves, core, 2, keepdims=False).reshape(rows, -1)
    att_away = lax.dynamic_index_in_dim(halves, 1 - core, 2, keepdims=False).reshape(rows, -1)
    out_moving = add_rows((out_own, 1), out_first)
    dmixed_moving, middle, middle_inverse, mixed, share, att_mine, att_away, out_moving = tie(
        dmixed_moving, middle, middle_inverse, mixed, share, att_mine, att_away, out_moving
    )
    out_moving = chip_shift(out_moving)
    dlogits, mixnorm_term, dmiddle, dprojected, dattended_own = owner_backward(
        dmixed_moving,
        own,
        swapped[chips - 3],
        share,
        router,
        middle,
        middle_inverse,
        mix_gain,
        cotangent,
        full_output,
    )

    pairs = dattended_own.reshape(chips, 2, rows, columns)
    _, chip, _ = place_of()
    parts = [
        lax.dynamic_index_in_dim(pairs, lax.rem(chip + step, chips), 0, keepdims=False)
        for step in range(chips)
    ]
    parts, dprojected = tie(parts, dprojected)
    parts = parts[:1] + [chip_shift(parts[step], step) for step in range(1, chips)]
    output_mine = weight_grad(att_mine, dprojected)
    output_away = weight_grad(att_away, dprojected)
    parts, output_mine, output_away, out_moving = tie(parts, output_mine, output_away, out_moving)
    kept = [lax.dynamic_index_in_dim(part, core, 0) for part in parts]
    given = [lax.dynamic_index_in_dim(part, 1 - core, 0) for part in parts]
    dattended = exchange_cores(kept, jnp.concatenate(given, axis=0)).reshape(all_rows, columns)
    out_second = partner_swap(out_away[2])
    out_moving = add_rows(out_moving, (out_own, 2), out_second)

    out_moving, dattended, output_mine, output_away = tie(
        out_moving, dattended, output_mine, output_away
    )
    out_moving = chip_shift(out_moving)
    out_swapped = [partner_swap(out_away[step]) for step in (3, 0)]
    output_swapped = partner_swap(output_away)
    dquery, dkey, dvalue, query_part, key_part = attention_backward(
        queries, keys, values, attended_mine, dattended, lse, starts, highest
    )
    out_moving, out_swapped, output_swapped, dquery, dkey, dvalue, query_part, key_part = tie(
        out_moving, out_swapped, output_swapped, dquery, dkey, dvalue, query_part, key_part
    )
    out_moving = add_rows(out_moving, (out_own, 3), out_swapped[0])
    partials = jnp.stack(
        [jnp.sum(query_part[:, :, 0], axis=0), jnp.sum(key_part[:, :, 0], axis=0)], axis=1
    )
    partials, out_moving = tie(partials, out_moving)
    (means,) = exchange_small(3, added=partials)
    out_moving, means, output_mine, output_swapped = tie(
        out_moving, means, output_mine, output_swapped
    )
    out_moving = chip_shift(out_moving)
    back = (products, squares, my_gains, cosine, sine, dquery, dkey, dvalue)
    dpre, dn_own_1, dn_away_1, gains_1 = project_back(
        [source_chip(1)], core, *back, means, in_weight, None
    )
    dnormed_moving = add_rows((dn_own_1, 0), partner_swap(dn_away_1[0]))
    dnormed_moving, dpre = tie(dnormed_moving, dpre)
    dnormed_moving = chip_shift(dnormed_moving)
    dpre, dn_own, dn_away, gains_2 = project_back(
        [source_chip(step) for step in rest], core, *back, means, in_weight, dpre
    )
    gain_terms = gains_1 + gains_2

    def spread(row):
        return lax.dynamic_update_slice(jnp.zeros((1, width), F32), row, (0, me * columns))

    rows8 = jnp.concatenate(
        [
            mixnorm_term[:1],
            spread(gain_terms[:1]),
            spread(gain_terms[1:2]),
            jnp.zeros((5, width), F32),
        ],
        axis=0,
    )
    in_term = in_weight_grad(normed, dpre, mixed, dlogits, rows8, experts)
    dnormed_moving, dn_own, dn_away, in_term, out_moving, sums, output_mine = tie(
        dnormed_moving, dn_own, dn_away, in_term, out_moving, sums, output_mine
    )
    output_sum = lax.psum_scatter(
        add_rows(output_mine, output_swapped), "group", scatter_dimension=0, tiled=True
    )
    dnormed_moving = add_rows(dnormed_moving, (dn_own, 0), partner_swap(dn_away[0]))
    dnormed_moving, dn_own, dn_away, sums, out_moving = tie(
        dnormed_moving, dn_own, dn_away, sums, out_moving
    )
    dnormed_moving = chip_shift(dnormed_moving)
    dn_swapped = [partner_swap(dn_away[i]) for i in range(1, chips - 1)]
    in_sum = lax.psum_scatter(in_term, "group", scatter_dimension=0, tiled=True)
    down_sum, gate_sum = sums[0].astype(F32)[None], sums[1].astype(F32)[None]
    layer_result = (
        middle
        + out_moving.astype(F32)
        + out_own[0].astype(F32)
        + out_swapped[1].astype(F32)
    ).astype(BF)
    dnormed_moving, dn_swapped, down_sum, gate_sum, layer_result = tie(
        dnormed_moving, dn_swapped, down_sum, gate_sum, layer_result
    )
    dnormed_moving = add_rows(dnormed_moving, (dn_own, 1), dn_swapped[0])
    dnormed_moving, up_sum = tie(dnormed_moving, sums[2])
    dnormed_moving = chip_shift(dnormed_moving)
    up_sum = up_sum.astype(F32)[None]
    output_pairs = output_sum.reshape(chips, shard, width)

    def to_chip(array, step):
        return lax.dynamic_index_in_dim(
            array, lax.rem(chip + step, chips), 0, keepdims=False
        )

    output_parts = [to_chip(output_pairs, step) for step in range(chips)]
    output_parts = output_parts[:1] + [chip_shift(output_parts[i], i) for i in range(1, chips)]
    output_parts, dnormed_moving, up_sum, in_sum = tie(
        output_parts, dnormed_moving, up_sum, in_sum
    )
    in_pairs = in_sum.reshape(chips, 2, shard, 3 * columns + 128)
    in_parts = [to_chip(in_pairs, step) for step in range(chips)]
    (in_parts,) = tie(in_parts)
    in_parts = in_parts[:1] + [chip_shift(in_parts[i], i) for i in range(1, chips)]
    output_sum = sum(part.astype(F32) for part in output_parts)
    (in_parts,) = tie(in_parts)
    kept = [lax.dynamic_index_in_dim(part, core, 0) for part in in_parts]
    given = jnp.concatenate(
        [lax.dynamic_index_in_dim(part, 1 - core, 0) for part in in_parts], axis=0
    )
    in_sum = exchange_cores(kept, given)
    dnormed = (
        dnormed_moving.astype(F32)
        + dn_own[chips - 2].astype(F32)
        + dn_swapped[chips - 3].astype(F32)
    )

    raw = [
        in_sum[:, :, i * columns : (i + 1) * columns]
        .transpose(1, 0, 2)
        .reshape(shard, width)
        .astype(F32)
        for i in range(3)
    ]
    others = jnp.sum(in_sum[:, :, 3 * columns :].astype(F32), axis=0)
    attnorm_grad = sum(
        jnp.sum(grad * weight.astype(F32), axis=1)
        for grad, weight in zip(raw, (query_weight, key_weight, value_weight))
    )
    query_sum, key_sum, value_sum = (grad * own_gain for grad in raw)
    own_f = tokens.astype(F32)
    own_inverse = lax.rsqrt(jnp.mean(own_f * own_f, axis=-1, keepdims=True) + EPS)
    scaled = own_f * own_inverse
    dinput = own_inverse * (dnormed - scaled * jnp.mean(scaled * dnormed, axis=-1, keepdims=True))
    tokens_grad = (dmiddle + dinput).astype(BF)
    return (
        layer_result,
        tokens_grad,
        query_sum,
        key_sum,
        value_sum,
        output_sum,
        others[:, :experts],
        attnorm_grad,
        others[:, experts + 1],
        others[:, experts + 2],
        others[:, experts],
        gate_sum,
        up_sum,
        down_sum,
    )


def solution(mesh):
    rows = P(("group", "expert"), None)
    line = P(("group", "expert"))
    expert = P("expert", None, None)
    group = P("group", None)
    return jax.shard_map(
        body,
        mesh=mesh,
        in_specs=(
            (rows,) * 6 + (line,) * 4 + (expert,) * 3 + (rows, group, group, rows)
        ),
        out_specs=(rows,) * 7 + (line,) * 4 + (expert,) * 3,
        check_vma=False,
    )
```

```python
import functools

import jax
import jax.numpy as jnp
from jax import lax
from jax.experimental import pallas as pl
from jax.experimental.pallas import tpu as pltpu
from jax.sharding import PartitionSpec as P

HEADS = 16
HEAD_DIM = 128
TOP = 2
EPS = 1e-05
NEG = -1e30
MESH = pl.DeviceIdType.MESH
BF = jnp.bfloat16
F32 = jnp.float32


def cost(microseconds):
    return pl.CostEstimate(
        flops=int(microseconds * 1e6), bytes_accessed=1 << 16, transcendentals=0
    )


def row_sums(x):
    ones = jnp.ones((8, x.shape[1]), BF)
    high = x.astype(BF)
    low = (x - high.astype(F32)).astype(BF)
    contract = (((1,), (1,)), ((), ()))
    return (
        lax.dot_general(ones, high, contract, preferred_element_type=F32)
        + lax.dot_general(ones, low, contract, preferred_element_type=F32)
    )[:1]


def exchange_small(collective_id, world=None, group=None, added=None):
    groups, ranks = lax.axis_size("group"), lax.axis_size("expert")
    total = groups * ranks
    near_blocks = [block for block in (group, added) if block is not None]
    count = len(near_blocks)

    def kernel(*refs):
        refs = list(refs)
        world_in = refs.pop(0) if world is not None else None
        near_in = [refs.pop(0) for _ in range(count)]
        world_out = refs.pop(0) if world is not None else None
        near_out = [refs.pop(0) for _ in range(count)]
        rank = lax.axis_index("expert")
        me = lax.axis_index("group") * ranks + rank
        barrier = pltpu.get_barrier_semaphore()

        def far(step):
            flat = lax.rem(me + step, total)
            return (flat // ranks, lax.rem(flat, ranks))

        def near(step):
            return {"expert": lax.rem(rank + step, ranks)}

        if world is not None:

            def greet(step, carry):
                pl.semaphore_signal(barrier, inc=1, device_id=far(step), device_id_type=MESH)
                return carry

            lax.fori_loop(1, total, greet, 0)
            pl.semaphore_wait(barrier, total - 1)
        else:
            for step in range(1, ranks):
                pl.semaphore_signal(barrier, inc=1, device_id=near(step), device_id_type=MESH)
            pl.semaphore_wait(barrier, ranks - 1)
        lands = list(near_out)
        if added is not None:
            lands[-1] = refs.pop(0)
        if count:
            near_send, near_recv = refs.pop(0), refs.pop(0)
        near_copies = []
        for which in range(count):
            for step in range(1, ranks):
                copy = pltpu.make_async_remote_copy(
                    src_ref=near_in[which],
                    dst_ref=lands[which].at[rank],
                    send_sem=near_send.at[which, step],
                    recv_sem=near_recv.at[which, step],
                    device_id=near(step),
                    device_id_type=MESH,
                )
                copy.start()
                near_copies.append(copy)
            lands[which][rank] = near_in[which][...]
        if world is not None:
            far_send, far_recv = refs.pop(0), refs.pop(0)

            def far_copy(step):
                return pltpu.make_async_remote_copy(
                    src_ref=world_in,
                    dst_ref=world_out.at[me],
                    send_sem=far_send.at[step],
                    recv_sem=far_recv.at[step],
                    device_id=far(step),
                    device_id_type=MESH,
                )

            def send(step, carry):
                far_copy(step).start()
                return carry

            lax.fori_loop(1, total, send, 0)
            world_out[me] = world_in[...]

            def settle(step, carry):
                far_copy(step).wait()
                return carry

            lax.fori_loop(1, total, settle, 0)
        for copy in near_copies:
            copy.wait()
        if added is not None:
            summed = lands[-1][0]
            for other in range(1, ranks):
                summed = summed + lands[-1][other]
            near_out[-1][...] = summed

    inputs, outputs, scratch = [], [], []
    if world is not None:
        inputs.append(world)
        outputs.append(jax.ShapeDtypeStruct((total,) + world.shape, world.dtype))
    if group is not None:
        inputs.append(group)
        outputs.append(jax.ShapeDtypeStruct((ranks,) + group.shape, group.dtype))
    if added is not None:
        inputs.append(added)
        outputs.append(jax.ShapeDtypeStruct(added.shape, added.dtype))
        scratch.append(pltpu.VMEM((ranks,) + added.shape, added.dtype))
    if count:
        scratch += [pltpu.SemaphoreType.DMA((count, ranks))] * 2
    if world is not None:
        scratch += [pltpu.SemaphoreType.DMA((total,)), pltpu.SemaphoreType.DMA((total,))]
    vmem = pl.BlockSpec(memory_space=pltpu.VMEM)
    return pl.pallas_call(
        kernel,
        out_shape=tuple(outputs),
        in_specs=[vmem] * len(inputs),
        out_specs=tuple([vmem] * len(outputs)),
        scratch_shapes=scratch,
        compiler_params=pltpu.CompilerParams(collective_id=collective_id, has_side_effects=True),
        name="exchange_small",
    )(*inputs)


def tie(*trees):
    leaves, shape = jax.tree.flatten(trees)
    return jax.tree.unflatten(shape, lax.optimization_barrier(leaves))


def partner_swap(block):
    ranks = lax.axis_size("expert")
    return lax.ppermute(block, "expert", [(i, i ^ 1) for i in range(ranks)])


def chip_shift(block, step=1):
    ranks = lax.axis_size("expert")
    return lax.ppermute(block, "expert", [(i, (i + 2 * step) % ranks) for i in range(ranks)])


def place_of():
    ranks = lax.axis_size("expert")
    me = lax.axis_index("expert")
    return ranks // 2, me // 2, me % 2


def source_chip(step):
    chips, chip, _ = place_of()
    return lax.rem(chip - step + chips, chips)


def assemble(pieces, axis):
    _, _, core = place_of()
    first = pieces[0][0]
    size = first.shape[axis]
    shape = list(first.shape)
    shape[axis] = size * 2 * len(pieces)
    whole = jnp.zeros(shape, first.dtype)
    for step, (mine, other) in enumerate(pieces):
        at = source_chip(step) * 2
        whole = lax.dynamic_update_slice_in_dim(whole, mine, (at + core) * size, axis)
        whole = lax.dynamic_update_slice_in_dim(whole, other, (at + 1 - core) * size, axis)
    return whole


def exchange_chips(blocks):
    chips, chip, core = place_of()
    pairs = blocks.reshape((chips, 2) + blocks.shape[1:])
    keep, give = [], []
    for step in range(chips):
        pair = lax.dynamic_index_in_dim(pairs, lax.rem(chip + step, chips), 0, keepdims=False)
        if step:
            pair = chip_shift(pair, step)
        keep.append(lax.dynamic_index_in_dim(pair, core, 0))
        give.append(lax.dynamic_index_in_dim(pair, 1 - core, 0))
    return keep, jnp.concatenate(give, axis=0)


def exchange_cores(keep, give):
    given = partner_swap(give)
    return assemble([(part, given[i : i + 1]) for i, part in enumerate(keep)], 0)


def rank_exchange(blocks):
    return exchange_cores(*exchange_chips(blocks))


def add_rows(*parts):
    parts = [part if isinstance(part, tuple) else (part[None], 0) for part in parts]
    _, rows, width = parts[0][0].shape
    tile = rows // 2

    def kernel(*refs):
        total = refs[0][0].astype(F32)
        for ref in refs[1:-1]:
            total = total + ref[0].astype(F32)
        refs[-1][...] = total.astype(BF)

    def spec(which):
        return pl.BlockSpec((1, tile, width), lambda i: (which, i, 0))

    return pl.pallas_call(
        kernel,
        out_shape=jax.ShapeDtypeStruct((rows, width), BF),
        grid=(2,),
        in_specs=[spec(which) for _, which in parts],
        out_specs=pl.BlockSpec((tile, width), lambda i: (i, 0)),
        cost_estimate=cost(3),
        name="add_rows",
    )(*[array for array, _ in parts])


def attention_forward(queries, keys, values, starts, lowest):
    rows, columns = queries.shape
    heads = columns // HEAD_DIM
    blocks, _, block = starts.shape
    scale = HEAD_DIM ** (-0.5)

    def kernel(low_ref, start_ref, q_ref, k_ref, v_ref, o_ref, lse_ref):
        i = pl.program_id(0)
        start = start_ref[0]
        q_index = i * block + lax.broadcasted_iota(jnp.int32, (1, block), 1)
        k_local = lax.broadcasted_iota(jnp.int32, (block, block), 0)

        def step(j, carry):
            at = pl.ds(pl.multiple_of(j * block, block), block)
            k_index = k_local + j * block
            allowed = (k_index <= q_index) & (k_index >= start)
            after = []
            for h in range(heads):
                top, total, acc = carry[h]
                lanes = slice(h * HEAD_DIM, (h + 1) * HEAD_DIM)
                s = lax.dot_general(
                    k_ref[at, lanes],
                    q_ref[:, lanes],
                    (((1,), (1,)), ((), ())),
                    preferred_element_type=F32,
                )
                s = jnp.where(allowed, s * scale, NEG)
                new_top = jnp.maximum(top, jnp.max(s, axis=0, keepdims=True))
                p = jnp.exp(s - new_top)
                shrink = jnp.exp(top - new_top)
                total = total * shrink + jnp.sum(p, axis=0, keepdims=True)
                acc = acc * shrink + lax.dot_general(
                    v_ref[at, lanes],
                    p.astype(BF),
                    (((0,), (0,)), ((), ())),
                    preferred_element_type=F32,
                )
                after.append((new_top, total, acc))
            return tuple(after)

        begin = (
            jnp.full((1, block), NEG, F32),
            jnp.zeros((1, block), F32),
            jnp.zeros((HEAD_DIM, block), F32),
        )
        done = lax.fori_loop(low_ref[i], i + 1, step, (begin,) * heads)
        for h, (top, total, acc) in enumerate(done):
            o_ref[:, h * HEAD_DIM : (h + 1) * HEAD_DIM] = (acc / total).T.astype(BF)
            lse_ref[h, 0] = top + jnp.log(total)

    return pl.pallas_call(
        kernel,
        out_shape=(
            jax.ShapeDtypeStruct((rows, columns), BF),
            jax.ShapeDtypeStruct((heads, blocks, 1, block), F32),
        ),
        grid_spec=pltpu.PrefetchScalarGridSpec(
            num_scalar_prefetch=1,
            grid=(blocks,),
            in_specs=[
                pl.BlockSpec((1, 1, block), lambda i, low: (i, 0, 0)),
                pl.BlockSpec((block, columns), lambda i, low: (i, 0)),
                pl.BlockSpec((rows, columns), lambda i, low: (0, 0)),
                pl.BlockSpec((rows, columns), lambda i, low: (0, 0)),
            ],
            out_specs=[
                pl.BlockSpec((block, columns), lambda i, low: (i, 0)),
                pl.BlockSpec((heads, 1, 1, block), lambda i, low: (0, i, 0, 0)),
            ],
        ),
        compiler_params=pltpu.CompilerParams(vmem_limit_bytes=48 << 20),
        cost_estimate=cost(35),
        name="attention_forward",
    )(lowest, starts, queries, keys, values)


def attention_backward(queries, keys, values, outs, douts, lse, starts, highest):
    rows, columns = queries.shape
    heads = columns // HEAD_DIM
    blocks, _, block = starts.shape
    scale = HEAD_DIM ** (-0.5)

    def kernel(
        high_ref,
        start_ref,
        q_ref,
        o_ref,
        do_ref,
        k_ref,
        v_ref,
        lse_ref,
        dq_ref,
        dk_ref,
        dv_ref,
        q_sum_ref,
        k_sum_ref,
        delta_ref,
    ):
        j = pl.program_id(0)

        @pl.when(j == 0)
        def _():
            dq_ref[...] = jnp.zeros_like(dq_ref)
            for h in range(heads):
                lanes = slice(h * HEAD_DIM, (h + 1) * HEAD_DIM)
                for i in range(blocks):
                    at = slice(i * block, (i + 1) * block)
                    delta_ref[h, i] = row_sums(
                        o_ref[at, lanes].astype(F32) * do_ref[at, lanes].astype(F32)
                    )

        k_index = j * block + lax.broadcasted_iota(jnp.int32, (block, block), 0)
        q_local = lax.broadcasted_iota(jnp.int32, (1, block), 1)
        contract = (((1,), (1,)), ((), ()))

        def step(i, carry):
            at = pl.ds(pl.multiple_of(i * block, block), block)
            allowed = (k_index <= q_local + i * block) & (k_index >= start_ref[i])
            after = []
            for h in range(heads):
                dk, dv = carry[h]
                lanes = slice(h * HEAD_DIM, (h + 1) * HEAD_DIM)
                q, do = q_ref[at, lanes], do_ref[at, lanes]
                k, v = k_ref[:, lanes], v_ref[:, lanes]
                s = lax.dot_general(k, q, contract, preferred_element_type=F32) * scale
                p = jnp.exp(jnp.where(allowed, s, NEG) - lse_ref[h, i])
                dv = dv + jnp.dot(p.astype(BF), do, preferred_element_type=F32)
                dp = lax.dot_general(v, do, contract, preferred_element_type=F32)
                ds = (p * (dp - delta_ref[h, i])).astype(BF)
                dk = dk + jnp.dot(ds, q, preferred_element_type=F32)
                dq_ref[at, lanes] += (
                    lax.dot_general(ds, k, (((0,), (0,)), ((), ())), preferred_element_type=F32)
                    * scale
                )
                after.append((dk, dv))
            return tuple(after)

        zero = jnp.zeros((block, HEAD_DIM), F32)
        done = lax.fori_loop(j, high_ref[j] + 1, step, ((zero, zero),) * heads)
        for h, (dk, dv) in enumerate(done):
            lanes = slice(h * HEAD_DIM, (h + 1) * HEAD_DIM)
            dk = dk * scale
            dk_ref[:, lanes] = dk
            dv_ref[:, lanes] = dv.astype(BF)
            k_sum_ref[h, 0] = row_sums(k_ref[:, lanes].astype(F32) * dk)
            at = pl.ds(pl.multiple_of(j * block, block), block)
            q_sum_ref[h, 0] = row_sums(q_ref[at, lanes].astype(F32) * dq_ref[at, lanes])

    whole = pl.BlockSpec((rows, columns), lambda j, high: (0, 0))
    part = pl.BlockSpec((block, columns), lambda j, high: (j, 0))
    line = pl.BlockSpec((heads, blocks, 1, block), lambda j, high: (0, 0, 0, 0))
    bit = pl.BlockSpec((heads, 1, 1, block), lambda j, high: (0, j, 0, 0))
    shape = jax.ShapeDtypeStruct((rows, columns), F32)
    sums = jax.ShapeDtypeStruct((heads, blocks, 1, block), F32)
    return pl.pallas_call(
        kernel,
        out_shape=(shape, shape, jax.ShapeDtypeStruct((rows, columns), BF), sums, sums),
        grid_spec=pltpu.PrefetchScalarGridSpec(
            num_scalar_prefetch=1,
            grid=(blocks,),
            in_specs=[
                pl.BlockSpec((blocks, 1, block), lambda j, high: (0, 0, 0)),
                whole,
                whole,
                whole,
                part,
                part,
                line,
            ],
            out_specs=[whole, part, part, bit, bit],
            scratch_shapes=[pltpu.VMEM((heads, blocks, 1, block), F32)],
        ),
        compiler_params=pltpu.CompilerParams(vmem_limit_bytes=48 << 20),
        cost_estimate=cost(46),
        name="attention_backward",
    )(highest, starts, queries, outs, douts, keys, values, lse)


def gather_heads(tokens, pick, mine, other, source, core, out_weight, whole):
    ranks, capacity, rows = pick.shape
    columns = mine.shape[1]
    width = out_weight.shape[1]
    first = whole is None
    pair = 2 * capacity

    def kernel(at_ref, base_ref, pick_ref, mine_ref, other_ref, w_ref, out_ref, parts):
        core = at_ref[1]
        for half in range(2):
            at = half * capacity
            chosen = pick_ref[half]
            spots = slice(half * rows, (half + 1) * rows)
            if first:
                out_ref[at : at + capacity, :] = jnp.dot(
                    chosen, base_ref[spots, :], preferred_element_type=F32
                )
            for part_ref, which in ((mine_ref, core), (other_ref, 1 - core)):
                parts[
                    at : at + capacity, pl.ds(pl.multiple_of(which * columns, columns), columns)
                ] = jnp.dot(chosen, part_ref[spots, :], preferred_element_type=F32).astype(BF)
        base = out_ref if first else base_ref
        out_ref[...] = base[...] + jnp.dot(
            parts[...], w_ref[...], preferred_element_type=F32
        )

    heads_spec = pl.BlockSpec((2 * rows, columns), lambda r, at: (r, 0))
    total_spec = pl.BlockSpec((pair, width), lambda r, at: (r, 0))
    return pl.pallas_call(
        kernel,
        out_shape=jax.ShapeDtypeStruct((ranks * capacity, width), F32),
        grid_spec=pltpu.PrefetchScalarGridSpec(
            num_scalar_prefetch=1,
            grid=(ranks // 2,),
            in_specs=[
                pl.BlockSpec((2 * rows, width), lambda r, at: (r, 0)) if first else total_spec,
                pl.BlockSpec((2, capacity, rows), lambda r, at: (r, 0, 0)),
                heads_spec,
                heads_spec,
                pl.BlockSpec((2 * columns, width), lambda r, at: (at[0], 0)),
            ],
            out_specs=total_spec,
            scratch_shapes=[pltpu.VMEM((pair, 2 * columns), BF)],
        ),
        input_output_aliases={} if first else {1: 0},
        compiler_params=pltpu.CompilerParams(vmem_limit_bytes=40 << 20),
        cost_estimate=cost(8),
        name="gather_heads",
    )(
        jnp.stack([source, core]).astype(jnp.int32),
        tokens if first else whole,
        pick,
        mine,
        other,
        out_weight,
    )


def expert_forward(
    order, whole, pick, pick_t, mine, other, out_weight, mix_gain, router, hot, gate_w, up_w, down_w
):
    ranks, capacity, rows = pick.shape
    columns = mine.shape[1]
    width = out_weight.shape[1]
    hidden_width = gate_w.shape[1]
    chips = ranks // 2
    pair = 2 * capacity

    def kernel(
        order_ref,
        base_ref,
        pick_ref,
        turned_ref,
        mine_ref,
        other_ref,
        wo_ref,
        gain_ref,
        router_ref,
        hot_ref,
        wg_ref,
        wu_ref,
        wd_ref,
        mixed_ref,
        gates_ref,
        gate_ref,
        up_ref,
        hidden_ref,
        out_ref,
        own_ref,
        away_ref,
        scratch,
        parts,
    ):
        core = order_ref[2 * chips + 1]
        for half in range(2):
            at = half * capacity
            for part_ref, which in ((mine_ref, core), (other_ref, 1 - core)):
                parts[
                    at : at + capacity, pl.ds(pl.multiple_of(which * columns, columns), columns)
                ] = jnp.dot(
                    pick_ref[half],
                    part_ref[half * rows : (half + 1) * rows, :],
                    preferred_element_type=F32,
                ).astype(BF)
        total = base_ref[...] + jnp.dot(parts[...], wo_ref[...], preferred_element_type=F32)
        inverse = lax.rsqrt(jnp.mean(total * total, axis=1, keepdims=True) + EPS)
        mixed = (total * inverse * gain_ref[...]).astype(BF)
        mixed_ref[...] = mixed
        logits = lax.dot_general(
            mixed, router_ref[...], (((1,), (1,)), ((), ())), preferred_element_type=F32
        )
        lane = lax.broadcasted_iota(jnp.int32, logits.shape, 1)
        logits = jnp.where(lane < ranks, logits, NEG)
        shifted = jnp.exp(logits - jnp.max(logits, axis=1, keepdims=True))
        gates = jnp.sum(shifted * hot_ref[...], axis=1, keepdims=True) / jnp.sum(
            shifted, axis=1, keepdims=True
        )
        gates_ref[...] = jnp.broadcast_to(gates, gates_ref.shape)
        gate = jnp.dot(mixed, wg_ref[...], preferred_element_type=F32)
        gate_ref[...] = gate
        up = jnp.dot(mixed, wu_ref[...], preferred_element_type=F32)
        up_ref[...] = up
        hidden = (gate * jax.nn.sigmoid(gate) * up).astype(BF)
        hidden_ref[...] = hidden
        result = jnp.dot(hidden, wd_ref[...], preferred_element_type=F32).astype(BF)
        out_ref[...] = result
        scratch[...] = (gates * result.astype(F32)).astype(BF)
        for half, place_ref in ((core, own_ref), (1 - core, away_ref)):
            at = pl.ds(pl.multiple_of(half * capacity, capacity), capacity)
            place_ref[0] = jnp.dot(
                turned_ref[half], scratch[at, :], preferred_element_type=F32
            ).astype(BF)

    def chip_rows(n, m):
        return pl.BlockSpec((n, m), lambda i, order: (order[i], 0))

    def fixed(n, m):
        return pl.BlockSpec((n, m), lambda i, order: (0, 0), pipeline_mode=pl.Buffered(1))

    def slot(i, order):
        return (order[chips + i], 0, 0)

    all_slots = ranks * capacity
    return pl.pallas_call(
        kernel,
        out_shape=(
            jax.ShapeDtypeStruct((all_slots, width), BF),
            jax.ShapeDtypeStruct((all_slots, 128), F32),
            jax.ShapeDtypeStruct((all_slots, hidden_width), F32),
            jax.ShapeDtypeStruct((all_slots, hidden_width), F32),
            jax.ShapeDtypeStruct((all_slots, hidden_width), BF),
            jax.ShapeDtypeStruct((all_slots, width), BF),
            jax.ShapeDtypeStruct((chips, rows, width), BF),
            jax.ShapeDtypeStruct((chips, rows, width), BF),
        ),
        grid_spec=pltpu.PrefetchScalarGridSpec(
            num_scalar_prefetch=1,
            grid=(chips,),
            in_specs=[
                chip_rows(pair, width),
                pl.BlockSpec((2, capacity, rows), lambda i, order: (order[i], 0, 0)),
                pl.BlockSpec((2, rows, capacity), lambda i, order: (order[i], 0, 0)),
                chip_rows(2 * rows, columns),
                chip_rows(2 * rows, columns),
                pl.BlockSpec(
                    (2 * columns, width),
                    lambda i, order: (order[2 * chips], 0),
                    pipeline_mode=pl.Buffered(1),
                ),
                fixed(1, width),
                fixed(128, width),
                fixed(1, 128),
                fixed(width, hidden_width),
                fixed(width, hidden_width),
                fixed(hidden_width, width),
            ],
            out_specs=[
                chip_rows(pair, width),
                chip_rows(pair, 128),
                chip_rows(pair, hidden_width),
                chip_rows(pair, hidden_width),
                chip_rows(pair, hidden_width),
                chip_rows(pair, width),
                pl.BlockSpec((1, rows, width), slot),
                pl.BlockSpec((1, rows, width), slot),
            ],
            scratch_shapes=[pltpu.VMEM((pair, width), BF), pltpu.VMEM((pair, 2 * columns), BF)],
        ),
        compiler_params=pltpu.CompilerParams(vmem_limit_bytes=58 << 20),
        cost_estimate=cost(45),
        name="expert_forward",
    )(
        order.astype(jnp.int32),
        whole,
        pick,
        pick_t,
        mine,
        other,
        out_weight,
        mix_gain,
        router,
        hot,
        gate_w,
        up_w,
        down_w,
    )


def expert_backward(
    sources, core, rank, pick, pick_t, cotangents, gates, gate, up, hidden, result, weights, whole
):
    ranks, capacity, rows = pick.shape
    count = len(sources)
    width = cotangents[0][0].shape[1]
    hidden_width = weights[0].shape[1]
    pair = 2 * capacity
    wide = width + 128

    def kernel(at_ref, pick_ref, turned_ref, *refs):
        cots = refs[: 2 * count]
        gates_ref, gate_ref, up_ref, out_ref, wg_ref, wu_ref, wd_ref = refs[2 * count : 2 * count + 7]
        own_ref, away_ref, dcopy_ref, dgate_ref, dup_ref, rows_s, back_s, gates_s = refs[-8:]
        core, rank = at_ref[count], at_ref[count + 1]
        step = pl.program_id(0)

        for which in range(count):

            @pl.when(step == which)
            def _(which=which):
                for half, part_ref in ((core, cots[2 * which]), (1 - core, cots[2 * which + 1])):
                    at = pl.ds(pl.multiple_of(half * capacity, capacity), capacity)
                    rows_s[at, :] = jnp.dot(
                        pick_ref[half], part_ref[...], preferred_element_type=F32
                    )

        incoming = rows_s[...]
        dgates = jnp.sum(out_ref[...].astype(F32) * incoming, axis=1, keepdims=True)
        high = dgates.astype(BF)
        low = (dgates - high.astype(F32)).astype(BF)
        lane = lax.broadcasted_iota(jnp.int32, (pair, 128), 1)
        gates_s[...] = jnp.where(
            lane == rank,
            high.astype(F32),
            jnp.where(lane == rank + ranks, low.astype(F32), 0.0),
        ).astype(BF)
        dcopy = (gates_ref[:, :1] * incoming).astype(BF)
        dcopy_ref[...] = dcopy
        dhidden = lax.dot_general(
            dcopy, wd_ref[...], (((1,), (1,)), ((), ())), preferred_element_type=F32
        )
        gate, up = gate_ref[...], up_ref[...]
        sigma = jax.nn.sigmoid(gate)
        scaled = dhidden * sigma
        dgate = (scaled * up * (1.0 + gate * (1.0 - sigma))).astype(BF)
        dup = (scaled * gate).astype(BF)
        dgate_ref[...] = dgate
        dup_ref[...] = dup
        back_s[...] = (
            lax.dot_general(
                dgate, wg_ref[...], (((1,), (1,)), ((), ())), preferred_element_type=F32
            )
            + lax.dot_general(
                dup, wu_ref[...], (((1,), (1,)), ((), ())), preferred_element_type=F32
            )
        ).astype(BF)
        for half, place_ref in ((core, own_ref), (1 - core, away_ref)):
            at = pl.ds(pl.multiple_of(half * capacity, capacity), capacity)
            turned = turned_ref[half]
            place_ref[0, :, :width] = jnp.dot(
                turned, back_s[at, :], preferred_element_type=F32
            ).astype(BF)
            place_ref[0, :, width:] = jnp.dot(
                turned, gates_s[at, :], preferred_element_type=F32
            ).astype(BF)

    def chip_rows(n, m):
        return pl.BlockSpec((n, m), lambda i, at: (at[i], 0))

    def fixed(n, m):
        return pl.BlockSpec((n, m), lambda i, at: (0, 0), pipeline_mode=pl.Buffered(1))

    extra = [] if whole is None else list(whole)
    all_slots = ranks * capacity
    piece = pl.BlockSpec((1, rows, wide), lambda i, at: (i, 0, 0))
    return pl.pallas_call(
        kernel,
        out_shape=(
            jax.ShapeDtypeStruct((count, rows, wide), BF),
            jax.ShapeDtypeStruct((count, rows, wide), BF),
            jax.ShapeDtypeStruct((all_slots, width), BF),
            jax.ShapeDtypeStruct((all_slots, hidden_width), BF),
            jax.ShapeDtypeStruct((all_slots, hidden_width), BF),
        ),
        grid_spec=pltpu.PrefetchScalarGridSpec(
            num_scalar_prefetch=1,
            grid=(count,),
            in_specs=[
                pl.BlockSpec((2, capacity, rows), lambda i, at: (at[i], 0, 0)),
                pl.BlockSpec((2, rows, capacity), lambda i, at: (at[i], 0, 0)),
            ]
            + [fixed(rows, width)] * (2 * count)
            + [
                chip_rows(pair, 128),
                chip_rows(pair, hidden_width),
                chip_rows(pair, hidden_width),
                chip_rows(pair, width),
                fixed(width, hidden_width),
                fixed(width, hidden_width),
                fixed(hidden_width, width),
            ]
            + [pl.BlockSpec(memory_space=pl.ANY)] * len(extra),
            out_specs=[
                piece,
                piece,
                chip_rows(pair, width),
                chip_rows(pair, hidden_width),
                chip_rows(pair, hidden_width),
            ],
            scratch_shapes=[
                pltpu.VMEM((pair, width), F32),
                pltpu.VMEM((pair, width), BF),
                pltpu.VMEM((pair, 128), BF),
            ],
        ),
        input_output_aliases={10 + 2 * count + i: 2 + i for i in range(len(extra))},
        compiler_params=pltpu.CompilerParams(vmem_limit_bytes=60 << 20),
        cost_estimate=cost(12 * count),
        name="expert_backward",
    )(
        jnp.stack(list(sources) + [core, rank]).astype(jnp.int32),
        pick,
        pick_t,
        *[part for parts in cotangents for part in parts],
        gates,
        gate,
        up,
        result,
        *weights,
        *extra,
    )


def owner_backward(
    arrived, mine, swapped, share, router, middle, inverse, mix_gain, cotangent, out_weight
):
    rows, width = middle.shape
    ranks = lax.axis_size("expert")
    columns = width // ranks
    wide = arrived.shape[1]
    tile = rows // 2

    def kernel(
        arrived_ref,
        mine_ref,
        swapped_ref,
        share_ref,
        router_ref,
        middle_ref,
        inverse_ref,
        gain_ref,
        cot_ref,
        w_ref,
        dlogits_ref,
        norm_ref,
        dmiddle_ref,
        dprojected_ref,
        dattended_ref,
    ):
        @pl.when(pl.program_id(0) == 0)
        def _():
            norm_ref[...] = jnp.zeros_like(norm_ref)

        total = (
            arrived_ref[...].astype(F32)
            + mine_ref[0].astype(F32)
            + swapped_ref[...].astype(F32)
        )
        share = share_ref[...]
        dshare = total[:, width:]
        dshare = dshare + pltpu.roll(dshare, 128 - ranks, 1)
        dlogits = (
            share * (dshare - jnp.sum(share * dshare, axis=1, keepdims=True))
        ).astype(BF)
        dlogits_ref[...] = dlogits
        dmixed = total[:, :width] + jnp.dot(
            dlogits, router_ref[...], preferred_element_type=F32
        )
        inverse = inverse_ref[:, :1]
        scaled = middle_ref[...] * inverse
        weighted = dmixed * gain_ref[...]
        norm_ref[:1, :] += jnp.sum(dmixed * scaled, axis=0, keepdims=True)
        mean = jnp.mean(scaled * weighted, axis=1, keepdims=True)
        dmiddle = cot_ref[...].astype(F32) + inverse * (weighted - scaled * mean)
        dmiddle_ref[...] = dmiddle
        dprojected = dmiddle.astype(BF)
        dprojected_ref[...] = dprojected
        dattended = lax.dot_general(
            dprojected, w_ref[...], (((1,), (1,)), ((), ())), preferred_element_type=F32
        ).astype(BF)
        for rank in range(ranks):
            dattended_ref[rank] = dattended[:, rank * columns : (rank + 1) * columns]

    def rows_of(n):
        return pl.BlockSpec((tile, n), lambda i: (i, 0))

    def fixed(n, m):
        return pl.BlockSpec((n, m), lambda i: (0, 0))

    return pl.pallas_call(
        kernel,
        out_shape=(
            jax.ShapeDtypeStruct((rows, 128), BF),
            jax.ShapeDtypeStruct((8, width), F32),
            jax.ShapeDtypeStruct((rows, width), F32),
            jax.ShapeDtypeStruct((rows, width), BF),
            jax.ShapeDtypeStruct((ranks, rows, columns), BF),
        ),
        grid=(rows // tile,),
        in_specs=[
            rows_of(wide),
            pl.BlockSpec((1, tile, wide), lambda i: (mine.shape[0] - 1, i, 0)),
            rows_of(wide),
            rows_of(128),
            fixed(128, width),
            rows_of(width),
            rows_of(128),
            fixed(1, width),
            rows_of(width),
            fixed(width, width),
        ],
        out_specs=(
            rows_of(128),
            fixed(8, width),
            rows_of(width),
            rows_of(width),
            pl.BlockSpec((ranks, tile, columns), lambda i: (0, i, 0)),
        ),
        compiler_params=pltpu.CompilerParams(vmem_limit_bytes=48 << 20),
        cost_estimate=cost(14),
        name="owner_backward",
    )(
        arrived, mine, swapped, share, router, middle, inverse, mix_gain, cotangent, out_weight
    )


def project_in(mine, other, chip, core, weight, whole):
    rows, width = mine.shape
    ranks = lax.axis_size("expert")
    columns = width // ranks

    def kernel(at_ref, mine_ref, other_ref, w_ref, *refs):
        x_out, n_out, p_out, v_out, s_out = refs[-5:]
        core = at_ref[1]

        def handle(x_ref, half):
            at = pl.ds(pl.multiple_of(half * rows, rows), rows)
            x = x_ref[...]
            xf = x.astype(F32)
            n = (xf * lax.rsqrt(jnp.mean(xf * xf, axis=1, keepdims=True) + EPS)).astype(BF)
            x_out[at, :] = x
            n_out[at, :] = n
            product = jnp.dot(n, w_ref[...], preferred_element_type=F32)
            p_out[at, :] = product[:, : 2 * columns]
            v_out[at, :] = product[:, 2 * columns :].astype(BF)
            for which in range(2):
                part = product[:, which * columns : (which + 1) * columns]
                s_out[half, which : which + 1, :] = row_sums(part * part)

        handle(mine_ref, core)
        handle(other_ref, 1 - core)

    shapes = (
        jax.ShapeDtypeStruct((rows * ranks, width), BF),
        jax.ShapeDtypeStruct((rows * ranks, width), BF),
        jax.ShapeDtypeStruct((rows * ranks, 2 * columns), F32),
        jax.ShapeDtypeStruct((rows * ranks, columns), BF),
        jax.ShapeDtypeStruct((ranks, 2, rows), F32),
    )
    out_specs = [
        pl.BlockSpec((2 * rows, shape.shape[1]), lambda i, at: (at[0], 0)) for shape in shapes[:4]
    ] + [pl.BlockSpec((2, 2, rows), lambda i, at: (at[0], 0, 0))]
    extra = [] if whole is None else list(whole)
    full = pl.BlockSpec((rows, width), lambda i, at: (0, 0))
    return pl.pallas_call(
        kernel,
        out_shape=shapes,
        grid_spec=pltpu.PrefetchScalarGridSpec(
            num_scalar_prefetch=1,
            grid=(1,),
            in_specs=[full, full, pl.BlockSpec((width, 3 * columns), lambda i, at: (0, 0))]
            + [pl.BlockSpec(memory_space=pl.ANY)] * len(extra),
            out_specs=out_specs,
        ),
        input_output_aliases={4 + i: i for i in range(len(extra))},
        compiler_params=pltpu.CompilerParams(vmem_limit_bytes=48 << 20),
        cost_estimate=cost(8),
        name="project_in",
    )(jnp.stack([chip, core]).astype(jnp.int32), mine, other, weight, *extra)


def column_of(pair, function):
    pair = function(pair)
    return jnp.concatenate([pair, jnp.zeros((6, pair.shape[1]), F32)], axis=0).T


def make_heads(products, squares, gains, cosine, sine, width):
    rows = products.shape[0]
    columns = products.shape[1] // 2
    tile = squares.shape[2]

    def kernel(p_ref, s_ref, g_ref, c_ref, n_ref, q_ref, k_ref):
        cos, sin = c_ref[...], n_ref[...]
        inverses = column_of(s_ref[0], lambda total: lax.rsqrt(total / width + EPS))
        for which, out in ((0, q_ref), (1, k_ref)):
            inverse = inverses[:, which : which + 1]
            for h in range(0, columns, HEAD_DIM):
                x = p_ref[:, which * columns + h : which * columns + h + HEAD_DIM]
                x = x * inverse * g_ref[which : which + 1, h : h + HEAD_DIM]
                out[:, h : h + HEAD_DIM] = (
                    x * cos + pltpu.roll(x, HEAD_DIM // 2, 1) * sin
                ).astype(BF)

    def rows_of(n):
        return pl.BlockSpec((tile, n), lambda i: (i, 0))

    shape = jax.ShapeDtypeStruct((rows, columns), BF)
    return pl.pallas_call(
        kernel,
        out_shape=(shape, shape),
        grid=(rows // tile,),
        in_specs=[
            rows_of(2 * columns),
            pl.BlockSpec((1, 2, tile), lambda i: (i, 0, 0)),
            pl.BlockSpec((2, columns), lambda i: (0, 0)),
            rows_of(HEAD_DIM),
            rows_of(HEAD_DIM),
        ],
        out_specs=[rows_of(columns)] * 2,
        cost_estimate=cost(8),
        name="make_heads",
    )(products, squares, gains, cosine, sine)


def project_back(
    sources, core, products, squares, gains, cosine, sine, dq, dk, dv, means, weight, whole
):
    all_rows = products.shape[0]
    columns = products.shape[1] // 2
    rows = squares.shape[2]
    width = weight.shape[0]
    count = len(sources)

    def kernel(at_ref, p_ref, s_ref, m_ref, g_ref, c_ref, n_ref, dq_ref, dk_ref, dv_ref, w_ref, *refs):
        out_ref, own_ref, away_ref, gain_ref = refs[-4:]
        core = at_ref[count]

        @pl.when(pl.program_id(0) == 0)
        def _():
            gain_ref[...] = jnp.zeros_like(gain_ref)

        for half, place_ref in ((core, own_ref), (1 - core, away_ref)):
            at = pl.ds(pl.multiple_of(half * rows, rows), rows)
            cos, sin = c_ref[at, :], n_ref[at, :]
            inverses = column_of(s_ref[half], lambda total: lax.rsqrt(total / width + EPS))
            mean = column_of(m_ref[half], lambda total: total / width)
            for which, d_ref in ((0, dq_ref), (1, dk_ref)):
                inverse = inverses[:, which : which + 1]
                for h in range(0, columns, HEAD_DIM):
                    here = which * columns + h
                    scaled = p_ref[at, here : here + HEAD_DIM] * inverse
                    d = d_ref[at, h : h + HEAD_DIM]
                    d = d * cos - pltpu.roll(d, HEAD_DIM // 2, 1) * sin
                    weighted = d * g_ref[which : which + 1, h : h + HEAD_DIM]
                    gain_ref[which : which + 1, h : h + HEAD_DIM] += jnp.sum(
                        d * scaled, axis=0, keepdims=True
                    )
                    out_ref[at, here : here + HEAD_DIM] = (
                        inverse * (weighted - scaled * mean[:, which : which + 1])
                    ).astype(BF)
            out_ref[at, 2 * columns :] = dv_ref[at, :]
            place_ref[0] = lax.dot_general(
                out_ref[at, :], w_ref[...], (((1,), (1,)), ((), ())), preferred_element_type=F32
            ).astype(BF)

    def chip_rows(n):
        return pl.BlockSpec((2 * rows, n), lambda i, at: (at[i], 0))

    pair = pl.BlockSpec((2, 2, rows), lambda i, at: (at[i], 0, 0))
    piece = pl.BlockSpec((1, rows, width), lambda i, at: (i, 0, 0))
    extra = [] if whole is None else [whole]
    return pl.pallas_call(
        kernel,
        out_shape=(
            jax.ShapeDtypeStruct((all_rows, 3 * columns), BF),
            jax.ShapeDtypeStruct((count, rows, width), BF),
            jax.ShapeDtypeStruct((count, rows, width), BF),
            jax.ShapeDtypeStruct((8, columns), F32),
        ),
        grid_spec=pltpu.PrefetchScalarGridSpec(
            num_scalar_prefetch=1,
            grid=(count,),
            in_specs=[
                chip_rows(2 * columns),
                pair,
                pair,
                pl.BlockSpec((2, columns), lambda i, at: (0, 0)),
                chip_rows(HEAD_DIM),
                chip_rows(HEAD_DIM),
                chip_rows(columns),
                chip_rows(columns),
                chip_rows(columns),
                pl.BlockSpec((width, 3 * columns), lambda i, at: (0, 0)),
            ]
            + [pl.BlockSpec(memory_space=pl.ANY)] * len(extra),
            out_specs=[
                chip_rows(3 * columns),
                piece,
                piece,
                pl.BlockSpec((8, columns), lambda i, at: (0, 0)),
            ],
        ),
        input_output_aliases={11: 0} if extra else {},
        compiler_params=pltpu.CompilerParams(vmem_limit_bytes=48 << 20),
        cost_estimate=cost(8 * count),
        name="project_back",
    )(
        jnp.stack(list(sources) + [core]).astype(jnp.int32),
        products,
        squares,
        means,
        gains,
        cosine,
        sine,
        dq,
        dk,
        dv,
        weight,
        *extra,
    )


def norm_back(values, inverse, gain, grad):
    scaled = values * inverse
    weighted = grad * gain
    mean = jnp.mean(scaled * weighted, axis=-1, keepdims=True)
    return inverse * (weighted - scaled * mean), jnp.sum(grad * scaled, axis=0)


def weight_grad(a, b, tile=512):
    rows, m = a.shape
    n = b.shape[1]

    def kernel(a_ref, b_ref, o_ref):
        o_ref[...] = lax.dot_general(
            a_ref[...], b_ref[...], (((0,), (0,)), ((), ())), preferred_element_type=F32
        ).astype(BF)

    return pl.pallas_call(
        kernel,
        out_shape=jax.ShapeDtypeStruct((m, n), BF),
        grid=(m // tile,),
        in_specs=[
            pl.BlockSpec((rows, tile), lambda i: (0, i)),
            pl.BlockSpec((rows, n), lambda i: (0, 0)),
        ],
        out_specs=pl.BlockSpec((tile, n), lambda i: (i, 0)),
        compiler_params=pltpu.CompilerParams(vmem_limit_bytes=48 << 20),
        cost_estimate=cost(10),
        name="weight_grad",
    )(a, b)


def in_weight_grad(normed, dpre, mixed, dlogits, rows8, experts):
    rows, m = normed.shape
    own = mixed.shape[0]
    n = dpre.shape[1]
    tile = 512

    def kernel(a_ref, b_ref, m_ref, l_ref, r_ref, o_ref):
        contract = (((0,), (0,)), ((), ()))
        o_ref[:, :n] = lax.dot_general(
            a_ref[...], b_ref[...], contract, preferred_element_type=F32
        ).astype(BF)
        side = lax.dot_general(m_ref[...], l_ref[...], contract, preferred_element_type=F32)
        turned = r_ref[...].T
        lane = lax.broadcasted_iota(jnp.int32, side.shape, 1)
        for i in range(3):
            side = jnp.where(lane == experts + i, turned[:, i : i + 1], side)
        o_ref[:, n:] = side.astype(BF)

    return pl.pallas_call(
        kernel,
        out_shape=jax.ShapeDtypeStruct((m, n + 128), BF),
        grid=(m // tile,),
        in_specs=[
            pl.BlockSpec((rows, tile), lambda i: (0, i)),
            pl.BlockSpec((rows, n), lambda i: (0, 0)),
            pl.BlockSpec((own, tile), lambda i: (0, i)),
            pl.BlockSpec((own, 128), lambda i: (0, 0)),
            pl.BlockSpec((8, tile), lambda i: (0, i)),
        ],
        out_specs=pl.BlockSpec((tile, n + 128), lambda i: (i, 0)),
        compiler_params=pltpu.CompilerParams(vmem_limit_bytes=48 << 20),
        cost_estimate=cost(14),
        name="in_weight_grad",
    )(normed, dpre, mixed, dlogits, rows8)


def own_forward(places, pieces, tokens, out_weight, mix_gain, router, experts):
    rows, width = tokens.shape
    count = len(pieces)
    columns = width // count

    def kernel(at_ref, *refs):
        token_ref, w_ref, gain_ref, router_ref = refs[count : count + 4]
        att_ref, middle_ref, mixed_ref, share_ref, inverse_ref = refs[count + 4 :]
        for i in range(count):
            att_ref[:, pl.ds(pl.multiple_of(at_ref[i] * columns, columns), columns)] = refs[i][...]
        middle = token_ref[...].astype(F32) + jnp.dot(
            att_ref[...], w_ref[...], preferred_element_type=F32
        )
        middle_ref[...] = middle
        inverse = lax.rsqrt(jnp.mean(middle * middle, axis=1, keepdims=True) + EPS)
        inverse_ref[...] = jnp.broadcast_to(inverse, inverse_ref.shape)
        mixed = (middle * inverse * gain_ref[...]).astype(BF)
        mixed_ref[...] = mixed
        logits = lax.dot_general(
            mixed, router_ref[...], (((1,), (1,)), ((), ())), preferred_element_type=F32
        )
        lane = lax.broadcasted_iota(jnp.int32, logits.shape, 1)
        logits = jnp.where(lane < experts, logits, NEG)
        shifted = jnp.exp(logits - jnp.max(logits, axis=1, keepdims=True))
        share_ref[...] = shifted / jnp.sum(shifted, axis=1, keepdims=True)

    def fixed(n, m):
        return pl.BlockSpec((n, m), lambda i, at: (0, 0))

    return pl.pallas_call(
        kernel,
        out_shape=(
            jax.ShapeDtypeStruct((rows, width), BF),
            jax.ShapeDtypeStruct((rows, width), F32),
            jax.ShapeDtypeStruct((rows, width), BF),
            jax.ShapeDtypeStruct((rows, 128), F32),
            jax.ShapeDtypeStruct((rows, 128), F32),
        ),
        grid_spec=pltpu.PrefetchScalarGridSpec(
            num_scalar_prefetch=1,
            grid=(1,),
            in_specs=[pl.BlockSpec((rows, columns), lambda i, at: (at[count], 0))] * count
            + [fixed(rows, width), fixed(width, width), fixed(1, width), fixed(128, width)],
            out_specs=[
                fixed(rows, width),
                fixed(rows, width),
                fixed(rows, width),
                fixed(rows, 128),
                fixed(rows, 128),
            ],
        ),
        compiler_params=pltpu.CompilerParams(vmem_limit_bytes=48 << 20),
        cost_estimate=cost(10),
        name="own_forward",
    )(places, *pieces, tokens, out_weight, mix_gain, router)


def dot_nt(a, b):
    return lax.dot_general(a, b, (((1,), (1,)), ((), ())), preferred_element_type=F32)


def dot_tn(a, b):
    return lax.dot_general(a, b, (((0,), (0,)), ((), ())), preferred_element_type=F32)


def dot_nn(a, b):
    return jnp.dot(a, b, preferred_element_type=F32)


def layout_of(lengths, seq_order, rows):
    length_row, order_row = lengths[0], seq_order[0]
    count = order_row.shape[0]
    chosen = (order_row[:, None] == jnp.arange(count, dtype=jnp.int32)[None, :]).astype(jnp.int32)
    placed = jnp.sum(chosen * length_row[None, :], axis=1)
    ends = jnp.sum(
        jnp.where(jnp.arange(count)[None, :] <= jnp.arange(count)[:, None], placed[None, :], 0),
        axis=1,
    )
    index = jnp.arange(rows, dtype=jnp.int32)
    passed = (index[:, None] >= ends[None, :]).astype(jnp.int32)
    begin = jnp.sum(passed * placed[None, :], axis=1)
    segment = jnp.sum(passed, axis=1)
    inside = (segment[:, None] == jnp.arange(count, dtype=jnp.int32)[None, :]).astype(jnp.int32)
    final = jnp.sum(inside * ends[None, :], axis=1) - 1
    return index, begin, final


def body(
    tokens,
    query_weight,
    key_weight,
    value_weight,
    output_weight,
    router_weight,
    attnorm,
    querynorm,
    keynorm,
    mixnorm,
    gate_weight,
    up_weight,
    down_weight,
    routes,
    lengths,
    seq_order,
    cotangent,
):
    rows, width = tokens.shape
    ranks = lax.axis_size("expert")
    groups = lax.axis_size("group")
    me = lax.axis_index("expert")
    chips, _, core = place_of()
    all_rows = rows * ranks
    capacity = 2 * rows * TOP // ranks
    columns = width // ranks
    shard = query_weight.shape[0]
    experts = router_weight.shape[1]
    block = 512 if all_rows % 512 == 0 else rows
    blocks = all_rows // block
    heads = columns // HEAD_DIM

    own_gain = attnorm.astype(F32)[:, None]
    beside = jnp.concatenate(
        [querynorm[:, None], keynorm[:, None], mixnorm[:, None], router_weight], axis=1
    )
    beside = jnp.pad(beside, ((0, 0), (0, 128 - beside.shape[1])))
    stacked = jnp.concatenate(
        [
            (part.astype(F32) * own_gain)
            .astype(BF)
            .reshape(shard, ranks, columns)
            .transpose(1, 0, 2)
            for part in (query_weight, key_weight, value_weight)
        ]
        + [jnp.broadcast_to(beside, (ranks, shard, 128))],
        axis=2,
    )
    kept, given = exchange_chips(stacked)
    tokens_, kept, given = tie(tokens, kept, given)
    tok, tok_other = [tokens, chip_shift(tokens_)], [partner_swap(tokens_)]
    stacked = exchange_cores(kept, given)
    in_weight = lax.all_gather(
        stacked.reshape(ranks * shard, 3 * columns + 128), "group", axis=0, tiled=True
    )

    index, begin, final = layout_of(lengths, seq_order, all_rows)
    starts = begin.reshape(blocks, 1, block)
    lowest = begin.reshape(blocks, block)[:, 0] // block
    highest = final.reshape(blocks, block)[:, block - 1] // block
    position = (index - begin).astype(F32)
    frequency = 10000.0 ** (-(jnp.arange(HEAD_DIM // 2, dtype=F32) * 2.0 / HEAD_DIM))
    angles = position[:, None] * frequency[None, :]
    cosine, sine = jnp.cos(angles), jnp.sin(angles)
    cosine = jnp.concatenate([cosine, cosine], axis=1)
    sine = jnp.concatenate([-sine, sine], axis=1)

    tables = (starts, lowest, highest, cosine, sine)
    state, ready = None, 0
    for step in range(1, chips):
        tok, tok_other, state, tables = tie(tok, tok_other, state, tables)
        tok_other.append(partner_swap(tok[step]))
        if step + 1 < chips:
            tok.append(chip_shift(tok[step]))
        while ready <= step:
            state = project_in(
                tok[ready], tok_other[ready], source_chip(ready), core, in_weight, state
            )
            ready += 1
    starts, lowest, highest, cosine, sine = tables
    output_weight_, _ = tie(output_weight, tok)
    full_output = lax.all_gather(output_weight_, ("group", "expert"), axis=0, tiled=True)
    all_tokens, normed, products, values, squares = state
    packed_routes = (
        jnp.zeros((1024,), jnp.int32)
        .at[: rows * TOP]
        .set(routes.T.reshape(-1))
        .reshape(8, 128)
    )
    beside = in_weight[:, 3 * columns :]
    my_gains = lax.dynamic_slice_in_dim(beside, me * columns, columns, 0)[:, :2].T.astype(F32)
    mix_gain = beside[:, 2:3].T.astype(F32)
    router = jnp.pad(beside[:, 3 : 3 + experts].T, ((0, 128 - experts), (0, 0)))
    squares, packed_routes, my_gains, mix_gain, router = tie(
        squares, packed_routes, my_gains, mix_gain, router
    )
    all_routes, squares = exchange_small(2, group=packed_routes, added=squares)
    queries, keys = make_heads(products, squares, my_gains, cosine, sine, width)

    all_routes = all_routes.reshape(ranks, -1)[:, : rows * TOP].reshape(ranks, TOP, rows)
    named = jnp.any(all_routes == me, axis=1)
    counted = jnp.cumsum(named.astype(jnp.int32), axis=1) - 1
    slot_of = jnp.where(named, counted, -1)
    slots = jnp.arange(capacity, dtype=jnp.int32)
    pick = (slot_of[:, None, :] == slots[None, :, None]).astype(BF)
    pick_t = (slot_of[:, :, None] == slots[None, None, :]).astype(BF)

    cotangent_, _ = tie(cotangent, squares)
    cot = [cotangent_, chip_shift(cotangent_)]
    attended_mine, lse = attention_forward(queries, keys, values, starts, lowest)
    att = [attended_mine]
    att, cot, pick, pick_t, mix_gain, router = tie(att, cot, pick, pick_t, mix_gain, router)
    att_other = [partner_swap(att[0])]
    att.append(chip_shift(att[0]))
    att, att_other = tie(att, att_other)
    middle_e, ready = None, 0
    for step in range(1, chips):
        att_other.append(partner_swap(att[step]))
        if step + 1 < chips:
            att.append(chip_shift(att[step]))
            while ready < step or (ready == step and step + 2 == chips):
                middle_e = gather_heads(
                    all_tokens,
                    pick,
                    att[ready],
                    att_other[ready],
                    source_chip(ready),
                    core,
                    full_output,
                    middle_e,
                )
                ready += 1
            att, att_other, middle_e = tie(att, att_other, middle_e)

    cot, middle_e = tie(cot, middle_e)
    cot_other = [partner_swap(cot[0]), partner_swap(cot[1])]
    cot, _ = tie(cot, att)
    cot += [chip_shift(cot[1])] + [chip_shift(cot[0], step) for step in range(3, chips)]
    order = [source_chip(step % chips) for step in range(1, chips + 1)]
    order += [jnp.int32(step % chips) for step in range(1, chips + 1)]
    order += [source_chip(chips - 1), core]
    hot = (jnp.arange(128, dtype=jnp.int32) == me).astype(F32)[None]
    weights = (gate_weight[0], up_weight[0], down_weight[0])
    mixed_e, gates_e, gate_pre, up_pre, hidden, expert_out, out_own, out_away = expert_forward(
        jnp.stack(order),
        middle_e,
        pick,
        pick_t,
        att[-1],
        att_other[-1],
        full_output,
        mix_gain,
        router,
        hot,
        *weights,
    )
    forward = (gates_e, gate_pre, up_pre, hidden, expert_out)

    own_1, away_1, *saved = expert_backward(
        [source_chip(1)],
        core,
        me,
        pick,
        pick_t,
        [(cot[1], cot_other[1])],
        *forward,
        weights,
        None,
    )
    cot, cot_other, own_1, away_1, saved = tie(cot, cot_other, own_1, away_1, saved)
    cot_other += [partner_swap(cot[step]) for step in range(2, chips)]
    dmixed_moving = add_rows((own_1, 0), partner_swap(away_1[0]))
    cot_other, dmixed_moving, own_att_pieces = tie(
        cot_other, dmixed_moving, (att, att_other)
    )
    dmixed_moving = chip_shift(dmixed_moving)
    rest = list(range(2, chips)) + [0]
    own, away, *saved = expert_backward(
        [source_chip(step) for step in rest],
        core,
        me,
        pick,
        pick_t,
        [(cot[step], cot_other[step]) for step in rest],
        *forward,
        weights,
        saved,
    )
    dmixed_moving, own, away, saved, out_away = tie(dmixed_moving, own, away, saved, out_away)
    dmixed_moving = add_rows(dmixed_moving, (own, 0), partner_swap(away[0]))
    dmixed_moving, own, away, saved, out_away = tie(dmixed_moving, own, away, saved, out_away)
    dmixed_moving = chip_shift(dmixed_moving)
    swapped = [partner_swap(away[i]) for i in range(1, chips - 1)]
    out_first = partner_swap(out_away[1])
    dcopy, dgate_pre, dup_pre = saved
    sums = [
        weight_grad(hidden, dcopy),
        weight_grad(mixed_e, dgate_pre),
        weight_grad(mixed_e, dup_pre),
    ]
    dmixed_moving, own, swapped, sums = tie(dmixed_moving, own, swapped, sums)
    sums = lax.psum(tuple(sums), "group")
    for step in range(3, chips):
        dmixed_moving = add_rows(dmixed_moving, (own, step - 2), swapped[step - 3])
        dmixed_moving, pieces = tie(dmixed_moving, own_att_pieces)
        dmixed_moving = chip_shift(dmixed_moving)

    places = []
    for step in range(chips):
        places += [source_chip(step) * 2 + core, source_chip(step) * 2 + 1 - core]
    own_attended, middle, mixed, share, middle_inverse = own_forward(
        jnp.stack(places + [me]).astype(jnp.int32),
        [piece for pair in zip(*pieces) for piece in pair],
        tokens,
        full_output,
        mix_gain,
        router,
        experts,
    )
    halves = own_attended.reshape(rows, groups * chips, 2, shard)
    att_mine = lax.dynamic_index_in_dim(halves, core, 2, keepdims=False).reshape(rows, -1)
    att_away = lax.dynamic_index_in_dim(halves, 1 - core, 2, keepdims=False).reshape(rows, -1)
    out_moving = add_rows((out_own, 1), out_first)
    dmixed_moving, middle, middle_inverse, mixed, share, att_mine, att_away, out_moving = tie(
        dmixed_moving, middle, middle_inverse, mixed, share, att_mine, att_away, out_moving
    )
    out_moving = chip_shift(out_moving)
    dlogits, mixnorm_term, dmiddle, dprojected, dattended_own = owner_backward(
        dmixed_moving,
        own,
        swapped[chips - 3],
        share,
        router,
        middle,
        middle_inverse,
        mix_gain,
        cotangent,
        full_output,
    )

    pairs = dattended_own.reshape(chips, 2, rows, columns)
    _, chip, _ = place_of()
    parts = [
        lax.dynamic_index_in_dim(pairs, lax.rem(chip + step, chips), 0, keepdims=False)
        for step in range(chips)
    ]
    parts, dprojected = tie(parts, dprojected)
    parts = parts[:1] + [chip_shift(parts[step], step) for step in range(1, chips)]
    output_mine = weight_grad(att_mine, dprojected)
    output_away = weight_grad(att_away, dprojected)
    parts, output_mine, output_away, out_moving = tie(parts, output_mine, output_away, out_moving)
    kept = [lax.dynamic_index_in_dim(part, core, 0) for part in parts]
    given = [lax.dynamic_index_in_dim(part, 1 - core, 0) for part in parts]
    dattended = exchange_cores(kept, jnp.concatenate(given, axis=0)).reshape(all_rows, columns)
    out_second = partner_swap(out_away[2])
    out_moving = add_rows(out_moving, (out_own, 2), out_second)

    out_moving, dattended, output_mine, output_away = tie(
        out_moving, dattended, output_mine, output_away
    )
    out_moving = chip_shift(out_moving)
    out_swapped = [partner_swap(out_away[step]) for step in (3, 0)]
    output_swapped = partner_swap(output_away)
    dquery, dkey, dvalue, query_part, key_part = attention_backward(
        queries, keys, values, attended_mine, dattended, lse, starts, highest
    )
    out_moving, out_swapped, output_swapped, dquery, dkey, dvalue, query_part, key_part = tie(
        out_moving, out_swapped, output_swapped, dquery, dkey, dvalue, query_part, key_part
    )
    out_moving = add_rows(out_moving, (out_own, 3), out_swapped[0])
    partials = jnp.stack(
        [jnp.sum(part, axis=0).reshape(ranks, rows) for part in (query_part, key_part)], axis=1
    )
    partials, out_moving = tie(partials, out_moving)
    (means,) = exchange_small(3, added=partials)
    out_moving, means, output_mine, output_swapped = tie(
        out_moving, means, output_mine, output_swapped
    )
    out_moving = chip_shift(out_moving)
    back = (products, squares, my_gains, cosine, sine, dquery, dkey, dvalue)
    dpre, dn_own_1, dn_away_1, gains_1 = project_back(
        [source_chip(1)], core, *back, means, in_weight, None
    )
    dnormed_moving = add_rows((dn_own_1, 0), partner_swap(dn_away_1[0]))
    dnormed_moving, dpre = tie(dnormed_moving, dpre)
    dnormed_moving = chip_shift(dnormed_moving)
    dpre, dn_own, dn_away, gains_2 = project_back(
        [source_chip(step) for step in rest], core, *back, means, in_weight, dpre
    )
    gain_terms = gains_1 + gains_2

    def spread(row):
        return lax.dynamic_update_slice(jnp.zeros((1, width), F32), row, (0, me * columns))

    rows8 = jnp.concatenate(
        [
            mixnorm_term[:1],
            spread(gain_terms[:1]),
            spread(gain_terms[1:2]),
            jnp.zeros((5, width), F32),
        ],
        axis=0,
    )
    in_term = in_weight_grad(normed, dpre, mixed, dlogits, rows8, experts)
    dnormed_moving, dn_own, dn_away, in_term, out_moving, sums, output_mine = tie(
        dnormed_moving, dn_own, dn_away, in_term, out_moving, sums, output_mine
    )
    output_sum = lax.psum_scatter(
        add_rows(output_mine, output_swapped), "group", scatter_dimension=0, tiled=True
    )
    dnormed_moving = add_rows(dnormed_moving, (dn_own, 0), partner_swap(dn_away[0]))
    dnormed_moving, dn_own, dn_away, sums, out_moving = tie(
        dnormed_moving, dn_own, dn_away, sums, out_moving
    )
    dnormed_moving = chip_shift(dnormed_moving)
    dn_swapped = [partner_swap(dn_away[i]) for i in range(1, chips - 1)]
    in_sum = lax.psum_scatter(in_term, "group", scatter_dimension=0, tiled=True)
    down_sum, gate_sum = sums[0].astype(F32)[None], sums[1].astype(F32)[None]
    layer_result = (
        middle
        + out_moving.astype(F32)
        + out_own[0].astype(F32)
        + out_swapped[1].astype(F32)
    ).astype(BF)
    dnormed_moving, dn_swapped, down_sum, gate_sum, layer_result = tie(
        dnormed_moving, dn_swapped, down_sum, gate_sum, layer_result
    )
    dnormed_moving = add_rows(dnormed_moving, (dn_own, 1), dn_swapped[0])
    dnormed_moving, up_sum = tie(dnormed_moving, sums[2])
    dnormed_moving = chip_shift(dnormed_moving)
    up_sum = up_sum.astype(F32)[None]
    output_pairs = output_sum.reshape(chips, shard, width)

    def to_chip(array, step):
        return lax.dynamic_index_in_dim(
            array, lax.rem(chip + step, chips), 0, keepdims=False
        )

    output_parts = [to_chip(output_pairs, step) for step in range(chips)]
    output_parts = output_parts[:1] + [chip_shift(output_parts[i], i) for i in range(1, chips)]
    output_parts, dnormed_moving, up_sum, in_sum = tie(
        output_parts, dnormed_moving, up_sum, in_sum
    )
    in_pairs = in_sum.reshape(chips, 2, shard, 3 * columns + 128)
    in_parts = [to_chip(in_pairs, step) for step in range(chips)]
    (in_parts,) = tie(in_parts)
    in_parts = in_parts[:1] + [chip_shift(in_parts[i], i) for i in range(1, chips)]
    output_sum = sum(part.astype(F32) for part in output_parts)
    (in_parts,) = tie(in_parts)
    kept = [lax.dynamic_index_in_dim(part, core, 0) for part in in_parts]
    given = jnp.concatenate(
        [lax.dynamic_index_in_dim(part, 1 - core, 0) for part in in_parts], axis=0
    )
    in_sum = exchange_cores(kept, given)
    dnormed = (
        dnormed_moving.astype(F32)
        + dn_own[chips - 2].astype(F32)
        + dn_swapped[chips - 3].astype(F32)
    )

    raw = [
        in_sum[:, :, i * columns : (i + 1) * columns]
        .transpose(1, 0, 2)
        .reshape(shard, width)
        .astype(F32)
        for i in range(3)
    ]
    others = jnp.sum(in_sum[:, :, 3 * columns :].astype(F32), axis=0)
    attnorm_grad = sum(
        jnp.sum(grad * weight.astype(F32), axis=1)
        for grad, weight in zip(raw, (query_weight, key_weight, value_weight))
    )
    query_sum, key_sum, value_sum = (grad * own_gain for grad in raw)
    own_f = tokens.astype(F32)
    own_inverse = lax.rsqrt(jnp.mean(own_f * own_f, axis=-1, keepdims=True) + EPS)
    scaled = own_f * own_inverse
    dinput = own_inverse * (dnormed - scaled * jnp.mean(scaled * dnormed, axis=-1, keepdims=True))
    tokens_grad = (dmiddle + dinput).astype(BF)
    return (
        layer_result,
        tokens_grad,
        query_sum,
        key_sum,
        value_sum,
        output_sum,
        others[:, :experts],
        attnorm_grad,
        others[:, experts + 1],
        others[:, experts + 2],
        others[:, experts],
        gate_sum,
        up_sum,
        down_sum,
    )


def solution(mesh):
    rows = P(("group", "expert"), None)
    line = P(("group", "expert"))
    expert = P("expert", None, None)
    group = P("group", None)
    return jax.shard_map(
        body,
        mesh=mesh,
        in_specs=(
            (rows,) * 6 + (line,) * 4 + (expert,) * 3 + (rows, group, group, rows)
        ),
        out_specs=(rows,) * 7 + (line,) * 4 + (expert,) * 3,
        check_vma=False,
    )
```

```python
import functools

import jax
import jax.numpy as jnp
from jax import lax
from jax.experimental import pallas as pl
from jax.experimental.pallas import tpu as pltpu
from jax.sharding import PartitionSpec as P

HEADS = 16
HEAD_DIM = 128
TOP = 2
EPS = 1e-05
NEG = -1e30
LOG2E = 1.4426950408889634
MESH = pl.DeviceIdType.MESH
BF = jnp.bfloat16
F32 = jnp.float32


def cost(microseconds):
    return pl.CostEstimate(
        flops=int(microseconds * 1e6), bytes_accessed=1 << 16, transcendentals=0
    )


def row_sums(x):
    ones = jnp.ones((8, x.shape[1]), BF)
    high = x.astype(BF)
    low = (x - high.astype(F32)).astype(BF)
    contract = (((1,), (1,)), ((), ()))
    return (
        lax.dot_general(ones, high, contract, preferred_element_type=F32)
        + lax.dot_general(ones, low, contract, preferred_element_type=F32)
    )[:1]


def exchange_small(collective_id, world=None, group=None, added=None):
    groups, ranks = lax.axis_size("group"), lax.axis_size("expert")
    total = groups * ranks
    near_blocks = [block for block in (group, added) if block is not None]
    count = len(near_blocks)

    def kernel(*refs):
        refs = list(refs)
        world_in = refs.pop(0) if world is not None else None
        near_in = [refs.pop(0) for _ in range(count)]
        world_out = refs.pop(0) if world is not None else None
        near_out = [refs.pop(0) for _ in range(count)]
        rank = lax.axis_index("expert")
        me = lax.axis_index("group") * ranks + rank
        barrier = pltpu.get_barrier_semaphore()

        def far(step):
            flat = lax.rem(me + step, total)
            return (flat // ranks, lax.rem(flat, ranks))

        def near(step):
            return {"expert": lax.rem(rank + step, ranks)}

        if world is not None:

            def greet(step, carry):
                pl.semaphore_signal(barrier, inc=1, device_id=far(step), device_id_type=MESH)
                return carry

            lax.fori_loop(1, total, greet, 0)
            pl.semaphore_wait(barrier, total - 1)
        else:
            for step in range(1, ranks):
                pl.semaphore_signal(barrier, inc=1, device_id=near(step), device_id_type=MESH)
            pl.semaphore_wait(barrier, ranks - 1)
        lands = list(near_out)
        if added is not None:
            lands[-1] = refs.pop(0)
        if count:
            near_send, near_recv = refs.pop(0), refs.pop(0)
        near_copies = []
        for which in range(count):
            for step in range(1, ranks):
                copy = pltpu.make_async_remote_copy(
                    src_ref=near_in[which],
                    dst_ref=lands[which].at[rank],
                    send_sem=near_send.at[which, step],
                    recv_sem=near_recv.at[which, step],
                    device_id=near(step),
                    device_id_type=MESH,
                )
                copy.start()
                near_copies.append(copy)
            lands[which][rank] = near_in[which][...]
        if world is not None:
            far_send, far_recv = refs.pop(0), refs.pop(0)

            def far_copy(step):
                return pltpu.make_async_remote_copy(
                    src_ref=world_in,
                    dst_ref=world_out.at[me],
                    send_sem=far_send.at[step],
                    recv_sem=far_recv.at[step],
                    device_id=far(step),
                    device_id_type=MESH,
                )

            def send(step, carry):
                far_copy(step).start()
                return carry

            lax.fori_loop(1, total, send, 0)
            world_out[me] = world_in[...]

            def settle(step, carry):
                far_copy(step).wait()
                return carry

            lax.fori_loop(1, total, settle, 0)
        for copy in near_copies:
            copy.wait()
        if added is not None:
            summed = lands[-1][0]
            for other in range(1, ranks):
                summed = summed + lands[-1][other]
            near_out[-1][...] = summed

    inputs, outputs, scratch = [], [], []
    if world is not None:
        inputs.append(world)
        outputs.append(jax.ShapeDtypeStruct((total,) + world.shape, world.dtype))
    if group is not None:
        inputs.append(group)
        outputs.append(jax.ShapeDtypeStruct((ranks,) + group.shape, group.dtype))
    if added is not None:
        inputs.append(added)
        outputs.append(jax.ShapeDtypeStruct(added.shape, added.dtype))
        scratch.append(pltpu.VMEM((ranks,) + added.shape, added.dtype))
    if count:
        scratch += [pltpu.SemaphoreType.DMA((count, ranks))] * 2
    if world is not None:
        scratch += [pltpu.SemaphoreType.DMA((total,)), pltpu.SemaphoreType.DMA((total,))]
    vmem = pl.BlockSpec(memory_space=pltpu.VMEM)
    return pl.pallas_call(
        kernel,
        out_shape=tuple(outputs),
        in_specs=[vmem] * len(inputs),
        out_specs=tuple([vmem] * len(outputs)),
        scratch_shapes=scratch,
        compiler_params=pltpu.CompilerParams(collective_id=collective_id, has_side_effects=True),
        name="exchange_small",
    )(*inputs)


def tie(*trees):
    leaves, shape = jax.tree.flatten(trees)
    return jax.tree.unflatten(shape, lax.optimization_barrier(leaves))


def partner_swap(block):
    ranks = lax.axis_size("expert")
    return lax.ppermute(block, "expert", [(i, i ^ 1) for i in range(ranks)])


def chip_shift(block, step=1):
    ranks = lax.axis_size("expert")
    return lax.ppermute(block, "expert", [(i, (i + 2 * step) % ranks) for i in range(ranks)])


def place_of():
    ranks = lax.axis_size("expert")
    me = lax.axis_index("expert")
    return ranks // 2, me // 2, me % 2


def source_chip(step):
    chips, chip, _ = place_of()
    return lax.rem(chip - step + chips, chips)


def assemble(pieces, axis):
    _, _, core = place_of()
    first = pieces[0][0]
    size = first.shape[axis]
    shape = list(first.shape)
    shape[axis] = size * 2 * len(pieces)
    whole = jnp.zeros(shape, first.dtype)
    for step, (mine, other) in enumerate(pieces):
        at = source_chip(step) * 2
        whole = lax.dynamic_update_slice_in_dim(whole, mine, (at + core) * size, axis)
        whole = lax.dynamic_update_slice_in_dim(whole, other, (at + 1 - core) * size, axis)
    return whole


def exchange_chips(blocks):
    chips, chip, core = place_of()
    pairs = blocks.reshape((chips, 2) + blocks.shape[1:])
    keep, give = [], []
    for step in range(chips):
        pair = lax.dynamic_index_in_dim(pairs, lax.rem(chip + step, chips), 0, keepdims=False)
        if step:
            pair = chip_shift(pair, step)
        keep.append(lax.dynamic_index_in_dim(pair, core, 0))
        give.append(lax.dynamic_index_in_dim(pair, 1 - core, 0))
    return keep, jnp.concatenate(give, axis=0)


def exchange_cores(keep, give):
    given = partner_swap(give)
    return assemble([(part, given[i : i + 1]) for i, part in enumerate(keep)], 0)


def rank_exchange(blocks):
    return exchange_cores(*exchange_chips(blocks))


def add_rows(*parts):
    parts = [part if isinstance(part, tuple) else (part[None], 0) for part in parts]
    _, rows, width = parts[0][0].shape
    tile = rows // 2

    def kernel(*refs):
        total = refs[0][0].astype(F32)
        for ref in refs[1:-1]:
            total = total + ref[0].astype(F32)
        refs[-1][...] = total.astype(BF)

    def spec(which):
        return pl.BlockSpec((1, tile, width), lambda i: (which, i, 0))

    return pl.pallas_call(
        kernel,
        out_shape=jax.ShapeDtypeStruct((rows, width), BF),
        grid=(2,),
        in_specs=[spec(which) for _, which in parts],
        out_specs=pl.BlockSpec((tile, width), lambda i: (i, 0)),
        cost_estimate=cost(3),
        name="add_rows",
    )(*[array for array, _ in parts])


def attention_forward(queries, keys, values, starts, lowest):
    rows, columns = queries.shape
    heads = columns // HEAD_DIM
    blocks, _, block = starts.shape
    scale = HEAD_DIM ** (-0.5)

    def kernel(low_ref, start_ref, q_ref, k_ref, v_ref, o_ref, lse_ref):
        i = pl.program_id(0)
        start = start_ref[0]
        q_index = i * block + lax.broadcasted_iota(jnp.int32, (1, block), 1)
        k_local = lax.broadcasted_iota(jnp.int32, (block, block), 0)

        def step(j, carry):
            at = pl.ds(pl.multiple_of(j * block, block), block)
            k_index = k_local + j * block
            allowed = (k_index <= q_index) & (k_index >= start)
            after = []
            for h in range(heads):
                top, total, acc = carry[h]
                lanes = slice(h * HEAD_DIM, (h + 1) * HEAD_DIM)
                s = lax.dot_general(
                    k_ref[at, lanes],
                    q_ref[:, lanes],
                    (((1,), (1,)), ((), ())),
                    preferred_element_type=F32,
                )
                s = jnp.where(allowed, s * (scale * LOG2E), NEG)
                new_top = jnp.maximum(top, jnp.max(s, axis=0, keepdims=True))
                p = jnp.exp2(s - new_top)
                shrink = jnp.exp2(top - new_top)
                total = total * shrink + jnp.sum(p, axis=0, keepdims=True)
                acc = acc * shrink + lax.dot_general(
                    v_ref[at, lanes],
                    p.astype(BF),
                    (((0,), (0,)), ((), ())),
                    preferred_element_type=F32,
                )
                after.append((new_top, total, acc))
            return tuple(after)

        begin = (
            jnp.full((1, block), NEG, F32),
            jnp.zeros((1, block), F32),
            jnp.zeros((HEAD_DIM, block), F32),
        )
        done = lax.fori_loop(low_ref[i], i + 1, step, (begin,) * heads)
        for h, (top, total, acc) in enumerate(done):
            o_ref[:, h * HEAD_DIM : (h + 1) * HEAD_DIM] = (acc / total).T.astype(BF)
            lse_ref[h, 0] = top + jnp.log(total) * LOG2E

    return pl.pallas_call(
        kernel,
        out_shape=(
            jax.ShapeDtypeStruct((rows, columns), BF),
            jax.ShapeDtypeStruct((heads, blocks, 1, block), F32),
        ),
        grid_spec=pltpu.PrefetchScalarGridSpec(
            num_scalar_prefetch=1,
            grid=(blocks,),
            in_specs=[
                pl.BlockSpec((1, 1, block), lambda i, low: (i, 0, 0)),
                pl.BlockSpec((block, columns), lambda i, low: (i, 0)),
                pl.BlockSpec((rows, columns), lambda i, low: (0, 0)),
                pl.BlockSpec((rows, columns), lambda i, low: (0, 0)),
            ],
            out_specs=[
                pl.BlockSpec((block, columns), lambda i, low: (i, 0)),
                pl.BlockSpec((heads, 1, 1, block), lambda i, low: (0, i, 0, 0)),
            ],
        ),
        compiler_params=pltpu.CompilerParams(vmem_limit_bytes=48 << 20),
        cost_estimate=cost(35),
        name="attention_forward",
    )(lowest, starts, queries, keys, values)


def attention_backward(queries, keys, values, outs, douts, lse, starts, highest):
    rows, columns = queries.shape
    heads = columns // HEAD_DIM
    blocks, _, block = starts.shape
    scale = HEAD_DIM ** (-0.5)

    def kernel(
        high_ref,
        start_ref,
        q_ref,
        o_ref,
        do_ref,
        k_ref,
        v_ref,
        lse_ref,
        dq_ref,
        dk_ref,
        dv_ref,
        q_sum_ref,
        k_sum_ref,
        delta_ref,
    ):
        j = pl.program_id(0)

        @pl.when(j == 0)
        def _():
            dq_ref[...] = jnp.zeros_like(dq_ref)
            for h in range(heads):
                lanes = slice(h * HEAD_DIM, (h + 1) * HEAD_DIM)
                for i in range(blocks):
                    at = slice(i * block, (i + 1) * block)
                    delta_ref[h, i] = row_sums(
                        o_ref[at, lanes].astype(F32) * do_ref[at, lanes].astype(F32)
                    )

        k_index = j * block + lax.broadcasted_iota(jnp.int32, (block, block), 0)
        q_local = lax.broadcasted_iota(jnp.int32, (1, block), 1)
        contract = (((1,), (1,)), ((), ()))

        def step(i, carry):
            at = pl.ds(pl.multiple_of(i * block, block), block)
            allowed = (k_index <= q_local + i * block) & (k_index >= start_ref[i])
            after = []
            for h in range(heads):
                dk, dv = carry[h]
                lanes = slice(h * HEAD_DIM, (h + 1) * HEAD_DIM)
                q, do = q_ref[at, lanes], do_ref[at, lanes]
                k, v = k_ref[:, lanes], v_ref[:, lanes]
                s = lax.dot_general(k, q, contract, preferred_element_type=F32) * (scale * LOG2E)
                p = jnp.exp2(jnp.where(allowed, s, NEG) - lse_ref[h, i])
                dv = dv + jnp.dot(p.astype(BF), do, preferred_element_type=F32)
                dp = lax.dot_general(v, do, contract, preferred_element_type=F32)
                ds = (p * (dp - delta_ref[h, i])).astype(BF)
                dk = dk + jnp.dot(ds, q, preferred_element_type=F32)
                dq_ref[at, lanes] += lax.dot_general(
                    ds, k, (((0,), (0,)), ((), ())), preferred_element_type=F32
                )
                after.append((dk, dv))
            return tuple(after)

        zero = jnp.zeros((block, HEAD_DIM), F32)
        done = lax.fori_loop(j, high_ref[j] + 1, step, ((zero, zero),) * heads)
        for h, (dk, dv) in enumerate(done):
            lanes = slice(h * HEAD_DIM, (h + 1) * HEAD_DIM)
            dk = dk * scale
            dk_ref[:, lanes] = dk
            dv_ref[:, lanes] = dv.astype(BF)
            k_sum_ref[h, 0] = row_sums(k_ref[:, lanes].astype(F32) * dk)
            at = pl.ds(pl.multiple_of(j * block, block), block)
            dq = dq_ref[at, lanes] * scale
            dq_ref[at, lanes] = dq
            q_sum_ref[h, 0] = row_sums(q_ref[at, lanes].astype(F32) * dq)

    whole = pl.BlockSpec((rows, columns), lambda j, high: (0, 0))
    part = pl.BlockSpec((block, columns), lambda j, high: (j, 0))
    line = pl.BlockSpec((heads, blocks, 1, block), lambda j, high: (0, 0, 0, 0))
    bit = pl.BlockSpec((heads, 1, 1, block), lambda j, high: (0, j, 0, 0))
    shape = jax.ShapeDtypeStruct((rows, columns), F32)
    sums = jax.ShapeDtypeStruct((heads, blocks, 1, block), F32)
    return pl.pallas_call(
        kernel,
        out_shape=(shape, shape, jax.ShapeDtypeStruct((rows, columns), BF), sums, sums),
        grid_spec=pltpu.PrefetchScalarGridSpec(
            num_scalar_prefetch=1,
            grid=(blocks,),
            in_specs=[
                pl.BlockSpec((blocks, 1, block), lambda j, high: (0, 0, 0)),
                whole,
                whole,
                whole,
                part,
                part,
                line,
            ],
            out_specs=[whole, part, part, bit, bit],
            scratch_shapes=[pltpu.VMEM((heads, blocks, 1, block), F32)],
        ),
        compiler_params=pltpu.CompilerParams(vmem_limit_bytes=48 << 20),
        cost_estimate=cost(46),
        name="attention_backward",
    )(highest, starts, queries, outs, douts, keys, values, lse)


def gather_heads(tokens, pick, mine, other, source, core, out_weight, whole):
    ranks, capacity, rows = pick.shape
    columns = mine.shape[1]
    width = out_weight.shape[1]
    first = whole is None
    pair = 2 * capacity

    def kernel(at_ref, base_ref, pick_ref, mine_ref, other_ref, w_ref, out_ref, parts):
        core = at_ref[1]
        for half in range(2):
            at = half * capacity
            chosen = pick_ref[half]
            spots = slice(half * rows, (half + 1) * rows)
            if first:
                out_ref[at : at + capacity, :] = jnp.dot(
                    chosen, base_ref[spots, :], preferred_element_type=F32
                )
            for part_ref, which in ((mine_ref, core), (other_ref, 1 - core)):
                parts[
                    at : at + capacity, pl.ds(pl.multiple_of(which * columns, columns), columns)
                ] = jnp.dot(chosen, part_ref[spots, :], preferred_element_type=F32).astype(BF)
        base = out_ref if first else base_ref
        out_ref[...] = base[...] + jnp.dot(
            parts[...], w_ref[...], preferred_element_type=F32
        )

    heads_spec = pl.BlockSpec((2 * rows, columns), lambda r, at: (r, 0))
    total_spec = pl.BlockSpec((pair, width), lambda r, at: (r, 0))
    return pl.pallas_call(
        kernel,
        out_shape=jax.ShapeDtypeStruct((ranks * capacity, width), F32),
        grid_spec=pltpu.PrefetchScalarGridSpec(
            num_scalar_prefetch=1,
            grid=(ranks // 2,),
            in_specs=[
                pl.BlockSpec((2 * rows, width), lambda r, at: (r, 0)) if first else total_spec,
                pl.BlockSpec((2, capacity, rows), lambda r, at: (r, 0, 0)),
                heads_spec,
                heads_spec,
                pl.BlockSpec((2 * columns, width), lambda r, at: (at[0], 0)),
            ],
            out_specs=total_spec,
            scratch_shapes=[pltpu.VMEM((pair, 2 * columns), BF)],
        ),
        input_output_aliases={} if first else {1: 0},
        compiler_params=pltpu.CompilerParams(vmem_limit_bytes=40 << 20),
        cost_estimate=cost(8),
        name="gather_heads",
    )(
        jnp.stack([source, core]).astype(jnp.int32),
        tokens if first else whole,
        pick,
        mine,
        other,
        out_weight,
    )


def expert_forward(
    order, whole, pick, pick_t, mine, other, out_weight, mix_gain, router, hot, gate_w, up_w, down_w
):
    ranks, capacity, rows = pick.shape
    columns = mine.shape[1]
    width = out_weight.shape[1]
    hidden_width = gate_w.shape[1]
    chips = ranks // 2
    pair = 2 * capacity

    def kernel(
        order_ref,
        base_ref,
        pick_ref,
        turned_ref,
        mine_ref,
        other_ref,
        wo_ref,
        gain_ref,
        router_ref,
        hot_ref,
        wg_ref,
        wu_ref,
        wd_ref,
        mixed_ref,
        gates_ref,
        gate_ref,
        up_ref,
        hidden_ref,
        out_ref,
        own_ref,
        away_ref,
        scratch,
        parts,
    ):
        core = order_ref[2 * chips + 1]
        for half in range(2):
            at = half * capacity
            for part_ref, which in ((mine_ref, core), (other_ref, 1 - core)):
                parts[
                    at : at + capacity, pl.ds(pl.multiple_of(which * columns, columns), columns)
                ] = jnp.dot(
                    pick_ref[half],
                    part_ref[half * rows : (half + 1) * rows, :],
                    preferred_element_type=F32,
                ).astype(BF)
        total = base_ref[...] + jnp.dot(parts[...], wo_ref[...], preferred_element_type=F32)
        inverse = lax.rsqrt(jnp.mean(total * total, axis=1, keepdims=True) + EPS)
        mixed = (total * inverse * gain_ref[...]).astype(BF)
        mixed_ref[...] = mixed
        logits = lax.dot_general(
            mixed, router_ref[...], (((1,), (1,)), ((), ())), preferred_element_type=F32
        )
        lane = lax.broadcasted_iota(jnp.int32, logits.shape, 1)
        logits = jnp.where(lane < ranks, logits, NEG)
        shifted = jnp.exp(logits - jnp.max(logits, axis=1, keepdims=True))
        gates = jnp.sum(shifted * hot_ref[...], axis=1, keepdims=True) / jnp.sum(
            shifted, axis=1, keepdims=True
        )
        gates_ref[...] = jnp.broadcast_to(gates, gates_ref.shape)
        gate = jnp.dot(mixed, wg_ref[...], preferred_element_type=F32)
        gate_ref[...] = gate
        up = jnp.dot(mixed, wu_ref[...], preferred_element_type=F32)
        up_ref[...] = up
        hidden = (gate * jax.nn.sigmoid(gate) * up).astype(BF)
        hidden_ref[...] = hidden
        result = jnp.dot(hidden, wd_ref[...], preferred_element_type=F32).astype(BF)
        out_ref[...] = result
        scratch[...] = (gates * result.astype(F32)).astype(BF)
        for half, place_ref in ((core, own_ref), (1 - core, away_ref)):
            at = pl.ds(pl.multiple_of(half * capacity, capacity), capacity)
            place_ref[0] = jnp.dot(
                turned_ref[half], scratch[at, :], preferred_element_type=F32
            ).astype(BF)

    def chip_rows(n, m):
        return pl.BlockSpec((n, m), lambda i, order: (order[i], 0))

    def fixed(n, m):
        return pl.BlockSpec((n, m), lambda i, order: (0, 0), pipeline_mode=pl.Buffered(1))

    def slot(i, order):
        return (order[chips + i], 0, 0)

    all_slots = ranks * capacity
    return pl.pallas_call(
        kernel,
        out_shape=(
            jax.ShapeDtypeStruct((all_slots, width), BF),
            jax.ShapeDtypeStruct((all_slots, 128), F32),
            jax.ShapeDtypeStruct((all_slots, hidden_width), F32),
            jax.ShapeDtypeStruct((all_slots, hidden_width), F32),
            jax.ShapeDtypeStruct((all_slots, hidden_width), BF),
            jax.ShapeDtypeStruct((all_slots, width), BF),
            jax.ShapeDtypeStruct((chips, rows, width), BF),
            jax.ShapeDtypeStruct((chips, rows, width), BF),
        ),
        grid_spec=pltpu.PrefetchScalarGridSpec(
            num_scalar_prefetch=1,
            grid=(chips,),
            in_specs=[
                chip_rows(pair, width),
                pl.BlockSpec((2, capacity, rows), lambda i, order: (order[i], 0, 0)),
                pl.BlockSpec((2, rows, capacity), lambda i, order: (order[i], 0, 0)),
                chip_rows(2 * rows, columns),
                chip_rows(2 * rows, columns),
                pl.BlockSpec(
                    (2 * columns, width),
                    lambda i, order: (order[2 * chips], 0),
                    pipeline_mode=pl.Buffered(1),
                ),
                fixed(1, width),
                fixed(128, width),
                fixed(1, 128),
                fixed(width, hidden_width),
                fixed(width, hidden_width),
                fixed(hidden_width, width),
            ],
            out_specs=[
                chip_rows(pair, width),
                chip_rows(pair, 128),
                chip_rows(pair, hidden_width),
                chip_rows(pair, hidden_width),
                chip_rows(pair, hidden_width),
                chip_rows(pair, width),
                pl.BlockSpec((1, rows, width), slot),
                pl.BlockSpec((1, rows, width), slot),
            ],
            scratch_shapes=[pltpu.VMEM((pair, width), BF), pltpu.VMEM((pair, 2 * columns), BF)],
        ),
        compiler_params=pltpu.CompilerParams(vmem_limit_bytes=58 << 20),
        cost_estimate=cost(45),
        name="expert_forward",
    )(
        order.astype(jnp.int32),
        whole,
        pick,
        pick_t,
        mine,
        other,
        out_weight,
        mix_gain,
        router,
        hot,
        gate_w,
        up_w,
        down_w,
    )


def expert_backward(
    sources, core, rank, pick, pick_t, cotangents, gates, gate, up, hidden, result, weights, whole
):
    ranks, capacity, rows = pick.shape
    count = len(sources)
    width = cotangents[0][0].shape[1]
    hidden_width = weights[0].shape[1]
    pair = 2 * capacity
    wide = width + 128

    def kernel(at_ref, pick_ref, turned_ref, *refs):
        cots = refs[: 2 * count]
        gates_ref, gate_ref, up_ref, out_ref, wg_ref, wu_ref, wd_ref = refs[2 * count : 2 * count + 7]
        own_ref, away_ref, dcopy_ref, dgate_ref, dup_ref, rows_s, back_s, gates_s = refs[-8:]
        core, rank = at_ref[count], at_ref[count + 1]
        step = pl.program_id(0)

        for which in range(count):

            @pl.when(step == which)
            def _(which=which):
                for half, part_ref in ((core, cots[2 * which]), (1 - core, cots[2 * which + 1])):
                    at = pl.ds(pl.multiple_of(half * capacity, capacity), capacity)
                    rows_s[at, :] = jnp.dot(
                        pick_ref[half], part_ref[...], preferred_element_type=F32
                    )

        incoming = rows_s[...]
        dgates = jnp.sum(out_ref[...].astype(F32) * incoming, axis=1, keepdims=True)
        high = dgates.astype(BF)
        low = (dgates - high.astype(F32)).astype(BF)
        lane = lax.broadcasted_iota(jnp.int32, (pair, 128), 1)
        gates_s[...] = jnp.where(
            lane == rank,
            high.astype(F32),
            jnp.where(lane == rank + ranks, low.astype(F32), 0.0),
        ).astype(BF)
        dcopy = (gates_ref[:, :1] * incoming).astype(BF)
        dcopy_ref[...] = dcopy
        dhidden = lax.dot_general(
            dcopy, wd_ref[...], (((1,), (1,)), ((), ())), preferred_element_type=F32
        )
        gate, up = gate_ref[...], up_ref[...]
        sigma = jax.nn.sigmoid(gate)
        scaled = dhidden * sigma
        dgate = (scaled * up * (1.0 + gate * (1.0 - sigma))).astype(BF)
        dup = (scaled * gate).astype(BF)
        dgate_ref[...] = dgate
        dup_ref[...] = dup
        back_s[...] = (
            lax.dot_general(
                dgate, wg_ref[...], (((1,), (1,)), ((), ())), preferred_element_type=F32
            )
            + lax.dot_general(
                dup, wu_ref[...], (((1,), (1,)), ((), ())), preferred_element_type=F32
            )
        ).astype(BF)
        for half, place_ref in ((core, own_ref), (1 - core, away_ref)):
            at = pl.ds(pl.multiple_of(half * capacity, capacity), capacity)
            turned = turned_ref[half]
            place_ref[0, :, :width] = jnp.dot(
                turned, back_s[at, :], preferred_element_type=F32
            ).astype(BF)
            place_ref[0, :, width:] = jnp.dot(
                turned, gates_s[at, :], preferred_element_type=F32
            ).astype(BF)

    def chip_rows(n, m):
        return pl.BlockSpec((n, m), lambda i, at: (at[i], 0))

    def fixed(n, m):
        return pl.BlockSpec((n, m), lambda i, at: (0, 0), pipeline_mode=pl.Buffered(1))

    extra = [] if whole is None else list(whole)
    all_slots = ranks * capacity
    piece = pl.BlockSpec((1, rows, wide), lambda i, at: (i, 0, 0))
    return pl.pallas_call(
        kernel,
        out_shape=(
            jax.ShapeDtypeStruct((count, rows, wide), BF),
            jax.ShapeDtypeStruct((count, rows, wide), BF),
            jax.ShapeDtypeStruct((all_slots, width), BF),
            jax.ShapeDtypeStruct((all_slots, hidden_width), BF),
            jax.ShapeDtypeStruct((all_slots, hidden_width), BF),
        ),
        grid_spec=pltpu.PrefetchScalarGridSpec(
            num_scalar_prefetch=1,
            grid=(count,),
            in_specs=[
                pl.BlockSpec((2, capacity, rows), lambda i, at: (at[i], 0, 0)),
                pl.BlockSpec((2, rows, capacity), lambda i, at: (at[i], 0, 0)),
            ]
            + [fixed(rows, width)] * (2 * count)
            + [
                chip_rows(pair, 128),
                chip_rows(pair, hidden_width),
                chip_rows(pair, hidden_width),
                chip_rows(pair, width),
                fixed(width, hidden_width),
                fixed(width, hidden_width),
                fixed(hidden_width, width),
            ]
            + [pl.BlockSpec(memory_space=pl.ANY)] * len(extra),
            out_specs=[
                piece,
                piece,
                chip_rows(pair, width),
                chip_rows(pair, hidden_width),
                chip_rows(pair, hidden_width),
            ],
            scratch_shapes=[
                pltpu.VMEM((pair, width), F32),
                pltpu.VMEM((pair, width), BF),
                pltpu.VMEM((pair, 128), BF),
            ],
        ),
        input_output_aliases={10 + 2 * count + i: 2 + i for i in range(len(extra))},
        compiler_params=pltpu.CompilerParams(vmem_limit_bytes=60 << 20),
        cost_estimate=cost(12 * count),
        name="expert_backward",
    )(
        jnp.stack(list(sources) + [core, rank]).astype(jnp.int32),
        pick,
        pick_t,
        *[part for parts in cotangents for part in parts],
        gates,
        gate,
        up,
        result,
        *weights,
        *extra,
    )


def owner_backward(
    arrived, mine, swapped, share, router, middle, inverse, mix_gain, cotangent, out_weight
):
    rows, width = middle.shape
    ranks = lax.axis_size("expert")
    columns = width // ranks
    wide = arrived.shape[1]
    tile = rows // 2

    def kernel(
        arrived_ref,
        mine_ref,
        swapped_ref,
        share_ref,
        router_ref,
        middle_ref,
        inverse_ref,
        gain_ref,
        cot_ref,
        w_ref,
        dlogits_ref,
        norm_ref,
        dmiddle_ref,
        dprojected_ref,
        dattended_ref,
    ):
        @pl.when(pl.program_id(0) == 0)
        def _():
            norm_ref[...] = jnp.zeros_like(norm_ref)

        total = (
            arrived_ref[...].astype(F32)
            + mine_ref[0].astype(F32)
            + swapped_ref[...].astype(F32)
        )
        share = share_ref[...]
        dshare = total[:, width:]
        dshare = dshare + pltpu.roll(dshare, 128 - ranks, 1)
        dlogits = (
            share * (dshare - jnp.sum(share * dshare, axis=1, keepdims=True))
        ).astype(BF)
        dlogits_ref[...] = dlogits
        dmixed = total[:, :width] + jnp.dot(
            dlogits, router_ref[...], preferred_element_type=F32
        )
        inverse = inverse_ref[:, :1]
        scaled = middle_ref[...] * inverse
        weighted = dmixed * gain_ref[...]
        norm_ref[:1, :] += jnp.sum(dmixed * scaled, axis=0, keepdims=True)
        mean = jnp.mean(scaled * weighted, axis=1, keepdims=True)
        dmiddle = cot_ref[...].astype(F32) + inverse * (weighted - scaled * mean)
        dmiddle_ref[...] = dmiddle
        dprojected = dmiddle.astype(BF)
        dprojected_ref[...] = dprojected
        dattended = lax.dot_general(
            dprojected, w_ref[...], (((1,), (1,)), ((), ())), preferred_element_type=F32
        ).astype(BF)
        for rank in range(ranks):
            dattended_ref[rank] = dattended[:, rank * columns : (rank + 1) * columns]

    def rows_of(n):
        return pl.BlockSpec((tile, n), lambda i: (i, 0))

    def fixed(n, m):
        return pl.BlockSpec((n, m), lambda i: (0, 0))

    return pl.pallas_call(
        kernel,
        out_shape=(
            jax.ShapeDtypeStruct((rows, 128), BF),
            jax.ShapeDtypeStruct((8, width), F32),
            jax.ShapeDtypeStruct((rows, width), F32),
            jax.ShapeDtypeStruct((rows, width), BF),
            jax.ShapeDtypeStruct((ranks, rows, columns), BF),
        ),
        grid=(rows // tile,),
        in_specs=[
            rows_of(wide),
            pl.BlockSpec((1, tile, wide), lambda i: (mine.shape[0] - 1, i, 0)),
            rows_of(wide),
            rows_of(128),
            fixed(128, width),
            rows_of(width),
            rows_of(128),
            fixed(1, width),
            rows_of(width),
            fixed(width, width),
        ],
        out_specs=(
            rows_of(128),
            fixed(8, width),
            rows_of(width),
            rows_of(width),
            pl.BlockSpec((ranks, tile, columns), lambda i: (0, i, 0)),
        ),
        compiler_params=pltpu.CompilerParams(vmem_limit_bytes=48 << 20),
        cost_estimate=cost(14),
        name="owner_backward",
    )(
        arrived, mine, swapped, share, router, middle, inverse, mix_gain, cotangent, out_weight
    )


def project_in(mine, other, chip, core, weight, whole):
    rows, width = mine.shape
    ranks = lax.axis_size("expert")
    columns = width // ranks

    def kernel(at_ref, mine_ref, other_ref, w_ref, *refs):
        x_out, n_out, p_out, v_out, s_out = refs[-5:]
        core = at_ref[1]

        def handle(x_ref, half):
            at = pl.ds(pl.multiple_of(half * rows, rows), rows)
            x = x_ref[...]
            xf = x.astype(F32)
            n = (xf * lax.rsqrt(jnp.mean(xf * xf, axis=1, keepdims=True) + EPS)).astype(BF)
            x_out[at, :] = x
            n_out[at, :] = n
            product = jnp.dot(n, w_ref[...], preferred_element_type=F32)
            p_out[at, :] = product[:, : 2 * columns]
            v_out[at, :] = product[:, 2 * columns :].astype(BF)
            for which in range(2):
                part = product[:, which * columns : (which + 1) * columns]
                s_out[half, which : which + 1, :] = row_sums(part * part)

        handle(mine_ref, core)
        handle(other_ref, 1 - core)

    shapes = (
        jax.ShapeDtypeStruct((rows * ranks, width), BF),
        jax.ShapeDtypeStruct((rows * ranks, width), BF),
        jax.ShapeDtypeStruct((rows * ranks, 2 * columns), F32),
        jax.ShapeDtypeStruct((rows * ranks, columns), BF),
        jax.ShapeDtypeStruct((ranks, 2, rows), F32),
    )
    out_specs = [
        pl.BlockSpec((2 * rows, shape.shape[1]), lambda i, at: (at[0], 0)) for shape in shapes[:4]
    ] + [pl.BlockSpec((2, 2, rows), lambda i, at: (at[0], 0, 0))]
    extra = [] if whole is None else list(whole)
    full = pl.BlockSpec((rows, width), lambda i, at: (0, 0))
    return pl.pallas_call(
        kernel,
        out_shape=shapes,
        grid_spec=pltpu.PrefetchScalarGridSpec(
            num_scalar_prefetch=1,
            grid=(1,),
            in_specs=[full, full, pl.BlockSpec((width, 3 * columns), lambda i, at: (0, 0))]
            + [pl.BlockSpec(memory_space=pl.ANY)] * len(extra),
            out_specs=out_specs,
        ),
        input_output_aliases={4 + i: i for i in range(len(extra))},
        compiler_params=pltpu.CompilerParams(vmem_limit_bytes=48 << 20),
        cost_estimate=cost(8),
        name="project_in",
    )(jnp.stack([chip, core]).astype(jnp.int32), mine, other, weight, *extra)


def column_of(pair, function):
    pair = function(pair)
    return jnp.concatenate([pair, jnp.zeros((6, pair.shape[1]), F32)], axis=0).T


def make_heads(products, squares, gains, cosine, sine, width):
    rows = products.shape[0]
    columns = products.shape[1] // 2
    tile = squares.shape[2]

    def kernel(p_ref, s_ref, g_ref, c_ref, n_ref, q_ref, k_ref):
        cos, sin = c_ref[...], n_ref[...]
        inverses = column_of(s_ref[0], lambda total: lax.rsqrt(total / width + EPS))
        for which, out in ((0, q_ref), (1, k_ref)):
            inverse = inverses[:, which : which + 1]
            for h in range(0, columns, HEAD_DIM):
                x = p_ref[:, which * columns + h : which * columns + h + HEAD_DIM]
                x = x * inverse * g_ref[which : which + 1, h : h + HEAD_DIM]
                out[:, h : h + HEAD_DIM] = (
                    x * cos + pltpu.roll(x, HEAD_DIM // 2, 1) * sin
                ).astype(BF)

    def rows_of(n):
        return pl.BlockSpec((tile, n), lambda i: (i, 0))

    shape = jax.ShapeDtypeStruct((rows, columns), BF)
    return pl.pallas_call(
        kernel,
        out_shape=(shape, shape),
        grid=(rows // tile,),
        in_specs=[
            rows_of(2 * columns),
            pl.BlockSpec((1, 2, tile), lambda i: (i, 0, 0)),
            pl.BlockSpec((2, columns), lambda i: (0, 0)),
            rows_of(HEAD_DIM),
            rows_of(HEAD_DIM),
        ],
        out_specs=[rows_of(columns)] * 2,
        cost_estimate=cost(8),
        name="make_heads",
    )(products, squares, gains, cosine, sine)


def project_back(
    sources, core, products, squares, gains, cosine, sine, dq, dk, dv, means, weight, whole
):
    all_rows = products.shape[0]
    columns = products.shape[1] // 2
    rows = squares.shape[2]
    width = weight.shape[0]
    count = len(sources)

    def kernel(at_ref, p_ref, s_ref, m_ref, g_ref, c_ref, n_ref, dq_ref, dk_ref, dv_ref, w_ref, *refs):
        out_ref, own_ref, away_ref, gain_ref = refs[-4:]
        core = at_ref[count]

        @pl.when(pl.program_id(0) == 0)
        def _():
            gain_ref[...] = jnp.zeros_like(gain_ref)

        for half, place_ref in ((core, own_ref), (1 - core, away_ref)):
            at = pl.ds(pl.multiple_of(half * rows, rows), rows)
            cos, sin = c_ref[at, :], n_ref[at, :]
            inverses = column_of(s_ref[half], lambda total: lax.rsqrt(total / width + EPS))
            mean = column_of(m_ref[half], lambda total: total / width)
            for which, d_ref in ((0, dq_ref), (1, dk_ref)):
                inverse = inverses[:, which : which + 1]
                for h in range(0, columns, HEAD_DIM):
                    here = which * columns + h
                    scaled = p_ref[at, here : here + HEAD_DIM] * inverse
                    d = d_ref[at, h : h + HEAD_DIM]
                    d = d * cos - pltpu.roll(d, HEAD_DIM // 2, 1) * sin
                    weighted = d * g_ref[which : which + 1, h : h + HEAD_DIM]
                    gain_ref[which : which + 1, h : h + HEAD_DIM] += jnp.sum(
                        d * scaled, axis=0, keepdims=True
                    )
                    out_ref[at, here : here + HEAD_DIM] = (
                        inverse * (weighted - scaled * mean[:, which : which + 1])
                    ).astype(BF)
            out_ref[at, 2 * columns :] = dv_ref[at, :]
            place_ref[0] = lax.dot_general(
                out_ref[at, :], w_ref[...], (((1,), (1,)), ((), ())), preferred_element_type=F32
            ).astype(BF)

    def chip_rows(n):
        return pl.BlockSpec((2 * rows, n), lambda i, at: (at[i], 0))

    pair = pl.BlockSpec((2, 2, rows), lambda i, at: (at[i], 0, 0))
    piece = pl.BlockSpec((1, rows, width), lambda i, at: (i, 0, 0))
    extra = [] if whole is None else [whole]
    return pl.pallas_call(
        kernel,
        out_shape=(
            jax.ShapeDtypeStruct((all_rows, 3 * columns), BF),
            jax.ShapeDtypeStruct((count, rows, width), BF),
            jax.ShapeDtypeStruct((count, rows, width), BF),
            jax.ShapeDtypeStruct((8, columns), F32),
        ),
        grid_spec=pltpu.PrefetchScalarGridSpec(
            num_scalar_prefetch=1,
            grid=(count,),
            in_specs=[
                chip_rows(2 * columns),
                pair,
                pair,
                pl.BlockSpec((2, columns), lambda i, at: (0, 0)),
                chip_rows(HEAD_DIM),
                chip_rows(HEAD_DIM),
                chip_rows(columns),
                chip_rows(columns),
                chip_rows(columns),
                pl.BlockSpec((width, 3 * columns), lambda i, at: (0, 0)),
            ]
            + [pl.BlockSpec(memory_space=pl.ANY)] * len(extra),
            out_specs=[
                chip_rows(3 * columns),
                piece,
                piece,
                pl.BlockSpec((8, columns), lambda i, at: (0, 0)),
            ],
        ),
        input_output_aliases={11: 0} if extra else {},
        compiler_params=pltpu.CompilerParams(vmem_limit_bytes=48 << 20),
        cost_estimate=cost(8 * count),
        name="project_back",
    )(
        jnp.stack(list(sources) + [core]).astype(jnp.int32),
        products,
        squares,
        means,
        gains,
        cosine,
        sine,
        dq,
        dk,
        dv,
        weight,
        *extra,
    )


def norm_back(values, inverse, gain, grad):
    scaled = values * inverse
    weighted = grad * gain
    mean = jnp.mean(scaled * weighted, axis=-1, keepdims=True)
    return inverse * (weighted - scaled * mean), jnp.sum(grad * scaled, axis=0)


def weight_grad(a, b, tile=512):
    rows, m = a.shape
    n = b.shape[1]

    def kernel(a_ref, b_ref, o_ref):
        o_ref[...] = lax.dot_general(
            a_ref[...], b_ref[...], (((0,), (0,)), ((), ())), preferred_element_type=F32
        ).astype(BF)

    return pl.pallas_call(
        kernel,
        out_shape=jax.ShapeDtypeStruct((m, n), BF),
        grid=(m // tile,),
        in_specs=[
            pl.BlockSpec((rows, tile), lambda i: (0, i)),
            pl.BlockSpec((rows, n), lambda i: (0, 0)),
        ],
        out_specs=pl.BlockSpec((tile, n), lambda i: (i, 0)),
        compiler_params=pltpu.CompilerParams(vmem_limit_bytes=48 << 20),
        cost_estimate=cost(10),
        name="weight_grad",
    )(a, b)


def in_weight_grad(normed, dpre, mixed, dlogits, rows8, experts):
    rows, m = normed.shape
    own = mixed.shape[0]
    n = dpre.shape[1]
    tile = 512

    def kernel(a_ref, b_ref, m_ref, l_ref, r_ref, o_ref):
        contract = (((0,), (0,)), ((), ()))
        o_ref[:, :n] = lax.dot_general(
            a_ref[...], b_ref[...], contract, preferred_element_type=F32
        ).astype(BF)
        side = lax.dot_general(m_ref[...], l_ref[...], contract, preferred_element_type=F32)
        turned = r_ref[...].T
        lane = lax.broadcasted_iota(jnp.int32, side.shape, 1)
        for i in range(3):
            side = jnp.where(lane == experts + i, turned[:, i : i + 1], side)
        o_ref[:, n:] = side.astype(BF)

    return pl.pallas_call(
        kernel,
        out_shape=jax.ShapeDtypeStruct((m, n + 128), BF),
        grid=(m // tile,),
        in_specs=[
            pl.BlockSpec((rows, tile), lambda i: (0, i)),
            pl.BlockSpec((rows, n), lambda i: (0, 0)),
            pl.BlockSpec((own, tile), lambda i: (0, i)),
            pl.BlockSpec((own, 128), lambda i: (0, 0)),
            pl.BlockSpec((8, tile), lambda i: (0, i)),
        ],
        out_specs=pl.BlockSpec((tile, n + 128), lambda i: (i, 0)),
        compiler_params=pltpu.CompilerParams(vmem_limit_bytes=48 << 20),
        cost_estimate=cost(14),
        name="in_weight_grad",
    )(normed, dpre, mixed, dlogits, rows8)


def own_forward(places, pieces, tokens, out_weight, mix_gain, router, experts):
    rows, width = tokens.shape
    count = len(pieces)
    columns = width // count

    def kernel(at_ref, *refs):
        token_ref, w_ref, gain_ref, router_ref = refs[count : count + 4]
        att_ref, middle_ref, mixed_ref, share_ref, inverse_ref = refs[count + 4 :]
        for i in range(count):
            att_ref[:, pl.ds(pl.multiple_of(at_ref[i] * columns, columns), columns)] = refs[i][...]
        middle = token_ref[...].astype(F32) + jnp.dot(
            att_ref[...], w_ref[...], preferred_element_type=F32
        )
        middle_ref[...] = middle
        inverse = lax.rsqrt(jnp.mean(middle * middle, axis=1, keepdims=True) + EPS)
        inverse_ref[...] = jnp.broadcast_to(inverse, inverse_ref.shape)
        mixed = (middle * inverse * gain_ref[...]).astype(BF)
        mixed_ref[...] = mixed
        logits = lax.dot_general(
            mixed, router_ref[...], (((1,), (1,)), ((), ())), preferred_element_type=F32
        )
        lane = lax.broadcasted_iota(jnp.int32, logits.shape, 1)
        logits = jnp.where(lane < experts, logits, NEG)
        shifted = jnp.exp(logits - jnp.max(logits, axis=1, keepdims=True))
        share_ref[...] = shifted / jnp.sum(shifted, axis=1, keepdims=True)

    def fixed(n, m):
        return pl.BlockSpec((n, m), lambda i, at: (0, 0))

    return pl.pallas_call(
        kernel,
        out_shape=(
            jax.ShapeDtypeStruct((rows, width), BF),
            jax.ShapeDtypeStruct((rows, width), F32),
            jax.ShapeDtypeStruct((rows, width), BF),
            jax.ShapeDtypeStruct((rows, 128), F32),
            jax.ShapeDtypeStruct((rows, 128), F32),
        ),
        grid_spec=pltpu.PrefetchScalarGridSpec(
            num_scalar_prefetch=1,
            grid=(1,),
            in_specs=[pl.BlockSpec((rows, columns), lambda i, at: (at[count], 0))] * count
            + [fixed(rows, width), fixed(width, width), fixed(1, width), fixed(128, width)],
            out_specs=[
                fixed(rows, width),
                fixed(rows, width),
                fixed(rows, width),
                fixed(rows, 128),
                fixed(rows, 128),
            ],
        ),
        compiler_params=pltpu.CompilerParams(vmem_limit_bytes=48 << 20),
        cost_estimate=cost(10),
        name="own_forward",
    )(places, *pieces, tokens, out_weight, mix_gain, router)


def dot_nt(a, b):
    return lax.dot_general(a, b, (((1,), (1,)), ((), ())), preferred_element_type=F32)


def dot_tn(a, b):
    return lax.dot_general(a, b, (((0,), (0,)), ((), ())), preferred_element_type=F32)


def dot_nn(a, b):
    return jnp.dot(a, b, preferred_element_type=F32)


def layout_of(lengths, seq_order, rows):
    length_row, order_row = lengths[0], seq_order[0]
    count = order_row.shape[0]
    chosen = (order_row[:, None] == jnp.arange(count, dtype=jnp.int32)[None, :]).astype(jnp.int32)
    placed = jnp.sum(chosen * length_row[None, :], axis=1)
    ends = jnp.sum(
        jnp.where(jnp.arange(count)[None, :] <= jnp.arange(count)[:, None], placed[None, :], 0),
        axis=1,
    )
    index = jnp.arange(rows, dtype=jnp.int32)
    passed = (index[:, None] >= ends[None, :]).astype(jnp.int32)
    begin = jnp.sum(passed * placed[None, :], axis=1)
    segment = jnp.sum(passed, axis=1)
    inside = (segment[:, None] == jnp.arange(count, dtype=jnp.int32)[None, :]).astype(jnp.int32)
    final = jnp.sum(inside * ends[None, :], axis=1) - 1
    return index, begin, final


def body(
    tokens,
    query_weight,
    key_weight,
    value_weight,
    output_weight,
    router_weight,
    attnorm,
    querynorm,
    keynorm,
    mixnorm,
    gate_weight,
    up_weight,
    down_weight,
    routes,
    lengths,
    seq_order,
    cotangent,
):
    rows, width = tokens.shape
    ranks = lax.axis_size("expert")
    groups = lax.axis_size("group")
    me = lax.axis_index("expert")
    chips, _, core = place_of()
    all_rows = rows * ranks
    capacity = 2 * rows * TOP // ranks
    columns = width // ranks
    shard = query_weight.shape[0]
    experts = router_weight.shape[1]
    block = 512 if all_rows % 512 == 0 else rows
    blocks = all_rows // block
    heads = columns // HEAD_DIM

    own_gain = attnorm.astype(F32)[:, None]
    beside = jnp.concatenate(
        [querynorm[:, None], keynorm[:, None], mixnorm[:, None], router_weight], axis=1
    )
    beside = jnp.pad(beside, ((0, 0), (0, 128 - beside.shape[1])))
    stacked = jnp.concatenate(
        [
            (part.astype(F32) * own_gain)
            .astype(BF)
            .reshape(shard, ranks, columns)
            .transpose(1, 0, 2)
            for part in (query_weight, key_weight, value_weight)
        ]
        + [jnp.broadcast_to(beside, (ranks, shard, 128))],
        axis=2,
    )
    kept, given = exchange_chips(stacked)
    tokens_, kept, given = tie(tokens, kept, given)
    tok, tok_other = [tokens, chip_shift(tokens_)], [partner_swap(tokens_)]
    stacked = exchange_cores(kept, given)
    in_weight = lax.all_gather(
        stacked.reshape(ranks * shard, 3 * columns + 128), "group", axis=0, tiled=True
    )

    index, begin, final = layout_of(lengths, seq_order, all_rows)
    starts = begin.reshape(blocks, 1, block)
    lowest = begin.reshape(blocks, block)[:, 0] // block
    highest = final.reshape(blocks, block)[:, block - 1] // block
    position = (index - begin).astype(F32)
    frequency = 10000.0 ** (-(jnp.arange(HEAD_DIM // 2, dtype=F32) * 2.0 / HEAD_DIM))
    angles = position[:, None] * frequency[None, :]
    cosine, sine = jnp.cos(angles), jnp.sin(angles)
    cosine = jnp.concatenate([cosine, cosine], axis=1)
    sine = jnp.concatenate([-sine, sine], axis=1)

    tables = (starts, lowest, highest, cosine, sine)
    state, ready = None, 0
    for step in range(1, chips):
        tok, tok_other, state, tables = tie(tok, tok_other, state, tables)
        tok_other.append(partner_swap(tok[step]))
        if step + 1 < chips:
            tok.append(chip_shift(tok[step]))
        while ready <= step:
            state = project_in(
                tok[ready], tok_other[ready], source_chip(ready), core, in_weight, state
            )
            ready += 1
    starts, lowest, highest, cosine, sine = tables
    output_weight_, _ = tie(output_weight, tok)
    full_output = lax.all_gather(output_weight_, ("group", "expert"), axis=0, tiled=True)
    all_tokens, normed, products, values, squares = state
    packed_routes = (
        jnp.zeros((1024,), jnp.int32)
        .at[: rows * TOP]
        .set(routes.T.reshape(-1))
        .reshape(8, 128)
    )
    beside = in_weight[:, 3 * columns :]
    my_gains = lax.dynamic_slice_in_dim(beside, me * columns, columns, 0)[:, :2].T.astype(F32)
    mix_gain = beside[:, 2:3].T.astype(F32)
    router = jnp.pad(beside[:, 3 : 3 + experts].T, ((0, 128 - experts), (0, 0)))
    squares, packed_routes, my_gains, mix_gain, router = tie(
        squares, packed_routes, my_gains, mix_gain, router
    )
    all_routes, squares = exchange_small(2, group=packed_routes, added=squares)
    queries, keys = make_heads(products, squares, my_gains, cosine, sine, width)

    all_routes = all_routes.reshape(ranks, -1)[:, : rows * TOP].reshape(ranks, TOP, rows)
    named = jnp.any(all_routes == me, axis=1)
    counted = jnp.cumsum(named.astype(jnp.int32), axis=1) - 1
    slot_of = jnp.where(named, counted, -1)
    slots = jnp.arange(capacity, dtype=jnp.int32)
    pick = (slot_of[:, None, :] == slots[None, :, None]).astype(BF)
    pick_t = (slot_of[:, :, None] == slots[None, None, :]).astype(BF)

    cotangent_, _ = tie(cotangent, squares)
    cot = [cotangent_, chip_shift(cotangent_)]
    attended_mine, lse = attention_forward(queries, keys, values, starts, lowest)
    att = [attended_mine]
    att, cot, pick, pick_t, mix_gain, router = tie(att, cot, pick, pick_t, mix_gain, router)
    att_other = [partner_swap(att[0])]
    att.append(chip_shift(att[0]))
    att, att_other = tie(att, att_other)
    middle_e, ready = None, 0
    for step in range(1, chips):
        att_other.append(partner_swap(att[step]))
        if step + 1 < chips:
            att.append(chip_shift(att[step]))
            while ready < step or (ready == step and step + 2 == chips):
                middle_e = gather_heads(
                    all_tokens,
                    pick,
                    att[ready],
                    att_other[ready],
                    source_chip(ready),
                    core,
                    full_output,
                    middle_e,
                )
                ready += 1
            att, att_other, middle_e = tie(att, att_other, middle_e)

    cot, middle_e = tie(cot, middle_e)
    cot_other = [partner_swap(cot[0]), partner_swap(cot[1])]
    cot, _ = tie(cot, att)
    cot += [chip_shift(cot[1])] + [chip_shift(cot[0], step) for step in range(3, chips)]
    order = [source_chip(step % chips) for step in range(1, chips + 1)]
    order += [jnp.int32(step % chips) for step in range(1, chips + 1)]
    order += [source_chip(chips - 1), core]
    hot = (jnp.arange(128, dtype=jnp.int32) == me).astype(F32)[None]
    weights = (gate_weight[0], up_weight[0], down_weight[0])
    mixed_e, gates_e, gate_pre, up_pre, hidden, expert_out, out_own, out_away = expert_forward(
        jnp.stack(order),
        middle_e,
        pick,
        pick_t,
        att[-1],
        att_other[-1],
        full_output,
        mix_gain,
        router,
        hot,
        *weights,
    )
    forward = (gates_e, gate_pre, up_pre, hidden, expert_out)

    own_1, away_1, *saved = expert_backward(
        [source_chip(1)],
        core,
        me,
        pick,
        pick_t,
        [(cot[1], cot_other[1])],
        *forward,
        weights,
        None,
    )
    cot, cot_other, own_1, away_1, saved = tie(cot, cot_other, own_1, away_1, saved)
    cot_other += [partner_swap(cot[step]) for step in range(2, chips)]
    dmixed_moving = add_rows((own_1, 0), partner_swap(away_1[0]))
    cot_other, dmixed_moving, own_att_pieces = tie(
        cot_other, dmixed_moving, (att, att_other)
    )
    dmixed_moving = chip_shift(dmixed_moving)
    rest = list(range(2, chips)) + [0]
    own, away, *saved = expert_backward(
        [source_chip(step) for step in rest],
        core,
        me,
        pick,
        pick_t,
        [(cot[step], cot_other[step]) for step in rest],
        *forward,
        weights,
        saved,
    )
    dmixed_moving, own, away, saved, out_away = tie(dmixed_moving, own, away, saved, out_away)
    dmixed_moving = add_rows(dmixed_moving, (own, 0), partner_swap(away[0]))
    dmixed_moving, own, away, saved, out_away = tie(dmixed_moving, own, away, saved, out_away)
    dmixed_moving = chip_shift(dmixed_moving)
    swapped = [partner_swap(away[i]) for i in range(1, chips - 1)]
    out_first = partner_swap(out_away[1])
    dcopy, dgate_pre, dup_pre = saved
    sums = [
        weight_grad(hidden, dcopy),
        weight_grad(mixed_e, dgate_pre),
        weight_grad(mixed_e, dup_pre),
    ]
    dmixed_moving, own, swapped, sums = tie(dmixed_moving, own, swapped, sums)
    sums = lax.psum(tuple(sums), "group")
    for step in range(3, chips):
        dmixed_moving = add_rows(dmixed_moving, (own, step - 2), swapped[step - 3])
        dmixed_moving, pieces = tie(dmixed_moving, own_att_pieces)
        dmixed_moving = chip_shift(dmixed_moving)

    places = []
    for step in range(chips):
        places += [source_chip(step) * 2 + core, source_chip(step) * 2 + 1 - core]
    own_attended, middle, mixed, share, middle_inverse = own_forward(
        jnp.stack(places + [me]).astype(jnp.int32),
        [piece for pair in zip(*pieces) for piece in pair],
        tokens,
        full_output,
        mix_gain,
        router,
        experts,
    )
    halves = own_attended.reshape(rows, groups * chips, 2, shard)
    att_mine = lax.dynamic_index_in_dim(halves, core, 2, keepdims=False).reshape(rows, -1)
    att_away = lax.dynamic_index_in_dim(halves, 1 - core, 2, keepdims=False).reshape(rows, -1)
    out_moving = add_rows((out_own, 1), out_first)
    dmixed_moving, middle, middle_inverse, mixed, share, att_mine, att_away, out_moving = tie(
        dmixed_moving, middle, middle_inverse, mixed, share, att_mine, att_away, out_moving
    )
    out_moving = chip_shift(out_moving)
    dlogits, mixnorm_term, dmiddle, dprojected, dattended_own = owner_backward(
        dmixed_moving,
        own,
        swapped[chips - 3],
        share,
        router,
        middle,
        middle_inverse,
        mix_gain,
        cotangent,
        full_output,
    )

    pairs = dattended_own.reshape(chips, 2, rows, columns)
    _, chip, _ = place_of()
    parts = [
        lax.dynamic_index_in_dim(pairs, lax.rem(chip + step, chips), 0, keepdims=False)
        for step in range(chips)
    ]
    parts, dprojected = tie(parts, dprojected)
    parts = parts[:1] + [chip_shift(parts[step], step) for step in range(1, chips)]
    output_mine = weight_grad(att_mine, dprojected)
    output_away = weight_grad(att_away, dprojected)
    parts, output_mine, output_away, out_moving = tie(parts, output_mine, output_away, out_moving)
    kept = [lax.dynamic_index_in_dim(part, core, 0) for part in parts]
    given = [lax.dynamic_index_in_dim(part, 1 - core, 0) for part in parts]
    dattended = exchange_cores(kept, jnp.concatenate(given, axis=0)).reshape(all_rows, columns)
    out_second = partner_swap(out_away[2])
    out_moving = add_rows(out_moving, (out_own, 2), out_second)

    out_moving, dattended, output_mine, output_away = tie(
        out_moving, dattended, output_mine, output_away
    )
    out_moving = chip_shift(out_moving)
    out_swapped = [partner_swap(out_away[step]) for step in (3, 0)]
    output_swapped = partner_swap(output_away)
    dquery, dkey, dvalue, query_part, key_part = attention_backward(
        queries, keys, values, attended_mine, dattended, lse, starts, highest
    )
    out_moving, out_swapped, output_swapped, dquery, dkey, dvalue, query_part, key_part = tie(
        out_moving, out_swapped, output_swapped, dquery, dkey, dvalue, query_part, key_part
    )
    out_moving = add_rows(out_moving, (out_own, 3), out_swapped[0])
    partials = jnp.stack(
        [jnp.sum(part, axis=0).reshape(ranks, rows) for part in (query_part, key_part)], axis=1
    )
    partials, out_moving = tie(partials, out_moving)
    (means,) = exchange_small(3, added=partials)
    out_moving, means, output_mine, output_swapped = tie(
        out_moving, means, output_mine, output_swapped
    )
    out_moving = chip_shift(out_moving)
    back = (products, squares, my_gains, cosine, sine, dquery, dkey, dvalue)
    dpre, dn_own_1, dn_away_1, gains_1 = project_back(
        [source_chip(1)], core, *back, means, in_weight, None
    )
    dnormed_moving = add_rows((dn_own_1, 0), partner_swap(dn_away_1[0]))
    dnormed_moving, dpre = tie(dnormed_moving, dpre)
    dnormed_moving = chip_shift(dnormed_moving)
    dpre, dn_own, dn_away, gains_2 = project_back(
        [source_chip(step) for step in rest], core, *back, means, in_weight, dpre
    )
    gain_terms = gains_1 + gains_2

    def spread(row):
        return lax.dynamic_update_slice(jnp.zeros((1, width), F32), row, (0, me * columns))

    rows8 = jnp.concatenate(
        [
            mixnorm_term[:1],
            spread(gain_terms[:1]),
            spread(gain_terms[1:2]),
            jnp.zeros((5, width), F32),
        ],
        axis=0,
    )
    in_term = in_weight_grad(normed, dpre, mixed, dlogits, rows8, experts)
    dnormed_moving, dn_own, dn_away, in_term, out_moving, sums, output_mine = tie(
        dnormed_moving, dn_own, dn_away, in_term, out_moving, sums, output_mine
    )
    output_sum = lax.psum_scatter(
        add_rows(output_mine, output_swapped), "group", scatter_dimension=0, tiled=True
    )
    dnormed_moving = add_rows(dnormed_moving, (dn_own, 0), partner_swap(dn_away[0]))
    dnormed_moving, dn_own, dn_away, sums, out_moving = tie(
        dnormed_moving, dn_own, dn_away, sums, out_moving
    )
    dnormed_moving = chip_shift(dnormed_moving)
    dn_swapped = [partner_swap(dn_away[i]) for i in range(1, chips - 1)]
    in_sum = lax.psum_scatter(in_term, "group", scatter_dimension=0, tiled=True)
    down_sum, gate_sum = sums[0].astype(F32)[None], sums[1].astype(F32)[None]
    layer_result = (
        middle
        + out_moving.astype(F32)
        + out_own[0].astype(F32)
        + out_swapped[1].astype(F32)
    ).astype(BF)
    dnormed_moving, dn_swapped, down_sum, gate_sum, layer_result = tie(
        dnormed_moving, dn_swapped, down_sum, gate_sum, layer_result
    )
    dnormed_moving = add_rows(dnormed_moving, (dn_own, 1), dn_swapped[0])
    dnormed_moving, up_sum = tie(dnormed_moving, sums[2])
    dnormed_moving = chip_shift(dnormed_moving)
    up_sum = up_sum.astype(F32)[None]
    output_pairs = output_sum.reshape(chips, shard, width)

    def to_chip(array, step):
        return lax.dynamic_index_in_dim(
            array, lax.rem(chip + step, chips), 0, keepdims=False
        )

    output_parts = [to_chip(output_pairs, step) for step in range(chips)]
    output_parts = output_parts[:1] + [chip_shift(output_parts[i], i) for i in range(1, chips)]
    output_parts, dnormed_moving, up_sum, in_sum = tie(
        output_parts, dnormed_moving, up_sum, in_sum
    )
    in_pairs = in_sum.reshape(chips, 2, shard, 3 * columns + 128)
    in_parts = [to_chip(in_pairs, step) for step in range(chips)]
    (in_parts,) = tie(in_parts)
    in_parts = in_parts[:1] + [chip_shift(in_parts[i], i) for i in range(1, chips)]
    output_sum = sum(part.astype(F32) for part in output_parts)
    (in_parts,) = tie(in_parts)
    kept = [lax.dynamic_index_in_dim(part, core, 0) for part in in_parts]
    given = jnp.concatenate(
        [lax.dynamic_index_in_dim(part, 1 - core, 0) for part in in_parts], axis=0
    )
    in_sum = exchange_cores(kept, given)
    dnormed = (
        dnormed_moving.astype(F32)
        + dn_own[chips - 2].astype(F32)
        + dn_swapped[chips - 3].astype(F32)
    )

    raw = [
        in_sum[:, :, i * columns : (i + 1) * columns]
        .transpose(1, 0, 2)
        .reshape(shard, width)
        .astype(F32)
        for i in range(3)
    ]
    others = jnp.sum(in_sum[:, :, 3 * columns :].astype(F32), axis=0)
    attnorm_grad = sum(
        jnp.sum(grad * weight.astype(F32), axis=1)
        for grad, weight in zip(raw, (query_weight, key_weight, value_weight))
    )
    query_sum, key_sum, value_sum = (grad * own_gain for grad in raw)
    own_f = tokens.astype(F32)
    own_inverse = lax.rsqrt(jnp.mean(own_f * own_f, axis=-1, keepdims=True) + EPS)
    scaled = own_f * own_inverse
    dinput = own_inverse * (dnormed - scaled * jnp.mean(scaled * dnormed, axis=-1, keepdims=True))
    tokens_grad = (dmiddle + dinput).astype(BF)
    return (
        layer_result,
        tokens_grad,
        query_sum,
        key_sum,
        value_sum,
        output_sum,
        others[:, :experts],
        attnorm_grad,
        others[:, experts + 1],
        others[:, experts + 2],
        others[:, experts],
        gate_sum,
        up_sum,
        down_sum,
    )


def solution(mesh):
    rows = P(("group", "expert"), None)
    line = P(("group", "expert"))
    expert = P("expert", None, None)
    group = P("group", None)
    return jax.shard_map(
        body,
        mesh=mesh,
        in_specs=(
            (rows,) * 6 + (line,) * 4 + (expert,) * 3 + (rows, group, group, rows)
        ),
        out_specs=(rows,) * 7 + (line,) * 4 + (expert,) * 3,
        check_vma=False,
    )
```
